32 devices in a mesh: group: 4 (over y, x), fsdp: 8 (over z, core).
Axes of the slice: x: 2, y: 2, z: 4, core: 2. Of those that a mesh axis runs over, the one named last changes fastest.
Arguments:
- hidden_in: bfloat16 [128, 512, 768], P(('group', 'fsdp')), may hold values from -6 to 6
- lengths: int32 [128], P(('group', 'fsdp')), may hold values from 40 to 512, as said below
- out_grad: bfloat16 [128, 256, 768], P(('group', 'fsdp')), may hold values from -6 to 6
- weights: float32 [2, 9216, 768], P(None, 'fsdp')
- weight_m: float32 [4, 2, 9216, 768], P('group', None, 'fsdp')
- weight_v: float32 [4, 2, 9216, 768], P('group', None, 'fsdp'), as said below
- outer_mom: float32 [2, 9216, 768], P(None, 'fsdp'), may hold values from -0.12 to 0.12
- small: float32 [6168], replicated
- small_m: float32 [4, 6168], P('group')
- small_v: float32 [4, 6168], P('group'), as said below
- small_mom: float32 [6168], replicated, may hold values from -0.12 to 0.12
Outputs:
- block_out: bfloat16 [128, 256, 768], P(('group', 'fsdp'))
- input_grad: float32 [128, 512, 768], P(('group', 'fsdp'))
- new_weights: float32 [2, 9216, 768], P(None, 'fsdp')
- weights_low: bfloat16 [2, 9216, 768], P(None, 'fsdp')
- weight_m_new: float32 [4, 2, 9216, 768], P('group', None, 'fsdp')
- weight_v_new: float32 [4, 2, 9216, 768], P('group', None, 'fsdp')
- weight_delta: float32 [2, 9216, 768], P(None, 'fsdp')
- outer_mom_new: float32 [2, 9216, 768], P(None, 'fsdp')
- small_new: float32 [6168], replicated
- small_m_new: float32 [4, 6168], P('group')
- small_v_new: float32 [4, 6168], P('group')
- small_delta: float32 [6168], replicated
- small_mom_new: float32 [6168], replicated
The draws below stay inside these ranges and needn't reach their ends.
Inputs may be any that keep to these rules, and one draw needn't show every extreme that they name: lengths[b] counts the valid tokens of sequence b; the shortest and the longest allowed length occur in every draw. `weight_v`: second moments are positive. `small_v`: second moments are positive.
All inputs are finite; a program needn't handle non-finite values.
Results may differ from the reference program's by a relative error of at most 0.023.
Values may be sent and summed in bfloat16 or wider, within the bound.
A program may use at most 320 MiB of HBM per device.

```python
import jax
import jax.numpy as jnp
from jax import lax

D = 768
H = 12
DH = 64
FF = 3072
S = 512
LEN_MIN = 40
NLAYER = 2
STEP = 10
SEQ_DEV = 4
S2 = 256
GROUPS = 4
NSEQ = 128
ROWS = 9216
SMALL = 6168
GROUP_TOKENS = 8192


def block_pick(scale_query, scale_key, scale_value, scale_output, scale_inner, scale_outer):
    row_index = jnp.arange(4 * D + 2 * FF)
    picked = jnp.where(row_index < 4 * D + FF, scale_inner, scale_outer)
    picked = jnp.where(row_index < 4 * D, scale_output, picked)
    picked = jnp.where(row_index < 3 * D, scale_value, picked)
    picked = jnp.where(row_index < 2 * D, scale_key, picked)
    picked = jnp.where(row_index < D, scale_query, picked)
    return picked.astype(jnp.float32)


def gradient_scale():
    return float(GROUP_TOKENS) ** 0.5 * block_pick(0.25, 0.25, 0.35, 0.15, 0.2, 0.5)


def small_scale():
    entry_index = jnp.arange(4 * D + H)
    row_scale = jnp.where(entry_index >= 4 * D, 100.0, 1.0) * float(GROUP_TOKENS) ** 0.5
    return jnp.tile(row_scale, NLAYER).astype(jnp.float32)


def draw_lengths(key, part):
    drawn_lengths = jax.random.randint(key, (NSEQ,), LEN_MIN, S + 1, dtype=jnp.int32)
    return drawn_lengths.at[0].set(S).at[NSEQ - 1].set(LEN_MIN)


def draw_weights(key, part):
    scales = block_pick(D ** (-0.5), D ** (-0.5), D ** (-0.5), 4.0 * D ** (-0.5), D ** (-0.5), FF ** (-0.5))
    base_draw = jax.random.truncated_normal(key, -4.0, 4.0, (NLAYER, ROWS, D), jnp.float32)
    return base_draw * scales[None, :, None]


def draw_weight_m(key, part):
    base_draw = jax.random.truncated_normal(key, -4.0, 4.0, (GROUPS, NLAYER, ROWS, D), jnp.float32)
    return base_draw * (0.11 * gradient_scale())[None, None, :, None]


def draw_weight_v(key, part):
    factor = jnp.exp(jax.random.uniform(key, (GROUPS, NLAYER, ROWS, D), jnp.float32, jnp.log(0.5), jnp.log(8.0)))
    scale_row = gradient_scale()
    return factor * (0.001 * scale_row * scale_row)[None, None, :, None]


def draw_small(key, part):
    part_width = 4 * D + H
    entry_index = jnp.arange(part_width)
    noise_draw = jax.random.truncated_normal(jax.random.fold_in(key, 1), -4.0, 4.0, (NLAYER, part_width), jnp.float32)
    slope_draw = jnp.exp(jax.random.uniform(jax.random.fold_in(key, 2), (NLAYER, part_width), jnp.float32, jnp.log(0.002), jnp.log(0.03)))
    is_gain = (entry_index // D % 2 == 0)[None, :]
    values = jnp.where(is_gain, 1.0 + 0.1 * noise_draw, 0.2 * noise_draw)
    return jnp.where((entry_index >= 4 * D)[None, :], slope_draw, values).reshape(NLAYER * part_width)


def draw_small_m(key, part):
    base_draw = jax.random.truncated_normal(key, -4.0, 4.0, (GROUPS, SMALL), jnp.float32)
    return base_draw * (0.11 * small_scale())[None, :]


def draw_small_v(key, part):
    factor = jnp.exp(jax.random.uniform(key, (GROUPS, SMALL), jnp.float32, jnp.log(0.5), jnp.log(8.0)))
    scale_row = small_scale()
    return factor * (0.001 * scale_row * scale_row)[None, :]


def block_levels(rng, shape, split, least, top_value):
    def one(axis_at, shards_of):
        heights = jax.random.uniform(jax.random.fold_in(jax.random.fold_in(rng, 6), axis_at), (shards_of,), jnp.float32, least / len(split), top_value / len(split))
        return jnp.repeat(jnp.exp(heights), shape[axis_at] // shards_of).reshape((-1,) + (1,) * (len(shape) - axis_at - 1))

    factor_of = one(*split[0])
    for cut in split[1:]:
        factor_of = factor_of * one(*cut)
    return factor_of


def noise(stream_key, dims, scale, reach, split=(), kind=jnp.bfloat16):
    values = scale * jax.random.normal(stream_key, dims, jnp.float32)
    if split:
        values = values * block_levels(stream_key, dims, split, -0.22, 0.18)
    return jnp.clip(values, -reach, reach).astype(kind)


def setup_inputs(seed: int = 0) -> dict:
    key_list = jax.random.split(jax.random.key(seed), 12)
    return {
        "hidden_in": noise(key_list[0], (NSEQ, S, D), 1.0, 6.0, ((0, 32),)),
        "lengths": draw_lengths(jax.random.fold_in(key_list[11], 71), 0),
        "out_grad": noise(key_list[2], (NSEQ, S2, D), 1.0, 6.0, ((0, 32),)),
        "weights": draw_weights(jax.random.fold_in(key_list[11], 71), 0),
        "weight_m": draw_weight_m(jax.random.fold_in(key_list[11], 71), 0),
        "weight_v": draw_weight_v(jax.random.fold_in(key_list[11], 71), 0),
        "outer_mom": noise(key_list[6], (NLAYER, ROWS, D), 0.02, 0.12, ((1, 8),), jnp.float32),
        "small": draw_small(jax.random.fold_in(key_list[11], 71), 0),
        "small_m": draw_small_m(jax.random.fold_in(key_list[11], 71), 0),
        "small_v": draw_small_v(jax.random.fold_in(key_list[11], 71), 0),
        "small_mom": noise(key_list[10], (SMALL,), 0.02, 0.12, (), jnp.float32),
    }


EPS_NORM = 1e-06
MASK_FILL = -1e+30
BETA_ONE = 0.9
BETA_TWO = 0.999
ADAM_EPS = 1e-08
DECAY_RATE = 0.01
INNER_RATE = 0.03
SMALL_RATE = 0.6
OUTER_RATE = 0.7
MOMENTUM = 0.9
GELU_COEF = 0.7978845608028654

@jax.custom_vjp
def low(v):
    return lax.optimization_barrier(v.astype(jnp.bfloat16)).astype(jnp.float32)

@jax.custom_vjp
def low_back(v):
    return v

def low_keep(v):
    return (low(v), None)

def low_pass(kept, grad):
    return (grad,)

def back_keep(v):
    return (v, None)

def back_low(kept, grad):
    return (low(grad),)
low.defvjp(low_keep, low_pass)
low_back.defvjp(back_keep, back_low)

def matrix_product(form, left, right):
    return jnp.einsum(form, left, right, precision=lax.Precision.HIGHEST)

def norm_apply(values, gain_vec, bias_vec):
    center = values - lax.optimization_barrier(jnp.mean(values, axis=-1, keepdims=True))
    spread = lax.optimization_barrier(jnp.mean(center * center, axis=-1, keepdims=True))
    return center * lax.rsqrt(spread + EPS_NORM) * gain_vec + bias_vec

def gelu_tanh(values):
    return 0.5 * values * (1.0 + jnp.tanh(GELU_COEF * (values + 0.044715 * values * values * values)))

def layer_forward(residual, query_rows_reduced, memory_rows_reduced, matrix, small_part, key_mask, distance):
    weights_low = low(matrix)
    query_weight = weights_low[0:D]
    key_weight = weights_low[D:2 * D]
    value_weight = weights_low[2 * D:3 * D]
    output_weight = weights_low[3 * D:4 * D]
    inner_weight = weights_low[4 * D:4 * D + FF]
    outer_weight = weights_low[4 * D + FF:]
    gain_one = small_part[0:D]
    bias_one = small_part[D:2 * D]
    gain_two = small_part[2 * D:3 * D]
    bias_two = small_part[3 * D:4 * D]
    slopes = small_part[4 * D:]
    batch_size = residual.shape[0]
    query_rows = low_back(low(matrix_product('mhv,vx->mhx', query_rows_reduced, query_weight)))
    every_key_row = low_back(low(matrix_product('zho,og->zhg', memory_rows_reduced, key_weight)))
    every_value_row = low_back(low(matrix_product('zho,og->zhg', memory_rows_reduced, value_weight)))
    query_heads = query_rows.reshape(batch_size, -1, H, DH)
    key_heads = every_key_row.reshape(batch_size, -1, H, DH)
    value_heads = every_value_row.reshape(batch_size, -1, H, DH)
    raw_scores = matrix_product('bqhd,bkhd->bhqk', query_heads, key_heads) * DH ** (-0.5)
    biased = low_back(raw_scores) - slopes[None, :, None, None] * distance[None, None]
    masked = jnp.where(key_mask[:, None, None, :], biased, MASK_FILL)
    row_peak = lax.optimization_barrier(jnp.max(masked, axis=-1, keepdims=True))
    lifted = jnp.exp(masked - row_peak)
    shares = lifted / lax.optimization_barrier(jnp.sum(lifted, axis=-1, keepdims=True))
    mixed_heads = matrix_product('bhqk,bkhd->bqhd', low(shares), value_heads).reshape(batch_size, -1, D)
    attention_result = low_back(low(mixed_heads))
    first_branch = low_back(matrix_product('mhv,vx->mhx', attention_result, output_weight))
    normalized_rows = norm_apply(residual + first_branch, gain_one, bias_one)
    hidden_preactivation = low_back(matrix_product('aye,we->ayw', low(normalized_rows), inner_weight))
    hidden_activation = low(gelu_tanh(hidden_preactivation))
    second_branch = low_back(matrix_product('wma,ar->wmr', hidden_activation, outer_weight))
    return norm_apply(normalized_rows + second_branch, gain_two, bias_two)

def block_forward(hidden_in, matrices, small_vec, lengths):
    positions = jnp.arange(S).astype(jnp.int32)
    halves = jnp.arange(S2).astype(jnp.int32)
    mask_one = positions[None, :] < lengths[:, None]
    mask_two = 2 * halves[None, :] < lengths[:, None]
    distance_one = jnp.abs(2 * halves[:, None] - positions[None, :]).astype(jnp.float32)
    distance_two = (2 * jnp.abs(halves[:, None] - halves[None, :])).astype(jnp.float32)
    part_size = 4 * D + H
    pooled = (hidden_in[:, 0::2] + hidden_in[:, 1::2]) * 0.5
    first_out = layer_forward(pooled, low(pooled), hidden_in, matrices[0], small_vec[0:part_size], mask_one, distance_one)
    first_low = low(first_out)
    return layer_forward(first_out, first_low, first_low, matrices[1], small_vec[part_size:], mask_two, distance_two)

def adam_step(master, gradient, first_mom, second_mom, rate):
    first_new = BETA_ONE * first_mom + (1.0 - BETA_ONE) * gradient
    second_new = BETA_TWO * second_mom + (1.0 - BETA_TWO) * gradient * gradient
    first_hat = first_new / (1.0 - BETA_ONE ** STEP)
    second_hat = second_new / (1.0 - BETA_TWO ** STEP)
    inner_move = rate * (first_hat / (jnp.sqrt(second_hat) + ADAM_EPS) + DECAY_RATE * master)
    return (first_new, second_new, inner_move)

def outer_step(master, moves_sum, momentum_old, group_count):
    mean_move = moves_sum / group_count
    momentum_new = MOMENTUM * momentum_old + mean_move
    return (mean_move, momentum_new, master - OUTER_RATE * (mean_move + MOMENTUM * momentum_new))

def reference(hidden_in, lengths, out_grad, weights, weight_m, weight_v, outer_mom, small, small_m, small_v, small_mom):
    blocks = NSEQ // (GROUPS * SEQ_DEV)
    inputs = hidden_in.reshape(GROUPS, blocks, SEQ_DEV, S, D)
    length_blocks = lengths.reshape(GROUPS, blocks, SEQ_DEV)
    cotangents = out_grad.reshape(GROUPS, blocks, SEQ_DEV, S2, D)

    def one_block(totals, pieces):
        block_in, block_lengths, block_cot = pieces

        def forward(values_in, matrices, small_vec):
            return block_forward(values_in, matrices, small_vec, block_lengths)
        result, pullback = jax.vjp(forward, block_in.astype(jnp.float32), weights, small)
        back_in, back_matrix, back_small = pullback(block_cot.astype(jnp.float32))
        return ((totals[0] + back_matrix, totals[1] + back_small), (result.astype(jnp.bfloat16), back_in))

    def one_group(pieces):
        initial = (jnp.zeros_like(weights), jnp.zeros_like(small))
        gradient_sums, outputs = lax.scan(one_block, initial, pieces)
        return (gradient_sums[0], gradient_sums[1], outputs[0], outputs[1])
    grad_matrix, grad_small, block_outs, input_grads = lax.map(one_group, (inputs, length_blocks, cotangents))
    weight_first, weight_second, weight_move = adam_step(weights, grad_matrix, weight_m, weight_v, INNER_RATE)
    small_first, small_second, small_move = adam_step(small, grad_small, small_m, small_v, SMALL_RATE)
    weight_mean, weight_mom, weight_new = outer_step(weights, lax.optimization_barrier(jnp.sum(weight_move, axis=0)), outer_mom, GROUPS)
    small_mean, small_momentum, small_after = outer_step(small, lax.optimization_barrier(jnp.sum(small_move, axis=0)), small_mom, GROUPS)
    block_out = block_outs.reshape(NSEQ, S2, D)
    input_grad = input_grads.reshape(NSEQ, S, D)
    return (block_out, input_grad, weight_new, weight_new.astype(jnp.bfloat16), weight_first, weight_second, weight_mean, weight_mom, small_after, small_first, small_second, small_mean, small_momentum)
```

```python
import functools

import jax
import jax.numpy as jnp
from jax import lax
from jax.experimental import pallas as pl
from jax.experimental.pallas import tpu as pltpu
from jax.sharding import PartitionSpec as P

STEP = 10


EPS_NORM = 1e-06
MASK_FILL = -1e30
BETA_ONE = 0.9
BETA_TWO = 0.999
ADAM_EPS = 1e-08
DECAY_RATE = 0.01
INNER_RATE = 0.03
SMALL_RATE = 0.6
OUTER_RATE = 0.7
MOMENTUM = 0.9
GELU_COEF = 0.7978845608028654
GELU_CUBE = 0.044715

BF = jnp.bfloat16
F32 = jnp.float32
VMEM_LIMIT = 60 * 1024 * 1024


def dot_nn(left, right):
    return lax.dot_general(left, right, (((1,), (0,)), ((), ())), preferred_element_type=F32)


def dot_nt(left, right):
    return lax.dot_general(left, right, (((1,), (1,)), ((), ())), preferred_element_type=F32)


def dot_tn(left, right):
    return lax.dot_general(left, right, (((0,), (0,)), ((), ())), preferred_element_type=F32)


def norm_parts(total):
    center = total - jnp.mean(total, axis=-1, keepdims=True)
    inverse = lax.rsqrt(jnp.mean(center * center, axis=-1, keepdims=True) + EPS_NORM)
    return center * inverse, inverse


def norm_back(grad, unit, inverse, gain):
    scaled = grad * gain
    lead = jnp.mean(scaled, axis=-1, keepdims=True)
    along = jnp.mean(scaled * unit, axis=-1, keepdims=True)
    return inverse * (scaled - lead - unit * along)


def fill_distance(dist_ref, key_step, query_step):
    shape = dist_ref.shape
    keys = lax.broadcasted_iota(jnp.int32, shape, 0) * key_step
    queries = lax.broadcasted_iota(jnp.int32, shape, 1) * query_step
    dist_ref[...] = jnp.abs(queries - keys).astype(F32)


def fill_mask(mask_ref, key_step, length):
    keys = lax.broadcasted_iota(jnp.int32, mask_ref.shape, 0) * key_step
    mask_ref[...] = jnp.where(keys < length, 0.0, MASK_FILL)


def pick_rows(pair_rows, which):
    half = pair_rows.shape[0] // 2
    zero = jnp.zeros((half, pair_rows.shape[1]), pair_rows.dtype)
    if which == 0:
        return jnp.concatenate([pair_rows[:half], zero], axis=0)
    return jnp.concatenate([zero, pair_rows[half:]], axis=0)


def lane_half(width, which):
    lanes = lax.broadcasted_iota(jnp.int32, (1, width), 1)
    inside = lanes < width // 2 if which == 0 else lanes >= width // 2
    return jnp.where(inside, 1.0, 0.0).astype(BF)


def pair_matrix(queries, keys, value, by_query):
    shape = (queries, keys) if by_query else (keys, queries)
    query_index = lax.broadcasted_iota(jnp.int32, shape, 0 if by_query else 1)
    key_index = lax.broadcasted_iota(jnp.int32, shape, 1 if by_query else 0)
    offset = key_index - 2 * query_index
    return jnp.where((offset == 0) | (offset == 1), value, 0.0).astype(BF)


def weight_copies(weight_hbm, weight_ref, sems, cuts):
    return [
        pltpu.make_async_copy(
            weight_hbm.at[pl.ds(cuts[index], cuts[index + 1] - cuts[index])],
            weight_ref.at[pl.ds(cuts[index], cuts[index + 1] - cuts[index])],
            sems.at[index],
        )
        for index in range(len(cuts) - 1)
    ]


def ahead_kernel(
    is_first,
    head_count,
    lengths_ref,
    slopes_ref,
    x_ref,
    gains_ref,
    weight_hbm,
    query_out,
    key_out,
    value_out,
    lse_out,
    att_out,
    total_one_out,
    hidden_out,
    slope_out,
    total_two_out,
    layer_out,
    weight_ref,
    dist_ref,
    mask_ref,
    query_t,
    value_t,
    att_t,
    sems,
):
    step = pl.program_id(0)
    width = weight_ref.shape[1]
    inner = (weight_ref.shape[0] - 4 * width) // 2
    queries, keys = query_out.shape[1], key_out.shape[1]
    head = width // head_count
    cuts = [0, width, 3 * width, 4 * width, 4 * width + inner, 4 * width + 2 * inner]
    copies = weight_copies(weight_hbm, weight_ref, sems, cuts)
    key_step = 1 if is_first else 2

    @pl.when(step == 0)
    def _():
        for copy in copies:
            copy.start()
        fill_distance(dist_ref, key_step, 2)

    def need(index):
        @pl.when(step == 0)
        def _():
            copies[index].wait()

    fill_mask(mask_ref, key_step, lengths_ref[step])
    if is_first:
        memory_low = x_ref[0]
        residual = dot_nn(pair_matrix(queries, keys, 0.5, True), memory_low)
        query_low = residual.astype(BF)
    else:
        residual = x_ref[0]
        query_low = residual.astype(BF)
        memory_low = query_low
    need(0)
    query_rows = dot_nn(query_low, weight_ref[0:width]).astype(BF)
    query_out[0] = query_rows
    query_t[...] = (query_rows.astype(F32) * float(head) ** (-0.5)).T.astype(BF)
    need(1)
    key_out[0] = dot_nn(memory_low, weight_ref[width : 2 * width]).astype(BF)
    value_rows = dot_nn(memory_low, weight_ref[2 * width : 3 * width]).astype(BF)
    value_out[0] = value_rows
    value_t[...] = value_rows.astype(F32).T.astype(BF)

    def pair_step(pair, carry):
        start = pl.multiple_of(pair * 2 * head, 2 * head)
        key_pair = key_out[0, :, pl.ds(start, 2 * head)]
        query_pair = query_t[pl.ds(start, 2 * head), :]
        for which in range(2):
            index = 2 * pair + which
            scores = dot_nn(key_pair, pick_rows(query_pair, which))
            scores = scores - slopes_ref[index] * dist_ref[...] + mask_ref[...]
            peak = jnp.max(scores, axis=0, keepdims=True)
            lifted = jnp.exp(scores - peak)
            total = jnp.sum(lifted, axis=0, keepdims=True)
            shares = (lifted * (1.0 / total)).astype(BF)
            rows = pl.ds(start + which * head, head)
            mixed = dot_nn(value_t[rows, :], shares)
            att_t[rows, :] = mixed
            lse_out[0, pl.ds(index, 1), :] = peak + jnp.log(total)
        return carry

    lax.fori_loop(0, head_count // 2, pair_step, 0)
    attended = att_t[...].T.astype(BF)
    att_out[0] = attended
    need(2)
    total_one = residual + dot_nn(attended, weight_ref[3 * width : 4 * width])
    total_one_out[0] = total_one
    unit, _ = norm_parts(total_one)
    normed = unit * gains_ref[0:1] + gains_ref[1:2]
    normed_low = normed.astype(BF)
    need(3)
    need(4)
    total_two = normed
    for chunk in range(inner // width):
        inner_rows = pl.ds(4 * width + chunk * width, width)
        outer_rows = pl.ds(4 * width + inner + chunk * width, width)
        pre = dot_nt(normed_low, weight_ref[inner_rows, :])
        square = pre * pre
        bend = jnp.tanh(pre * (GELU_COEF + (GELU_COEF * GELU_CUBE) * square))
        half = 0.5 + 0.5 * bend
        hidden = (pre * half).astype(BF)
        steep = half + (0.5 * pre) * (1.0 - bend * bend) * (
            GELU_COEF + (3.0 * GELU_COEF * GELU_CUBE) * square
        )
        columns = pl.ds(chunk * width, width)
        hidden_out[0, :, columns] = hidden
        slope_out[0, :, columns] = steep.astype(BF)
        total_two = total_two + dot_nn(hidden, weight_ref[outer_rows, :])
    total_two_out[0] = total_two
    unit_two, _ = norm_parts(total_two)
    result = unit_two * gains_ref[2:3] + gains_ref[3:4]
    layer_out[0] = result.astype(layer_out.dtype)


def layer_ahead(is_first, x, lengths, slopes, gains, weight_full, out_dtype):
    batch, memory_length, width = x.shape
    queries = memory_length // 2 if is_first else memory_length
    keys = memory_length
    head_count = slopes.shape[0]
    rows = weight_full.shape[0]
    inner = (rows - 4 * width) // 2
    head_rows = -(-head_count // 8) * 8

    def block(length, size):
        return pl.BlockSpec((1, length, size), lambda i, *_: (i, 0, 0))

    def shape(length, size, dtype):
        return jax.ShapeDtypeStruct((batch, length, size), dtype)

    outs = [
        (queries, width, BF),
        (keys, width, BF),
        (keys, width, BF),
        (head_rows, queries, F32),
        (queries, width, BF),
        (queries, width, F32),
        (queries, inner, BF),
        (queries, inner, BF),
        (queries, width, F32),
        (queries, width, out_dtype),
    ]
    flops = 2 * batch * width * (
        2 * queries * width + 2 * keys * width + 2 * queries * inner + 2 * queries * keys
    )
    return pl.pallas_call(
        functools.partial(ahead_kernel, is_first, head_count),
        grid_spec=pltpu.PrefetchScalarGridSpec(
            num_scalar_prefetch=2,
            grid=(batch,),
            in_specs=[
                block(memory_length, width),
                pl.BlockSpec((4, width), lambda i, *_: (0, 0)),
                pl.BlockSpec(memory_space=pl.ANY),
            ],
            out_specs=[block(length, size) for length, size, _ in outs],
            scratch_shapes=[
                pltpu.VMEM((rows, width), BF),
                pltpu.VMEM((keys, queries), F32),
                pltpu.VMEM((keys, queries), F32),
                pltpu.VMEM((width, queries), BF),
                pltpu.VMEM((width, keys), BF),
                pltpu.VMEM((width, queries), F32),
                pltpu.SemaphoreType.DMA((5,)),
            ],
        ),
        out_shape=[shape(*out) for out in outs],
        compiler_params=pltpu.CompilerParams(vmem_limit_bytes=VMEM_LIMIT),
        cost_estimate=pl.CostEstimate(
            flops=flops, bytes_accessed=rows * width * 2 + 30000000, transcendentals=0
        ),
        name="layer_ahead",
    )(lengths, slopes, x, gains, weight_full)


def back_kernel(
    is_first,
    head_count,
    lengths_ref,
    slopes_ref,
    grad_ref,
    total_two_ref,
    total_one_ref,
    slope_ref,
    query_ref,
    key_ref,
    value_ref,
    att_ref,
    lse_ref,
    gains_ref,
    weight_hbm,
    two_out,
    pre_out,
    normed_out,
    one_out,
    query_grad_out,
    key_grad_out,
    value_grad_out,
    input_out,
    gains_out,
    slopes_out,
    weight_ref,
    dist_ref,
    mask_ref,
    query_t,
    key_t,
    mixed_t,
    mixed_rows,
    delta_ref,
    query_grad_t,
    sems,
):
    step = pl.program_id(0)
    width = weight_ref.shape[1]
    inner = (weight_ref.shape[0] - 4 * width) // 2
    queries, keys = query_ref.shape[1], key_ref.shape[1]
    head = width // head_count
    cuts = [0, 3 * width, 4 * width, 4 * width + inner, 4 * width + 2 * inner]
    copies = weight_copies(weight_hbm, weight_ref, sems, cuts)
    key_step = 1 if is_first else 2
    scale = float(head) ** (-0.5)

    @pl.when(step == 0)
    def _():
        for index in (3, 2, 1, 0):
            copies[index].start()
        fill_distance(dist_ref, key_step, 2)
        gains_out[...] = jnp.zeros_like(gains_out)
        slopes_out[...] = jnp.zeros_like(slopes_out)

    def need(index):
        @pl.when(step == 0)
        def _():
            copies[index].wait()

    fill_mask(mask_ref, key_step, lengths_ref[step])
    query_t[...] = (query_ref[0].astype(F32) * scale).T.astype(BF)
    key_t[...] = key_ref[0].astype(F32).T.astype(BF)

    grad = grad_ref[0].astype(F32)
    unit_two, inverse_two = norm_parts(total_two_ref[0])
    gains_out[2:3] += jnp.sum(grad * unit_two, axis=0, keepdims=True)
    gains_out[3:4] += jnp.sum(grad, axis=0, keepdims=True)
    back_two = norm_back(grad, unit_two, inverse_two, gains_ref[2:3])
    two_low = back_two.astype(BF)
    two_out[0] = two_low
    need(3)
    need(2)
    back_normed = back_two
    for chunk in range(inner // width):
        inner_rows = pl.ds(4 * width + chunk * width, width)
        outer_rows = pl.ds(4 * width + inner + chunk * width, width)
        columns = pl.ds(chunk * width, width)
        back_hidden = dot_nt(two_low, weight_ref[outer_rows, :])
        pre_grad = (back_hidden * slope_ref[0, :, columns].astype(F32)).astype(BF)
        pre_out[0, :, columns] = pre_grad
        back_normed = back_normed + dot_nn(pre_grad, weight_ref[inner_rows, :])
    unit_one, inverse_one = norm_parts(total_one_ref[0])
    normed_out[0] = (unit_one * gains_ref[0:1] + gains_ref[1:2]).astype(BF)
    gains_out[0:1] += jnp.sum(back_normed * unit_one, axis=0, keepdims=True)
    gains_out[1:2] += jnp.sum(back_normed, axis=0, keepdims=True)
    back_one = norm_back(back_normed, unit_one, inverse_one, gains_ref[0:1])
    one_low = back_one.astype(BF)
    one_out[0] = one_low
    need(1)
    back_mixed = dot_nt(one_low, weight_ref[3 * width : 4 * width])
    mixed_low = back_mixed.astype(BF)
    mixed_rows[...] = mixed_low
    mixed_wide = mixed_low.astype(F32).T
    mixed_t[...] = mixed_wide.astype(BF)
    product = mixed_wide * att_ref[0].astype(F32).T
    delta_ref[...] = jnp.sum(product.reshape(head_count, head, queries), axis=1)

    def pair_step(pair, carry):
        start = pl.multiple_of(pair * 2 * head, 2 * head)
        lanes = pl.ds(start, 2 * head)
        key_pair = key_ref[0, :, lanes]
        value_pair = value_ref[0, :, lanes]
        query_pair = query_ref[0, :, lanes]
        mixed_pair = mixed_rows[:, lanes]
        query_pair_t = query_t[lanes, :]
        mixed_pair_t = mixed_t[lanes, :]
        key_grad = jnp.zeros((keys, 2 * head), F32)
        value_grad = jnp.zeros((keys, 2 * head), F32)
        for which in range(2):
            index = 2 * pair + which
            half = lane_half(2 * head, which)
            scores = dot_nn(key_pair, pick_rows(query_pair_t, which))
            scores = scores - slopes_ref[index] * dist_ref[...] + mask_ref[...]
            shares = jnp.exp(scores - lse_ref[0, pl.ds(index, 1), :])
            back_shares = dot_nn(value_pair, pick_rows(mixed_pair_t, which))
            back_scores = shares * (back_shares - delta_ref[pl.ds(index, 1), :])
            slopes_out[pl.ds(index, 1), :] += jnp.sum(
                back_scores * dist_ref[...], axis=0, keepdims=True
            )
            scores_low = back_scores.astype(BF)
            value_grad = value_grad + dot_nn(shares.astype(BF), mixed_pair * half)
            key_grad = key_grad + dot_nn(scores_low, query_pair * half)
            rows = pl.ds(start + which * head, head)
            query_grad_t[rows, :] = dot_nn(key_t[rows, :], scores_low)
        key_grad_out[0, :, lanes] = (key_grad * scale).astype(BF)
        value_grad_out[0, :, lanes] = value_grad.astype(BF)
        return carry

    lax.fori_loop(0, head_count // 2, pair_step, 0)
    query_grad = (query_grad_t[...] * scale).T.astype(BF)
    query_grad_out[0] = query_grad
    need(0)
    back_query = back_one + dot_nt(query_grad, weight_ref[0:width])
    back_memory = dot_nt(key_grad_out[0], weight_ref[width : 2 * width]) + dot_nt(
        value_grad_out[0], weight_ref[2 * width : 3 * width]
    )
    if is_first:
        spread = pair_matrix(queries, keys, 1.0, False)
        half_grad = back_query * 0.5
        upper = half_grad.astype(BF)
        lower = (half_grad - upper.astype(F32)).astype(BF)
        back_memory = back_memory + dot_nn(spread, upper) + dot_nn(spread, lower)
        input_out[0] = back_memory
    else:
        input_out[0] = back_query + back_memory


def layer_back(is_first, grad, kept, lengths, slopes, gains, weight_full):
    (query_rows, key_rows, value_rows, lse, attended, total_one, steep, total_two) = kept
    batch, queries, width = query_rows.shape
    keys = key_rows.shape[1]
    head_count = slopes.shape[0]
    rows = weight_full.shape[0]
    inner = (rows - 4 * width) // 2
    head_rows = lse.shape[1]

    def block(length, size):
        return pl.BlockSpec((1, length, size), lambda i, *_: (i, 0, 0))

    def shape(length, size, dtype):
        return jax.ShapeDtypeStruct((batch, length, size), dtype)

    outs = [
        (queries, width, BF),
        (queries, inner, BF),
        (queries, width, BF),
        (queries, width, BF),
        (queries, width, BF),
        (keys, width, BF),
        (keys, width, BF),
        (keys, width, F32),
    ]
    flops = 2 * batch * width * (
        2 * queries * width + 2 * keys * width + 2 * queries * inner + 5 * queries * keys
    )
    return pl.pallas_call(
        functools.partial(back_kernel, is_first, head_count),
        grid_spec=pltpu.PrefetchScalarGridSpec(
            num_scalar_prefetch=2,
            grid=(batch,),
            in_specs=[
                block(queries, width),
                block(queries, width),
                block(queries, width),
                block(queries, inner),
                block(queries, width),
                block(keys, width),
                block(keys, width),
                block(queries, width),
                block(head_rows, queries),
                pl.BlockSpec((4, width), lambda i, *_: (0, 0)),
                pl.BlockSpec(memory_space=pl.ANY),
            ],
            out_specs=[block(length, size) for length, size, _ in outs]
            + [
                pl.BlockSpec((4, width), lambda i, *_: (0, 0)),
                pl.BlockSpec((head_rows, queries), lambda i, *_: (0, 0)),
            ],
            scratch_shapes=[
                pltpu.VMEM((rows, width), BF),
                pltpu.VMEM((keys, queries), F32),
                pltpu.VMEM((keys, queries), F32),
                pltpu.VMEM((width, queries), BF),
                pltpu.VMEM((width, keys), BF),
                pltpu.VMEM((width, queries), BF),
                pltpu.VMEM((queries, width), BF),
                pltpu.VMEM((head_count, queries), F32),
                pltpu.VMEM((width, queries), F32),
                pltpu.SemaphoreType.DMA((4,)),
            ],
        ),
        out_shape=[shape(*out) for out in outs]
        + [
            jax.ShapeDtypeStruct((4, width), F32),
            jax.ShapeDtypeStruct((head_rows, queries), F32),
        ],
        compiler_params=pltpu.CompilerParams(vmem_limit_bytes=VMEM_LIMIT),
        cost_estimate=pl.CostEstimate(
            flops=flops, bytes_accessed=rows * width * 2 + 40000000, transcendentals=0
        ),
        name="layer_back",
    )(
        lengths,
        slopes,
        grad,
        total_two,
        total_one,
        steep,
        query_rows,
        key_rows,
        value_rows,
        attended,
        lse,
        gains,
        weight_full,
    )


def weight_product(left, right):
    return lax.dot_general(
        left, right, (((0, 1), (0, 1)), ((), ())), preferred_element_type=F32
    )


def matrix_gradient(query_low, memory_low, attended, hidden, back):
    (two_low, pre_grad, normed_low, one_low, query_grad, key_grad, value_grad) = back
    return jnp.concatenate(
        [
            weight_product(query_low, query_grad),
            weight_product(memory_low, key_grad),
            weight_product(memory_low, value_grad),
            weight_product(attended, one_low),
            weight_product(pre_grad, normed_low),
            weight_product(hidden, two_low),
        ],
        axis=0,
    )


def adam_step(master, gradient, first_mom, second_mom, rate):
    first_new = BETA_ONE * first_mom + (1.0 - BETA_ONE) * gradient
    second_new = BETA_TWO * second_mom + (1.0 - BETA_TWO) * gradient * gradient
    first_hat = first_new / (1.0 - BETA_ONE**STEP)
    second_hat = second_new / (1.0 - BETA_TWO**STEP)
    inner_move = rate * (first_hat / (jnp.sqrt(second_hat) + ADAM_EPS) + DECAY_RATE * master)
    return (first_new, second_new, inner_move)


def outer_step(master, moves_sum, momentum_old, group_count):
    mean_move = moves_sum / group_count
    momentum_new = MOMENTUM * momentum_old + mean_move
    return (mean_move, momentum_new, master - OUTER_RATE * (mean_move + MOMENTUM * momentum_new))


def shards(
    hidden_in,
    lengths,
    out_grad,
    weights,
    weight_m,
    weight_v,
    outer_mom,
    small,
    small_m,
    small_v,
    small_mom,
):
    width = weights.shape[2]
    part_size = small.shape[0] // 2
    masters_low = weights.astype(BF)

    def fetch(layer_index):
        return lax.all_gather(masters_low[layer_index], "fsdp", axis=0, tiled=True)

    def reduce_layer(grad_rows):
        return lax.psum_scatter(
            grad_rows.astype(BF), "fsdp", scatter_dimension=0, tiled=True
        ).astype(F32)

    gains = []
    slopes = []
    for layer in range(2):
        part = small[layer * part_size : (layer + 1) * part_size]
        gains.append(part[: 4 * width].reshape(4, width))
        slopes.append(part[4 * width :])

    matrix_one = fetch(0)
    matrix_two = fetch(1)
    (q1, k1, v1, lse1, att1, one1, hid1, steep1, two1, first_out) = layer_ahead(
        True, hidden_in, lengths, slopes[0], gains[0], matrix_one, F32
    )
    (q2, k2, v2, lse2, att2, one2, hid2, steep2, two2, block_out) = layer_ahead(
        False, first_out, lengths, slopes[1], gains[1], matrix_two, BF
    )
    back_two = layer_back(
        False,
        out_grad,
        (q2, k2, v2, lse2, att2, one2, steep2, two2),
        lengths,
        slopes[1],
        gains[1],
        matrix_two,
    )
    first_low = first_out.astype(BF)
    shard_two = reduce_layer(matrix_gradient(first_low, first_low, att2, hid2, back_two[:7]))
    back_one = layer_back(
        True,
        back_two[7],
        (q1, k1, v1, lse1, att1, one1, steep1, two1),
        lengths,
        slopes[0],
        gains[0],
        matrix_one,
    )
    input_grad = back_one[7]
    hidden_wide = hidden_in.astype(F32)
    pooled_low = ((hidden_wide[:, 0::2] + hidden_wide[:, 1::2]) * 0.5).astype(BF)
    shard_one = reduce_layer(matrix_gradient(pooled_low, hidden_in, att1, hid1, back_one[:7]))
    grad_shard = jnp.stack([shard_one, shard_two])
    head_count = slopes[0].shape[0]
    small_parts = []
    for back in (back_one, back_two):
        small_parts += [back[8].reshape(-1), -jnp.sum(back[9][:head_count], axis=1)]
    small_grad = lax.psum(jnp.concatenate(small_parts), "fsdp")
    weight_first, weight_second, weight_move = adam_step(
        weights, grad_shard[None], weight_m, weight_v, INNER_RATE
    )
    small_first, small_second, small_move = adam_step(
        small, small_grad[None], small_m, small_v, SMALL_RATE
    )
    weight_sum, small_sum = (
        lax.psum(weight_move[0].astype(BF), "group").astype(F32),
        lax.psum(small_move[0].astype(BF), "group").astype(F32),
    )
    group_count = lax.axis_size("group")
    weight_mean, weight_mom, weight_new = outer_step(weights, weight_sum, outer_mom, group_count)
    small_mean, small_momentum, small_after = outer_step(small, small_sum, small_mom, group_count)
    return (
        block_out,
        input_grad,
        weight_new,
        weight_new.astype(BF),
        weight_first,
        weight_second,
        weight_mean,
        weight_mom,
        small_after,
        small_first,
        small_second,
        small_mean,
        small_momentum,
    )


def solution(mesh):
    in_specs = (
        P(("group", "fsdp"), None, None),
        P(("group", "fsdp")),
        P(("group", "fsdp"), None, None),
        P(None, "fsdp", None),
        P("group", None, "fsdp", None),
        P("group", None, "fsdp", None),
        P(None, "fsdp", None),
        P(),
        P("group", None),
        P("group", None),
        P(),
    )
    out_specs = (
        P(("group", "fsdp"), None, None),
        P(("group", "fsdp"), None, None),
        P(None, "fsdp", None),
        P(None, "fsdp", None),
        P("group", None, "fsdp", None),
        P("group", None, "fsdp", None),
        P(None, "fsdp", None),
        P(None, "fsdp", None),
        P(),
        P("group", None),
        P("group", None),
        P(),
        P(),
    )
    return jax.shard_map(shards, mesh=mesh, in_specs=in_specs, out_specs=out_specs, check_vma=False)
```

```python
import functools

import jax
import jax.numpy as jnp
from jax import lax
from jax.experimental import pallas as pl
from jax.experimental.pallas import tpu as pltpu
from jax.sharding import PartitionSpec as P

STEP = 10


EPS_NORM = 1e-06
MASK_FILL = -1e30
BETA_ONE = 0.9
BETA_TWO = 0.999
ADAM_EPS = 1e-08
DECAY_RATE = 0.01
INNER_RATE = 0.03
SMALL_RATE = 0.6
OUTER_RATE = 0.7
MOMENTUM = 0.9
GELU_COEF = 0.7978845608028654
GELU_CUBE = 0.044715

BF = jnp.bfloat16
F32 = jnp.float32
VMEM_LIMIT = 60 * 1024 * 1024
MESH_ID = pl.DeviceIdType.MESH


def dot_nn(left, right):
    return lax.dot_general(left, right, (((1,), (0,)), ((), ())), preferred_element_type=F32)


def dot_nt(left, right):
    return lax.dot_general(left, right, (((1,), (1,)), ((), ())), preferred_element_type=F32)


def dot_tn(left, right):
    return lax.dot_general(left, right, (((0,), (0,)), ((), ())), preferred_element_type=F32)


def norm_parts(total):
    center = total - jnp.mean(total, axis=-1, keepdims=True)
    inverse = lax.rsqrt(jnp.mean(center * center, axis=-1, keepdims=True) + EPS_NORM)
    return center * inverse, inverse


def norm_back(grad, unit, inverse, gain):
    scaled = grad * gain
    lead = jnp.mean(scaled, axis=-1, keepdims=True)
    along = jnp.mean(scaled * unit, axis=-1, keepdims=True)
    return inverse * (scaled - lead - unit * along)


def fill_distance(dist_ref, key_step, query_step):
    shape = dist_ref.shape
    keys = lax.broadcasted_iota(jnp.int32, shape, 0) * key_step
    queries = lax.broadcasted_iota(jnp.int32, shape, 1) * query_step
    dist_ref[...] = jnp.abs(queries - keys).astype(F32)


def fill_mask(mask_ref, key_step, length):
    keys = lax.broadcasted_iota(jnp.int32, mask_ref.shape, 0) * key_step
    mask_ref[...] = jnp.where(keys < length, 0.0, MASK_FILL)


def pick_rows(pair_rows, which):
    half = pair_rows.shape[0] // 2
    zero = jnp.zeros((half, pair_rows.shape[1]), pair_rows.dtype)
    if which == 0:
        return jnp.concatenate([pair_rows[:half], zero], axis=0)
    return jnp.concatenate([zero, pair_rows[half:]], axis=0)


def lane_half(width, which):
    lanes = lax.broadcasted_iota(jnp.int32, (1, width), 1)
    inside = lanes < width // 2 if which == 0 else lanes >= width // 2
    return jnp.where(inside, 1.0, 0.0).astype(BF)


def pair_matrix(queries, keys, value, by_query):
    shape = (queries, keys) if by_query else (keys, queries)
    query_index = lax.broadcasted_iota(jnp.int32, shape, 0 if by_query else 1)
    key_index = lax.broadcasted_iota(jnp.int32, shape, 1 if by_query else 0)
    offset = key_index - 2 * query_index
    return jnp.where((offset == 0) | (offset == 1), value, 0.0).astype(BF)


def remote(source, target, send_sem, recv_sem, device):
    return pltpu.make_async_remote_copy(
        src_ref=source,
        dst_ref=target,
        send_sem=send_sem,
        recv_sem=recv_sem,
        device_id=device,
        device_id_type=pl.DeviceIdType.MESH,
    )


class Spot:
    def __init__(self, chips, group_count):
        self.chips = chips
        self.group_count = group_count
        self.group = lax.axis_index("group")
        self.member = lax.axis_index("fsdp")
        self.chip = self.member // 2
        self.core = self.member % 2

    def line(self, chip):
        return {"fsdp": 2 * chip + self.core}

    def partner(self):
        return {"fsdp": 2 * self.chip + 1 - self.core}

    def other(self, turn):
        return {"group": lax.rem(self.group + turn, self.group_count)}

    def back_group(self, turn):
        return lax.rem(self.group + self.group_count - turn, self.group_count)

    def ahead_chip(self, hop):
        return lax.rem(self.chip + hop, self.chips)

    def back_chip(self, hop):
        return lax.rem(self.chip + self.chips - hop, self.chips)


def meet(spot):
    barrier = pltpu.get_barrier_semaphore()
    for hop in range(1, spot.chips):
        pl.semaphore_signal(
            barrier, inc=1, device_id=spot.line(spot.ahead_chip(hop)), device_id_type=MESH_ID
        )
    pl.semaphore_signal(barrier, inc=1, device_id=spot.partner(), device_id_type=MESH_ID)
    for turn in range(1, spot.group_count):
        pl.semaphore_signal(barrier, inc=1, device_id=spot.other(turn), device_id_type=MESH_ID)
    pl.semaphore_wait(barrier, spot.chips - 1 + 1 + spot.group_count - 1)


class Gather:
    def __init__(self, spot, shard_ref, full_ref, sems):
        self.spot = spot
        self.shard = shard_ref
        self.full = full_ref
        self.line_send, self.line_recv, self.cross_send, self.cross_recv = sems[:4]
        self.core_send, self.core_recv, self.own_sem = sems[4:]
        self.rows = shard_ref.shape[0]
        self.part = self.rows // spot.group_count
        self.tick_count = 2 * spot.chips

    def piece(self, chip, core, group):
        start = (2 * chip + core) * self.rows + group * self.part
        return self.full.at[pl.ds(start, self.part)]

    def whole(self, chip, core):
        return self.full.at[pl.ds((2 * chip + core) * self.rows, self.rows)]

    def line_copy(self, hop):
        spot = self.spot
        return remote(
            self.shard.at[pl.ds(spot.group * self.part, self.part)],
            self.piece(spot.chip, spot.core, spot.group),
            self.line_send.at[hop],
            self.line_recv.at[hop],
            spot.line(spot.ahead_chip(hop)),
        )

    def line_arrival(self, hop):
        spot = self.spot
        here = self.piece(spot.back_chip(hop), spot.core, spot.group)
        return remote(
            here, here, self.line_send.at[hop], self.line_recv.at[hop], spot.partner()
        )

    def cross_copy(self, hop, turn):
        spot = self.spot
        here = self.piece(spot.back_chip(hop), spot.core, spot.group)
        slot = hop * spot.group_count + turn
        return remote(
            here, here, self.cross_send.at[slot], self.cross_recv.at[slot], spot.other(turn)
        )

    def cross_arrival(self, hop, turn):
        spot = self.spot
        here = self.piece(spot.back_chip(hop), spot.core, spot.back_group(turn))
        slot = hop * spot.group_count + turn
        return remote(
            here, here, self.cross_send.at[slot], self.cross_recv.at[slot], spot.partner()
        )

    def core_copy(self, hop, turn):
        spot = self.spot
        slot = hop * spot.group_count + turn
        if hop == 0:
            source, target = self.shard, self.whole(spot.chip, spot.core)
        else:
            source = self.piece(spot.back_chip(hop), spot.core, spot.back_group(turn))
            target = source
        return remote(
            source, target, self.core_send.at[slot], self.core_recv.at[slot], spot.partner()
        )

    def core_arrival(self, hop, turn):
        spot = self.spot
        slot = hop * spot.group_count + turn
        if hop == 0:
            here = self.whole(spot.chip, 1 - spot.core)
        else:
            here = self.piece(spot.back_chip(hop), 1 - spot.core, spot.back_group(turn))
        return remote(
            here, here, self.core_send.at[slot], self.core_recv.at[slot], spot.partner()
        )

    def own_copy(self):
        return pltpu.make_async_copy(
            self.shard, self.whole(self.spot.chip, self.spot.core), self.own_sem.at[0]
        )

    def tick(self, index):
        chips, groups = self.spot.chips, self.spot.group_count
        if index == 0:
            for hop in range(1, chips):
                self.line_copy(hop).start()
            self.core_copy(0, 0).start()
            self.own_copy().start()
        elif index < chips:
            hop = index
            self.line_arrival(hop).wait_recv()
            for turn in range(1, groups):
                self.cross_copy(hop, turn).start()
            self.core_copy(hop, 0).start()
        elif index < 2 * chips - 1:
            hop = index - chips + 1
            for turn in range(1, groups):
                self.cross_arrival(hop, turn).wait_recv()
                self.core_copy(hop, turn).start()
        else:
            self.own_copy().wait()
            self.core_copy(0, 0).wait_send()
            self.core_arrival(0, 0).wait_recv()
            for hop in range(1, chips):
                self.line_copy(hop).wait_send()
                self.core_copy(hop, 0).wait_send()
                self.core_arrival(hop, 0).wait_recv()
                for turn in range(1, groups):
                    self.cross_copy(hop, turn).wait_send()
                    self.core_copy(hop, turn).wait_send()
                    self.core_arrival(hop, turn).wait_recv()


def gather_sems(chips, group_count):
    dma = pltpu.SemaphoreType.DMA
    crossing = (chips * group_count,)
    return [dma((chips,)), dma((chips,))] + [dma(crossing)] * 4 + [dma((1,))]


def gather_kernel(chips, group_count, shard_ref, full_ref, *sems):
    spot = Spot(chips, group_count)
    job = Gather(spot, shard_ref, full_ref, sems)
    meet(spot)
    for index in range(job.tick_count):
        job.tick(index)


def gather_rows(shard):
    members, group_count = lax.axis_size("fsdp"), lax.axis_size("group")
    rows, width = shard.shape
    return pl.pallas_call(
        functools.partial(gather_kernel, members // 2, group_count),
        out_shape=jax.ShapeDtypeStruct((rows * members, width), BF),
        in_specs=[pl.BlockSpec(memory_space=pl.ANY)],
        out_specs=pl.BlockSpec(memory_space=pl.ANY),
        scratch_shapes=gather_sems(members // 2, group_count),
        compiler_params=pltpu.CompilerParams(collective_id=0, has_side_effects=True),
        name="gather_rows",
    )(shard)


def weight_copies(weight_hbm, weight_ref, sems, cuts):
    return [
        pltpu.make_async_copy(
            weight_hbm.at[pl.ds(cuts[index], cuts[index + 1] - cuts[index])],
            weight_ref.at[pl.ds(cuts[index], cuts[index + 1] - cuts[index])],
            sems.at[index],
        )
        for index in range(len(cuts) - 1)
    ]


def ahead_kernel(
    is_first,
    head_count,
    place,
    lengths_ref,
    slopes_ref,
    x_ref,
    gains_ref,
    weight_hbm,
    *rest,
):
    if place is not None:
        shard_ref, rest = rest[0], rest[1:]
        full_ref, rest = rest[11], rest[:11] + rest[12:]
        job_sems = rest[18:]
    (
        query_out,
    key_out,
    value_out,
    lse_out,
    att_out,
    total_one_out,
    hidden_out,
    slope_out,
    total_two_out,
    layer_out,
    low_out,
    weight_ref,
    dist_ref,
    mask_ref,
    query_t,
    value_t,
    att_t,
    sems,
    ) = rest[:18]
    step = pl.program_id(0)
    if place is not None:
        spot = Spot(*place)
        job = Gather(spot, shard_ref, full_ref, job_sems)
        spread = [round(index * 7 / (job.tick_count - 1)) for index in range(job.tick_count)]

    def tick(quarter):
        if place is None:
            return
        for index in range(job.tick_count):
            if spread[index] % 2 == quarter:

                @pl.when(step == spread[index] // 2)
                def _():
                    if index == 0:
                        meet(spot)
                    job.tick(index)

    tick(0)
    width = weight_ref.shape[1]
    inner = (weight_ref.shape[0] - 4 * width) // 2
    queries, keys = query_out.shape[1], key_out.shape[1]
    head = width // head_count
    cuts = [0, width, 3 * width, 4 * width, 4 * width + inner, 4 * width + 2 * inner]
    copies = weight_copies(weight_hbm, weight_ref, sems, cuts)
    key_step = 1 if is_first else 2

    @pl.when(step == 0)
    def _():
        for copy in copies:
            copy.start()
        fill_distance(dist_ref, key_step, 2)

    def need(index):
        @pl.when(step == 0)
        def _():
            copies[index].wait()

    fill_mask(mask_ref, key_step, lengths_ref[step])
    if is_first:
        memory_low = x_ref[0]
        residual = dot_nn(pair_matrix(queries, keys, 0.5, True), memory_low)
        query_low = residual.astype(BF)
    else:
        residual = x_ref[0]
        query_low = residual.astype(BF)
        memory_low = query_low
    low_out[0] = query_low
    need(0)
    query_rows = dot_nn(query_low, weight_ref[0:width]).astype(BF)
    query_out[0] = query_rows
    query_t[...] = (query_rows.astype(F32) * float(head) ** (-0.5)).T.astype(BF)
    need(1)
    key_out[0] = dot_nn(memory_low, weight_ref[width : 2 * width]).astype(BF)
    value_rows = dot_nn(memory_low, weight_ref[2 * width : 3 * width]).astype(BF)
    value_out[0] = value_rows
    value_t[...] = value_rows.astype(F32).T.astype(BF)

    def pair_step(pair, carry):
        start = pl.multiple_of(pair * 2 * head, 2 * head)
        key_pair = key_out[0, :, pl.ds(start, 2 * head)]
        query_pair = query_t[pl.ds(start, 2 * head), :]
        for which in range(2):
            index = 2 * pair + which
            scores = dot_nn(key_pair, pick_rows(query_pair, which))
            scores = scores - slopes_ref[index] * dist_ref[...] + mask_ref[...]
            peak = jnp.max(scores, axis=0, keepdims=True)
            lifted = jnp.exp(scores - peak)
            total = jnp.sum(lifted, axis=0, keepdims=True)
            shares = (lifted * (1.0 / total)).astype(BF)
            rows = pl.ds(start + which * head, head)
            mixed = dot_nn(value_t[rows, :], shares)
            att_t[rows, :] = mixed
            lse_out[0, pl.ds(index, 1), :] = peak + jnp.log(total)
        return carry

    lax.fori_loop(0, head_count // 2, pair_step, 0)
    attended = att_t[...].T.astype(BF)
    att_out[0] = attended
    need(2)
    total_one = residual + dot_nn(attended, weight_ref[3 * width : 4 * width])
    total_one_out[0] = total_one
    unit, _ = norm_parts(total_one)
    normed = unit * gains_ref[0:1] + gains_ref[1:2]
    normed_low = normed.astype(BF)
    need(3)
    need(4)
    total_two = normed
    for chunk in range(inner // width):
        inner_rows = pl.ds(4 * width + chunk * width, width)
        outer_rows = pl.ds(4 * width + inner + chunk * width, width)
        pre = dot_nt(normed_low, weight_ref[inner_rows, :])
        square = pre * pre
        bend = jnp.tanh(pre * (GELU_COEF + (GELU_COEF * GELU_CUBE) * square))
        half = 0.5 + 0.5 * bend
        hidden = (pre * half).astype(BF)
        steep = half + (0.5 * pre) * (1.0 - bend * bend) * (
            GELU_COEF + (3.0 * GELU_COEF * GELU_CUBE) * square
        )
        columns = pl.ds(chunk * width, width)
        hidden_out[0, :, columns] = hidden
        slope_out[0, :, columns] = steep.astype(BF)
        total_two = total_two + dot_nn(hidden, weight_ref[outer_rows, :])
    total_two_out[0] = total_two
    unit_two, _ = norm_parts(total_two)
    result = unit_two * gains_ref[2:3] + gains_ref[3:4]
    layer_out[0] = result.astype(layer_out.dtype)
    tick(1)


def layer_ahead(is_first, x, lengths, slopes, gains, weight_full, out_dtype, shard=None):
    batch, memory_length, width = x.shape
    queries = memory_length // 2 if is_first else memory_length
    keys = memory_length
    head_count = slopes.shape[0]
    rows = weight_full.shape[0]
    inner = (rows - 4 * width) // 2
    head_rows = -(-head_count // 8) * 8

    def block(length, size):
        return pl.BlockSpec((1, length, size), lambda i, *_: (i, 0, 0))

    def shape(length, size, dtype):
        return jax.ShapeDtypeStruct((batch, length, size), dtype)

    outs = [
        (queries, width, BF),
        (keys, width, BF),
        (keys, width, BF),
        (head_rows, queries, F32),
        (queries, width, BF),
        (queries, width, F32),
        (queries, inner, BF),
        (queries, inner, BF),
        (queries, width, F32),
        (queries, width, out_dtype),
        (queries, width, BF),
    ]
    flops = 2 * batch * width * (
        2 * queries * width + 2 * keys * width + 2 * queries * inner + 2 * queries * keys
    )
    hosted = shard is not None
    place = (lax.axis_size("fsdp") // 2, lax.axis_size("group")) if hosted else None
    anywhere = [pl.BlockSpec(memory_space=pl.ANY)] * hosted
    full_shape = [jax.ShapeDtypeStruct((rows, width), BF)] * hosted
    job_sems = gather_sems(*place) if hosted else []
    params = dict(collective_id=1, has_side_effects=True) if hosted else {}
    return pl.pallas_call(
        functools.partial(ahead_kernel, is_first, head_count, place),
        grid_spec=pltpu.PrefetchScalarGridSpec(
            num_scalar_prefetch=2,
            grid=(batch,),
            in_specs=[
                block(memory_length, width),
                pl.BlockSpec((4, width), lambda i, *_: (0, 0)),
                pl.BlockSpec(memory_space=pl.ANY),
            ]
            + anywhere,
            out_specs=[block(length, size) for length, size, _ in outs] + anywhere,
            scratch_shapes=[
                pltpu.VMEM((rows, width), BF),
                pltpu.VMEM((keys, queries), F32),
                pltpu.VMEM((keys, queries), F32),
                pltpu.VMEM((width, queries), BF),
                pltpu.VMEM((width, keys), BF),
                pltpu.VMEM((width, queries), F32),
                pltpu.SemaphoreType.DMA((5,)),
            ]
            + job_sems,
        ),
        out_shape=[shape(*out) for out in outs] + full_shape,
        compiler_params=pltpu.CompilerParams(vmem_limit_bytes=VMEM_LIMIT, **params),
        cost_estimate=pl.CostEstimate(
            flops=flops, bytes_accessed=rows * width * 2 + 30000000, transcendentals=0
        ),
        name="layer_ahead",
    )(lengths, slopes, x, gains, weight_full, *([shard] * hosted))


def back_kernel(
    is_first,
    head_count,
    lengths_ref,
    slopes_ref,
    grad_ref,
    total_two_ref,
    total_one_ref,
    slope_ref,
    query_ref,
    key_ref,
    value_ref,
    att_ref,
    lse_ref,
    gains_ref,
    weight_hbm,
    two_out,
    pre_out,
    normed_out,
    one_out,
    query_grad_out,
    key_grad_out,
    value_grad_out,
    input_out,
    gains_out,
    slopes_out,
    weight_ref,
    dist_ref,
    mask_ref,
    query_t,
    key_t,
    mixed_t,
    mixed_rows,
    delta_ref,
    query_grad_t,
    sems,
):
    step = pl.program_id(0)
    width = weight_ref.shape[1]
    inner = (weight_ref.shape[0] - 4 * width) // 2
    queries, keys = query_ref.shape[1], key_ref.shape[1]
    head = width // head_count
    cuts = [0, 3 * width, 4 * width, 4 * width + inner, 4 * width + 2 * inner]
    copies = weight_copies(weight_hbm, weight_ref, sems, cuts)
    key_step = 1 if is_first else 2
    scale = float(head) ** (-0.5)

    @pl.when(step == 0)
    def _():
        for index in (3, 2, 1, 0):
            copies[index].start()
        fill_distance(dist_ref, key_step, 2)
        gains_out[...] = jnp.zeros_like(gains_out)
        slopes_out[...] = jnp.zeros_like(slopes_out)

    def need(index):
        @pl.when(step == 0)
        def _():
            copies[index].wait()

    fill_mask(mask_ref, key_step, lengths_ref[step])
    query_t[...] = (query_ref[0].astype(F32) * scale).T.astype(BF)
    key_t[...] = key_ref[0].astype(F32).T.astype(BF)

    grad = grad_ref[0].astype(F32)
    unit_two, inverse_two = norm_parts(total_two_ref[0])
    gains_out[2:3] += jnp.sum(grad * unit_two, axis=0, keepdims=True)
    gains_out[3:4] += jnp.sum(grad, axis=0, keepdims=True)
    back_two = norm_back(grad, unit_two, inverse_two, gains_ref[2:3])
    two_low = back_two.astype(BF)
    two_out[0] = two_low
    need(3)
    need(2)
    back_normed = back_two
    for chunk in range(inner // width):
        inner_rows = pl.ds(4 * width + chunk * width, width)
        outer_rows = pl.ds(4 * width + inner + chunk * width, width)
        columns = pl.ds(chunk * width, width)
        back_hidden = dot_nt(two_low, weight_ref[outer_rows, :])
        pre_grad = (back_hidden * slope_ref[0, :, columns].astype(F32)).astype(BF)
        pre_out[0, :, columns] = pre_grad
        back_normed = back_normed + dot_nn(pre_grad, weight_ref[inner_rows, :])
    unit_one, inverse_one = norm_parts(total_one_ref[0])
    normed_out[0] = (unit_one * gains_ref[0:1] + gains_ref[1:2]).astype(BF)
    gains_out[0:1] += jnp.sum(back_normed * unit_one, axis=0, keepdims=True)
    gains_out[1:2] += jnp.sum(back_normed, axis=0, keepdims=True)
    back_one = norm_back(back_normed, unit_one, inverse_one, gains_ref[0:1])
    one_low = back_one.astype(BF)
    one_out[0] = one_low
    need(1)
    back_mixed = dot_nt(one_low, weight_ref[3 * width : 4 * width])
    mixed_low = back_mixed.astype(BF)
    mixed_rows[...] = mixed_low
    mixed_wide = mixed_low.astype(F32).T
    mixed_t[...] = mixed_wide.astype(BF)
    product = mixed_wide * att_ref[0].astype(F32).T
    delta_ref[...] = jnp.sum(product.reshape(head_count, head, queries), axis=1)

    def pair_step(pair, carry):
        start = pl.multiple_of(pair * 2 * head, 2 * head)
        lanes = pl.ds(start, 2 * head)
        key_pair = key_ref[0, :, lanes]
        value_pair = value_ref[0, :, lanes]
        query_pair = query_ref[0, :, lanes]
        mixed_pair = mixed_rows[:, lanes]
        query_pair_t = query_t[lanes, :]
        mixed_pair_t = mixed_t[lanes, :]
        key_grad = jnp.zeros((keys, 2 * head), F32)
        value_grad = jnp.zeros((keys, 2 * head), F32)
        for which in range(2):
            index = 2 * pair + which
            half = lane_half(2 * head, which)
            scores = dot_nn(key_pair, pick_rows(query_pair_t, which))
            scores = scores - slopes_ref[index] * dist_ref[...] + mask_ref[...]
            shares = jnp.exp(scores - lse_ref[0, pl.ds(index, 1), :])
            back_shares = dot_nn(value_pair, pick_rows(mixed_pair_t, which))
            back_scores = shares * (back_shares - delta_ref[pl.ds(index, 1), :])
            slopes_out[pl.ds(index, 1), :] += jnp.sum(
                back_scores * dist_ref[...], axis=0, keepdims=True
            )
            scores_low = back_scores.astype(BF)
            value_grad = value_grad + dot_nn(shares.astype(BF), mixed_pair * half)
            key_grad = key_grad + dot_nn(scores_low, query_pair * half)
            rows = pl.ds(start + which * head, head)
            query_grad_t[rows, :] = dot_nn(key_t[rows, :], scores_low)
        key_grad_out[0, :, lanes] = (key_grad * scale).astype(BF)
        value_grad_out[0, :, lanes] = value_grad.astype(BF)
        return carry

    lax.fori_loop(0, head_count // 2, pair_step, 0)
    query_grad = (query_grad_t[...] * scale).T.astype(BF)
    query_grad_out[0] = query_grad
    need(0)
    back_query = back_one + dot_nt(query_grad, weight_ref[0:width])
    back_memory = dot_nt(key_grad_out[0], weight_ref[width : 2 * width]) + dot_nt(
        value_grad_out[0], weight_ref[2 * width : 3 * width]
    )
    if is_first:
        spread = pair_matrix(queries, keys, 1.0, False)
        half_grad = back_query * 0.5
        upper = half_grad.astype(BF)
        lower = (half_grad - upper.astype(F32)).astype(BF)
        back_memory = back_memory + dot_nn(spread, upper) + dot_nn(spread, lower)
        input_out[0] = back_memory
    else:
        input_out[0] = back_query + back_memory


def layer_back(is_first, grad, kept, lengths, slopes, gains, weight_full):
    (query_rows, key_rows, value_rows, lse, attended, total_one, steep, total_two) = kept
    batch, queries, width = query_rows.shape
    keys = key_rows.shape[1]
    head_count = slopes.shape[0]
    rows = weight_full.shape[0]
    inner = (rows - 4 * width) // 2
    head_rows = lse.shape[1]

    def block(length, size):
        return pl.BlockSpec((1, length, size), lambda i, *_: (i, 0, 0))

    def shape(length, size, dtype):
        return jax.ShapeDtypeStruct((batch, length, size), dtype)

    outs = [
        (queries, width, BF),
        (queries, inner, BF),
        (queries, width, BF),
        (queries, width, BF),
        (queries, width, BF),
        (keys, width, BF),
        (keys, width, BF),
        (keys, width, F32),
    ]
    flops = 2 * batch * width * (
        2 * queries * width + 2 * keys * width + 2 * queries * inner + 5 * queries * keys
    )
    return pl.pallas_call(
        functools.partial(back_kernel, is_first, head_count),
        grid_spec=pltpu.PrefetchScalarGridSpec(
            num_scalar_prefetch=2,
            grid=(batch,),
            in_specs=[
                block(queries, width),
                block(queries, width),
                block(queries, width),
                block(queries, inner),
                block(queries, width),
                block(keys, width),
                block(keys, width),
                block(queries, width),
                block(head_rows, queries),
                pl.BlockSpec((4, width), lambda i, *_: (0, 0)),
                pl.BlockSpec(memory_space=pl.ANY),
            ],
            out_specs=[block(length, size) for length, size, _ in outs]
            + [
                pl.BlockSpec((4, width), lambda i, *_: (0, 0)),
                pl.BlockSpec((head_rows, queries), lambda i, *_: (0, 0)),
            ],
            scratch_shapes=[
                pltpu.VMEM((rows, width), BF),
                pltpu.VMEM((keys, queries), F32),
                pltpu.VMEM((keys, queries), F32),
                pltpu.VMEM((width, queries), BF),
                pltpu.VMEM((width, keys), BF),
                pltpu.VMEM((width, queries), BF),
                pltpu.VMEM((queries, width), BF),
                pltpu.VMEM((head_count, queries), F32),
                pltpu.VMEM((width, queries), F32),
                pltpu.SemaphoreType.DMA((4,)),
            ],
        ),
        out_shape=[shape(*out) for out in outs]
        + [
            jax.ShapeDtypeStruct((4, width), F32),
            jax.ShapeDtypeStruct((head_rows, queries), F32),
        ],
        compiler_params=pltpu.CompilerParams(vmem_limit_bytes=VMEM_LIMIT),
        cost_estimate=pl.CostEstimate(
            flops=flops, bytes_accessed=rows * width * 2 + 40000000, transcendentals=0
        ),
        name="layer_back",
    )(
        lengths,
        slopes,
        grad,
        total_two,
        total_one,
        steep,
        query_rows,
        key_rows,
        value_rows,
        attended,
        lse,
        gains,
        weight_full,
    )


def weight_product(left, right):
    return lax.dot_general(
        left, right, (((0, 1), (0, 1)), ((), ())), preferred_element_type=F32
    )


def matrix_gradient(query_low, memory_low, attended, hidden, back):
    (two_low, pre_grad, normed_low, one_low, query_grad, key_grad, value_grad) = back
    return jnp.concatenate(
        [
            weight_product(query_low, query_grad),
            weight_product(memory_low, key_grad),
            weight_product(memory_low, value_grad),
            weight_product(attended, one_low),
            weight_product(pre_grad, normed_low),
            weight_product(hidden, two_low),
        ],
        axis=0,
    )


def adam_step(master, gradient, first_mom, second_mom, rate):
    first_new = BETA_ONE * first_mom + (1.0 - BETA_ONE) * gradient
    second_new = BETA_TWO * second_mom + (1.0 - BETA_TWO) * gradient * gradient
    first_hat = first_new / (1.0 - BETA_ONE**STEP)
    second_hat = second_new / (1.0 - BETA_TWO**STEP)
    inner_move = rate * (first_hat / (jnp.sqrt(second_hat) + ADAM_EPS) + DECAY_RATE * master)
    return (first_new, second_new, inner_move)


def outer_step(master, moves_sum, momentum_old, group_count):
    mean_move = moves_sum / group_count
    momentum_new = MOMENTUM * momentum_old + mean_move
    return (mean_move, momentum_new, master - OUTER_RATE * (mean_move + MOMENTUM * momentum_new))


def shards(
    hidden_in,
    lengths,
    out_grad,
    weights,
    weight_m,
    weight_v,
    outer_mom,
    small,
    small_m,
    small_v,
    small_mom,
):
    width = weights.shape[2]
    part_size = small.shape[0] // 2
    masters_low = weights.astype(BF)

    def reduce_layer(grad_rows):
        return lax.psum_scatter(
            grad_rows.astype(BF), "fsdp", scatter_dimension=0, tiled=True
        ).astype(F32)

    gains = []
    slopes = []
    for layer in range(2):
        part = small[layer * part_size : (layer + 1) * part_size]
        gains.append(part[: 4 * width].reshape(4, width))
        slopes.append(part[4 * width :])

    matrix_one = gather_rows(masters_low[0])
    (q1, k1, v1, lse1, att1, one1, hid1, steep1, two1, first_out, low1, matrix_two) = layer_ahead(
        True, hidden_in, lengths, slopes[0], gains[0], matrix_one, F32, masters_low[1]
    )
    (q2, k2, v2, lse2, att2, one2, hid2, steep2, two2, block_out, low2) = layer_ahead(
        False, first_out, lengths, slopes[1], gains[1], matrix_two, BF
    )
    back_two = layer_back(
        False,
        out_grad,
        (q2, k2, v2, lse2, att2, one2, steep2, two2),
        lengths,
        slopes[1],
        gains[1],
        matrix_two,
    )
    matrix_grad_two = matrix_gradient(low2, low2, att2, hid2, back_two[:7])
    first_grad, matrix_grad_two = lax.optimization_barrier(
        (back_two[7], matrix_grad_two.astype(BF))
    )
    shard_two = reduce_layer(matrix_grad_two)
    back_one = layer_back(
        True,
        first_grad,
        (q1, k1, v1, lse1, att1, one1, steep1, two1),
        lengths,
        slopes[0],
        gains[0],
        matrix_one,
    )
    input_grad = back_one[7]
    shard_one = reduce_layer(matrix_gradient(low1, hidden_in, att1, hid1, back_one[:7]))
    grad_shard = jnp.stack([shard_one, shard_two])
    head_count = slopes[0].shape[0]
    small_parts = []
    for back in (back_one, back_two):
        small_parts += [back[8].reshape(-1), -jnp.sum(back[9][:head_count], axis=1)]
    small_grad = lax.psum(jnp.concatenate(small_parts), "fsdp")
    weight_first, weight_second, weight_move = adam_step(
        weights, grad_shard[None], weight_m, weight_v, INNER_RATE
    )
    small_first, small_second, small_move = adam_step(
        small, small_grad[None], small_m, small_v, SMALL_RATE
    )
    weight_sum, small_sum = (
        lax.psum(weight_move[0].astype(BF), "group").astype(F32),
        lax.psum(small_move[0].astype(BF), "group").astype(F32),
    )
    group_count = lax.axis_size("group")
    weight_mean, weight_mom, weight_new = outer_step(weights, weight_sum, outer_mom, group_count)
    small_mean, small_momentum, small_after = outer_step(small, small_sum, small_mom, group_count)
    return (
        block_out,
        input_grad,
        weight_new,
        weight_new.astype(BF),
        weight_first,
        weight_second,
        weight_mean,
        weight_mom,
        small_after,
        small_first,
        small_second,
        small_mean,
        small_momentum,
    )


def solution(mesh):
    in_specs = (
        P(("group", "fsdp"), None, None),
        P(("group", "fsdp")),
        P(("group", "fsdp"), None, None),
        P(None, "fsdp", None),
        P("group", None, "fsdp", None),
        P("group", None, "fsdp", None),
        P(None, "fsdp", None),
        P(),
        P("group", None),
        P("group", None),
        P(),
    )
    out_specs = (
        P(("group", "fsdp"), None, None),
        P(("group", "fsdp"), None, None),
        P(None, "fsdp", None),
        P(None, "fsdp", None),
        P("group", None, "fsdp", None),
        P("group", None, "fsdp", None),
        P(None, "fsdp", None),
        P(None, "fsdp", None),
        P(),
        P("group", None),
        P("group", None),
        P(),
        P(),
    )
    return jax.shard_map(shards, mesh=mesh, in_specs=in_specs, out_specs=out_specs, check_vma=False)
```

```python
import functools

import jax
import jax.numpy as jnp
from jax import lax
from jax.experimental import pallas as pl
from jax.experimental.pallas import tpu as pltpu
from jax.sharding import PartitionSpec as P

STEP = 10


EPS_NORM = 1e-06
MASK_FILL = -1e30
BETA_ONE = 0.9
BETA_TWO = 0.999
ADAM_EPS = 1e-08
DECAY_RATE = 0.01
INNER_RATE = 0.03
SMALL_RATE = 0.6
OUTER_RATE = 0.7
MOMENTUM = 0.9
GELU_COEF = 0.7978845608028654
GELU_CUBE = 0.044715

BF = jnp.bfloat16
F32 = jnp.float32
VMEM_LIMIT = 60 * 1024 * 1024
MESH_ID = pl.DeviceIdType.MESH


def dot_nn(left, right):
    return lax.dot_general(left, right, (((1,), (0,)), ((), ())), preferred_element_type=F32)


def dot_nt(left, right):
    return lax.dot_general(left, right, (((1,), (1,)), ((), ())), preferred_element_type=F32)


def dot_tn(left, right):
    return lax.dot_general(left, right, (((0,), (0,)), ((), ())), preferred_element_type=F32)


def norm_parts(total):
    center = total - jnp.mean(total, axis=-1, keepdims=True)
    inverse = lax.rsqrt(jnp.mean(center * center, axis=-1, keepdims=True) + EPS_NORM)
    return center * inverse, inverse


def norm_back(grad, unit, inverse, gain):
    scaled = grad * gain
    lead = jnp.mean(scaled, axis=-1, keepdims=True)
    along = jnp.mean(scaled * unit, axis=-1, keepdims=True)
    return inverse * (scaled - lead - unit * along)


def fill_distance(dist_ref, key_step, query_step):
    shape = dist_ref.shape
    keys = lax.broadcasted_iota(jnp.int32, shape, 0) * key_step
    queries = lax.broadcasted_iota(jnp.int32, shape, 1) * query_step
    dist_ref[...] = jnp.abs(queries - keys).astype(F32)


def fill_mask(mask_ref, key_step, length):
    keys = lax.broadcasted_iota(jnp.int32, mask_ref.shape, 0) * key_step
    mask_ref[...] = jnp.where(keys < length, 0.0, MASK_FILL)


def pick_rows(pair_rows, which):
    half = pair_rows.shape[0] // 2
    zero = jnp.zeros((half, pair_rows.shape[1]), pair_rows.dtype)
    if which == 0:
        return jnp.concatenate([pair_rows[:half], zero], axis=0)
    return jnp.concatenate([zero, pair_rows[half:]], axis=0)


def lane_half(width, which):
    lanes = lax.broadcasted_iota(jnp.int32, (1, width), 1)
    inside = lanes < width // 2 if which == 0 else lanes >= width // 2
    return jnp.where(inside, 1.0, 0.0).astype(BF)


def pair_matrix(queries, keys, value, by_query):
    shape = (queries, keys) if by_query else (keys, queries)
    query_index = lax.broadcasted_iota(jnp.int32, shape, 0 if by_query else 1)
    key_index = lax.broadcasted_iota(jnp.int32, shape, 1 if by_query else 0)
    offset = key_index - 2 * query_index
    return jnp.where((offset == 0) | (offset == 1), value, 0.0).astype(BF)


def remote(source, target, send_sem, recv_sem, device):
    return pltpu.make_async_remote_copy(
        src_ref=source,
        dst_ref=target,
        send_sem=send_sem,
        recv_sem=recv_sem,
        device_id=device,
        device_id_type=pl.DeviceIdType.MESH,
    )


class Spot:
    def __init__(self, chips, group_count):
        self.chips = chips
        self.group_count = group_count
        self.group = lax.axis_index("group")
        self.member = lax.axis_index("fsdp")
        self.chip = self.member // 2
        self.core = self.member % 2

    def line(self, chip):
        return {"fsdp": 2 * chip + self.core}

    def partner(self):
        return {"fsdp": 2 * self.chip + 1 - self.core}

    def other(self, turn):
        return {"group": lax.rem(self.group + turn, self.group_count)}

    def back_group(self, turn):
        return lax.rem(self.group + self.group_count - turn, self.group_count)

    def ahead_chip(self, hop):
        return lax.rem(self.chip + hop, self.chips)

    def back_chip(self, hop):
        return lax.rem(self.chip + self.chips - hop, self.chips)


def meet(spot):
    barrier = pltpu.get_barrier_semaphore()
    for hop in range(1, spot.chips):
        pl.semaphore_signal(
            barrier, inc=1, device_id=spot.line(spot.ahead_chip(hop)), device_id_type=MESH_ID
        )
    pl.semaphore_signal(barrier, inc=1, device_id=spot.partner(), device_id_type=MESH_ID)
    for turn in range(1, spot.group_count):
        pl.semaphore_signal(barrier, inc=1, device_id=spot.other(turn), device_id_type=MESH_ID)
    pl.semaphore_wait(barrier, spot.chips - 1 + 1 + spot.group_count - 1)


class Gather:
    def __init__(self, spot, shard_ref, full_ref, sems):
        self.spot = spot
        self.shard = shard_ref
        self.full = full_ref
        self.line_send, self.line_recv, self.cross_send, self.cross_recv = sems[:4]
        self.core_send, self.core_recv, self.own_sem = sems[4:]
        self.rows = shard_ref.shape[0]
        self.part = self.rows // spot.group_count
        self.tick_count = 2 * spot.chips

    def piece(self, chip, core, group):
        start = (2 * chip + core) * self.rows + group * self.part
        return self.full.at[pl.ds(start, self.part)]

    def whole(self, chip, core):
        return self.full.at[pl.ds((2 * chip + core) * self.rows, self.rows)]

    def line_copy(self, hop):
        spot = self.spot
        return remote(
            self.shard.at[pl.ds(spot.group * self.part, self.part)],
            self.piece(spot.chip, spot.core, spot.group),
            self.line_send.at[hop],
            self.line_recv.at[hop],
            spot.line(spot.ahead_chip(hop)),
        )

    def line_arrival(self, hop):
        spot = self.spot
        here = self.piece(spot.back_chip(hop), spot.core, spot.group)
        return remote(
            here, here, self.line_send.at[hop], self.line_recv.at[hop], spot.partner()
        )

    def cross_copy(self, hop, turn):
        spot = self.spot
        here = self.piece(spot.back_chip(hop), spot.core, spot.group)
        slot = hop * spot.group_count + turn
        return remote(
            here, here, self.cross_send.at[slot], self.cross_recv.at[slot], spot.other(turn)
        )

    def cross_arrival(self, hop, turn):
        spot = self.spot
        here = self.piece(spot.back_chip(hop), spot.core, spot.back_group(turn))
        slot = hop * spot.group_count + turn
        return remote(
            here, here, self.cross_send.at[slot], self.cross_recv.at[slot], spot.partner()
        )

    def core_copy(self, hop, turn):
        spot = self.spot
        slot = hop * spot.group_count + turn
        if hop == 0:
            source, target = self.shard, self.whole(spot.chip, spot.core)
        else:
            source = self.piece(spot.back_chip(hop), spot.core, spot.back_group(turn))
            target = source
        return remote(
            source, target, self.core_send.at[slot], self.core_recv.at[slot], spot.partner()
        )

    def core_arrival(self, hop, turn):
        spot = self.spot
        slot = hop * spot.group_count + turn
        if hop == 0:
            here = self.whole(spot.chip, 1 - spot.core)
        else:
            here = self.piece(spot.back_chip(hop), 1 - spot.core, spot.back_group(turn))
        return remote(
            here, here, self.core_send.at[slot], self.core_recv.at[slot], spot.partner()
        )

    def own_copy(self):
        return pltpu.make_async_copy(
            self.shard, self.whole(self.spot.chip, self.spot.core), self.own_sem.at[0]
        )

    def tick(self, index):
        chips, groups = self.spot.chips, self.spot.group_count
        if index == 0:
            for hop in range(1, chips):
                self.line_copy(hop).start()
            self.core_copy(0, 0).start()
            self.own_copy().start()
        elif index < chips:
            hop = index
            self.line_arrival(hop).wait_recv()
            for turn in range(1, groups):
                self.cross_copy(hop, turn).start()
            self.core_copy(hop, 0).start()
        elif index < 2 * chips - 1:
            hop = index - chips + 1
            for turn in range(1, groups):
                self.cross_arrival(hop, turn).wait_recv()
                self.core_copy(hop, turn).start()
        else:
            self.own_copy().wait()
            self.core_copy(0, 0).wait_send()
            self.core_arrival(0, 0).wait_recv()
            for hop in range(1, chips):
                self.line_copy(hop).wait_send()
                self.core_copy(hop, 0).wait_send()
                self.core_arrival(hop, 0).wait_recv()
                for turn in range(1, groups):
                    self.cross_copy(hop, turn).wait_send()
                    self.core_copy(hop, turn).wait_send()
                    self.core_arrival(hop, turn).wait_recv()


def gather_sems(chips, group_count):
    dma = pltpu.SemaphoreType.DMA
    crossing = (chips * group_count,)
    return [dma((chips,)), dma((chips,))] + [dma(crossing)] * 4 + [dma((1,))]


def gather_kernel(chips, group_count, shard_ref, full_ref, *sems):
    spot = Spot(chips, group_count)
    job = Gather(spot, shard_ref, full_ref, sems)
    meet(spot)
    for index in range(job.tick_count):
        job.tick(index)


def gather_rows(shard):
    members, group_count = lax.axis_size("fsdp"), lax.axis_size("group")
    rows, width = shard.shape
    return pl.pallas_call(
        functools.partial(gather_kernel, members // 2, group_count),
        out_shape=jax.ShapeDtypeStruct((rows * members, width), BF),
        in_specs=[pl.BlockSpec(memory_space=pl.ANY)],
        out_specs=pl.BlockSpec(memory_space=pl.ANY),
        scratch_shapes=gather_sems(members // 2, group_count),
        compiler_params=pltpu.CompilerParams(collective_id=0, has_side_effects=True),
        name="gather_rows",
    )(shard)


def chunk_count(rows):
    return max(
        count for count in range(1, 7) if rows % (32 * count) == 0
    )


class Reduce:
    def __init__(self, spot, count, grad, swap, lands, loads, sends, sems):
        self.spot = spot
        self.count = count
        self.grad = grad
        self.swap = swap
        self.lands = lands
        self.loads = loads
        self.sends = sends
        (self.load_sems, self.send_sems, self.recv_sems, self.swap_send, self.swap_recv) = sems
        self.last = spot.chips - 1
        self.rows = grad.shape[0] // (2 * spot.chips)
        self.piece = self.rows // count
        self.items = self.last * count
        self.ticks = self.items + self.last
        self.slots = sends.shape[1]

    def swap_copy(self, chip, part):
        spot = self.spot
        start = part * self.piece
        source = (2 * chip + 1 - spot.core) * self.rows + start
        return remote(
            self.grad.at[pl.ds(pl.multiple_of(source, 8), self.piece)],
            self.swap.at[pl.ds(pl.multiple_of(chip * self.rows + start, 8), self.piece)],
            self.swap_send.at[chip * self.count + part],
            self.swap_recv.at[chip * self.count + part],
            spot.partner(),
        )

    def start(self):
        for chip in range(self.last, -1, -1):
            for part in range(self.count - 1, -1, -1):
                self.swap_copy(chip, part).start()
        self.fetch(0)

    def own_rows(self, chip, part):
        start = (2 * chip + self.spot.core) * self.rows + part * self.piece
        return self.grad.at[pl.ds(pl.multiple_of(start, 8), self.piece)]

    def swap_rows(self, chip, part):
        start = chip * self.rows + part * self.piece
        return self.swap.at[pl.ds(pl.multiple_of(start, 8), self.piece)]

    def land_rows(self, way, item):
        start = (way * self.items + item) * self.piece
        return self.lands.at[pl.ds(pl.multiple_of(start, 8), self.piece)]

    def plan(self, way, tick):
        spot, count, last = self.spot, self.count, self.last
        distance = spot.chip + way * (last - 2 * spot.chip)
        item = tick - distance
        raised = item + count * spot.chips
        chip = last - way - (lax.div(raised, count) - spot.chips)
        part = count - 1 - lax.rem(raised, count)
        inside = (item >= 0) & (item < self.items)
        ahead = (1 - 2 * way) * (chip - spot.chip)
        passes = inside & (ahead > 0)
        takes = distance > 0
        return item, chip, part, passes, takes

    def near_loads(self, way, tick, chip, part):
        turn = lax.rem(tick, 2)
        return [
            pltpu.make_async_copy(
                source,
                self.loads.at[way, 2 * turn + which],
                self.load_sems.at[way * 5 + 2 * turn + which],
            )
            for which, source in enumerate((self.own_rows(chip, part), self.swap_rows(chip, part)))
        ]

    def land_load(self, way, item):
        return pltpu.make_async_copy(
            self.land_rows(way, item), self.loads.at[way, 4], self.load_sems.at[way * 5 + 4]
        )

    def fetch(self, tick):
        for way in range(2):
            item, chip, part, passes, takes = self.plan(way, tick)

            @pl.when(passes)
            def _():
                self.swap_copy(chip, part).wait_recv()
                for copy in self.near_loads(way, tick, chip, part):
                    copy.start()

    def hop(self, way, item):
        spot = self.spot
        return remote(
            self.sends.at[way, lax.rem(item, self.slots)],
            self.land_rows(way, item),
            self.send_sems.at[way * self.items + item],
            self.recv_sems.at[way * self.items + item],
            spot.line(spot.chip + 1 - 2 * way),
        )

    def arrival(self, way, item):
        here = self.land_rows(way, item)
        sem = way * self.items + item
        return remote(
            here, here, self.send_sems.at[sem], self.recv_sems.at[sem], self.spot.partner()
        )

    def tick(self, tick):
        spot = self.spot
        nearer = jnp.where(2 * spot.chip > self.last, 1, 0)
        for turn in range(2):
            way = nearer if turn == 0 else 1 - nearer
            item, chip, part, passes, takes = self.plan(way, tick)

            @pl.when(passes)
            def _():
                @pl.when(takes)
                def _():
                    self.arrival(way, item).wait_recv()
                    self.land_load(way, item).start()

                slot = lax.rem(item, self.slots)
                first = way * (self.last - spot.chip) * self.count

                @pl.when(item - first >= self.slots)
                def _():
                    self.hop(way, item - self.slots).wait_send()

                for copy in self.near_loads(way, tick, chip, part):
                    copy.wait()

                @pl.when(takes)
                def _():
                    self.land_load(way, item).wait()
                    self.add(way, tick, slot, True)

                @pl.when(jnp.logical_not(takes))
                def _():
                    self.add(way, tick, slot, False)

                self.hop(way, item).start()

        self.fetch(tick + 1)

    def settle(self, order):
        spot = self.spot

        @pl.when(spot.chip > 0)
        def _():
            self.arrival(0, (self.last - spot.chip) * self.count + order).wait_recv()

        @pl.when(spot.chip < self.last)
        def _():
            self.arrival(1, (self.last - 1 - spot.chip) * self.count + order).wait_recv()

    def add(self, way, tick, slot, landed):
        block = 32
        near = 2 * lax.rem(tick, 2)

        def step(index, carry):
            rows = pl.ds(pl.multiple_of(index * block, block), block)
            total = self.loads[way, near, rows, :].astype(F32)
            total = total + self.loads[way, near + 1, rows, :].astype(F32)
            if landed:
                total = total + self.loads[way, 4, rows, :].astype(F32)
            self.sends[way, slot, rows, :] = total.astype(BF)
            return carry

        lax.fori_loop(0, self.piece // block, step, 0)

    def drain(self):
        spot = self.spot
        for way in range(2):
            begin = 0 if way == 0 else (self.last - spot.chip) * self.count
            end = (self.last - spot.chip) * self.count if way == 0 else self.items
            for back in range(1, self.slots + 1):

                @pl.when(end - back >= begin)
                def _():
                    self.hop(way, end - back).wait_send()

        for chip in range(spot.chips):
            for part in range(self.count):
                self.swap_copy(chip, part).wait_send()


def reduce_scratch(chips, rows, width):
    count = chunk_count(rows)
    dma = pltpu.SemaphoreType.DMA
    items = (chips - 1) * count
    return [
        pltpu.VMEM((2, 5, rows // count, width), BF),
        pltpu.VMEM((2, 4, rows // count, width), BF),
        dma((10,)),
        dma((2 * items,)),
        dma((2 * items,)),
        dma((chips * count,)),
        dma((chips * count,)),
    ]


def reduce_lands(chips, rows, width):
    return [
        jax.ShapeDtypeStruct((chips * rows, width), BF),
        jax.ShapeDtypeStruct((2 * (chips - 1) * rows, width), BF),
    ]


def move_of(master, gradient, first_mom, second_mom, rate):
    return adam_step(master, gradient, first_mom, second_mom, rate)[2]


def finish_kernel(
    chips,
    group_count,
    grad_zero,
    grad_one,
    swap_one,
    lands_one,
    weight_hbm,
    first_hbm,
    second_hbm,
    small_grad,
    small_ref,
    small_first,
    small_second,
    grad_out,
    sum_out,
    small_grad_out,
    small_sum_out,
    swap_zero,
    lands_zero,
    parts,
    states,
    grads,
    moves,
    quarters,
    sums,
    small_land,
    small_moves,
    small_move,
    part_sems,
    state_sems,
    grad_sems,
    cross_send,
    cross_recv,
    share_send,
    share_recv,
    share_own,
    small_send,
    small_recv,
    small_cross_send,
    small_cross_recv,
    *engine_scratch,
):
    tick = pl.program_id(0)
    spot = Spot(chips, group_count)
    rows = sum_out.shape[1]
    count = moves.shape[1]
    piece = rows // count
    quarter = piece // group_count
    engine = Reduce(
        spot,
        count,
        grad_zero,
        swap_zero,
        lands_zero,
        engine_scratch[0],
        engine_scratch[1],
        engine_scratch[2:],
    )
    members = 2 * chips
    last = chips - 1
    tops = ((grad_zero, swap_zero, lands_zero), (grad_one, swap_one, lands_one))

    def small_send_copy(hop):
        target = lax.rem(spot.member + hop, members)
        return remote(
            small_grad,
            small_land.at[spot.member],
            small_send.at[hop],
            small_recv.at[hop],
            {"fsdp": target},
        )

    def small_cross_copy(turn):
        return remote(
            small_move,
            small_moves.at[spot.group],
            small_cross_send.at[turn],
            small_cross_recv.at[turn],
            spot.other(turn),
        )

    @pl.when(tick == 0)
    def _():
        barrier = pltpu.get_barrier_semaphore()
        for hop in range(1, members):
            pl.semaphore_signal(
                barrier,
                inc=1,
                device_id={"fsdp": lax.rem(spot.member + hop, members)},
                device_id_type=MESH_ID,
            )
        for turn in range(1, group_count):
            pl.semaphore_signal(barrier, inc=1, device_id=spot.other(turn), device_id_type=MESH_ID)
        pl.semaphore_wait(barrier, members - 1 + group_count - 1)
        engine.start()
        for hop in range(1, members):
            small_send_copy(hop).start()
        parts[...] = jnp.zeros_like(parts)

    bases = (engine.ticks - count, 1)

    def part_loads(layer, order):
        top = tops[layer]
        part, slot = count - 1 - order, lax.rem(order, 2)
        here = pl.multiple_of(part * piece, 8)
        start = (2 * spot.chip + spot.core) * rows + here
        sources = (
            top[0].at[pl.ds(pl.multiple_of(start, 8), piece)],
            top[1].at[pl.ds(pl.multiple_of(spot.chip * rows + here, 8), piece)],
            top[2].at[
                pl.ds(pl.multiple_of(((last - spot.chip) * count + order) * piece, 8), piece)
            ],
            top[2].at[
                pl.ds(
                    pl.multiple_of(
                        ((2 * last - 1 - spot.chip) * count + order) * piece, 8
                    ),
                    piece,
                )
            ],
        )
        return [
            pltpu.make_async_copy(
                source,
                parts.at[layer, slot, which],
                part_sems.at[(2 * layer + slot) * 4 + which],
            )
            for which, source in enumerate(sources)
        ]

    def state_loads(layer, order):
        part, slot = count - 1 - order, lax.rem(order, 2)
        window = pl.ds(pl.multiple_of(part * piece, 8), piece)
        sources = (
            weight_hbm.at[layer, window],
            first_hbm.at[0, layer, window],
            second_hbm.at[0, layer, window],
        )
        return [
            pltpu.make_async_copy(
                source,
                states.at[layer, slot, which],
                state_sems.at[(2 * layer + slot) * 3 + which],
            )
            for which, source in enumerate(sources)
        ]

    def each_near(layer, order, act):
        copies = part_loads(layer, order)
        act(copies[0])
        act(copies[1])

    def each_landed(layer, order, act):
        copies = part_loads(layer, order)

        @pl.when(spot.chip > 0)
        def _():
            act(copies[2])

        @pl.when(spot.chip < last)
        def _():
            act(copies[3])

    def grad_store(layer, order):
        part = count - 1 - order
        return pltpu.make_async_copy(
            grads.at[layer, part],
            grad_out.at[layer, pl.ds(pl.multiple_of(part * piece, 8), piece)],
            grad_sems.at[layer * count + part],
        )

    def cross_copy(layer, order, turn):
        part = count - 1 - order
        target = lax.rem(spot.group + turn, group_count)
        sem = (layer * count + part) * group_count + turn
        return remote(
            moves.at[layer, part, pl.ds(pl.multiple_of(target * quarter, 8), quarter)],
            quarters.at[layer, part, turn],
            cross_send.at[sem],
            cross_recv.at[sem],
            spot.other(turn),
        )

    def share_rows(layer, part, group):
        start = pl.multiple_of(part * piece + group * quarter, 8)
        return sum_out.at[layer, pl.ds(start, quarter)]

    def share_copy(layer, order, turn):
        part = count - 1 - order
        sem = (layer * count + part) * group_count + turn
        return remote(
            sums.at[layer, part],
            share_rows(layer, part, spot.group),
            share_send.at[sem],
            share_recv.at[sem],
            spot.other(turn),
        )

    def share_local(layer, order):
        part = count - 1 - order
        return pltpu.make_async_copy(
            sums.at[layer, part],
            share_rows(layer, part, spot.group),
            share_own.at[layer * count + part],
        )

    def prepare(tick):
        for layer in range(2):
            order = tick - bases[layer]

            @pl.when((order >= 0) & (order < count))
            def _():
                if layer == 0:
                    engine.swap_copy(spot.chip, count - 1 - order).wait_recv()
                else:
                    each_landed(layer, order, lambda copy: copy.start())
                each_near(layer, order, lambda copy: copy.start())
                for copy in state_loads(layer, order):
                    copy.start()

    engine.tick(tick)
    prepare(tick + 1)
    landed = tick - bases[0]

    @pl.when((landed >= 0) & (landed < count))
    def _():
        engine.settle(landed)
        each_landed(0, landed, lambda copy: copy.start())

    for layer in range(2):
        later = tick - bases[layer] - 1

        @pl.when((later >= 0) & (later < count))
        def _():
            part = count - 1 - later
            for turn in range(1, group_count):
                cross_copy(layer, later, turn).wait_recv()
            total = moves[
                layer, part, pl.ds(pl.multiple_of(spot.group * quarter, 8), quarter), :
            ].astype(F32)
            for turn in range(1, group_count):
                total = total + quarters[layer, part, turn].astype(F32)
            sums[layer, part] = total.astype(sums.dtype)
            for turn in range(1, group_count):
                share_copy(layer, later, turn).start()
            share_local(layer, later).start()

        order = tick - bases[layer]

        @pl.when((order >= 0) & (order < count))
        def _():
            part, slot = count - 1 - order, lax.rem(order, 2)
            each_near(layer, order, lambda copy: copy.wait())
            each_landed(layer, order, lambda copy: copy.wait())
            for copy in state_loads(layer, order):
                copy.wait()

            def step(index, carry):
                window = pl.ds(pl.multiple_of(index * 32, 32), 32)
                total = parts[layer, slot, 0, window, :].astype(F32)
                for which in range(1, 4):
                    total = total + parts[layer, slot, which, window, :].astype(F32)
                low = total.astype(BF)
                grads[layer, part, window, :] = low
                move = move_of(
                    states[layer, slot, 0, window, :],
                    low.astype(F32),
                    states[layer, slot, 1, window, :],
                    states[layer, slot, 2, window, :],
                    INNER_RATE,
                )
                moves[layer, part, window, :] = move.astype(moves.dtype)
                return carry

            lax.fori_loop(0, piece // 32, step, 0)
            for turn in range(1, group_count):
                cross_copy(layer, order, turn).start()
            grad_store(layer, order).start()

    @pl.when(tick == 2)
    def _():
        small_land[spot.member] = small_grad[...]
        for hop in range(1, members):
            small_send_copy(hop).wait_recv()
        total = small_land[0]
        for member in range(1, members):
            total = total + small_land[member]
        small_grad_out[...] = total
        move = move_of(small_ref[...], total, small_first[...], small_second[...], SMALL_RATE)
        small_move[...] = move
        small_moves[spot.group] = move
        for turn in range(1, group_count):
            small_cross_copy(turn).start()

    @pl.when(tick == 4)
    def _():
        for turn in range(1, group_count):
            small_cross_copy(turn).wait_recv()
        total = small_moves[0]
        for group in range(1, group_count):
            total = total + small_moves[group]
        small_sum_out[...] = total

    @pl.when(tick == pl.num_programs(0) - 1)
    def _():
        engine.drain()
        for hop in range(1, members):
            small_send_copy(hop).wait_send()
        for turn in range(1, group_count):
            small_cross_copy(turn).wait_send()
        for layer in range(2):
            for order in range(count):
                grad_store(layer, order).wait()
                share_local(layer, order).wait()
                for turn in range(1, group_count):
                    cross_copy(layer, order, turn).wait_send()
                    share_copy(layer, order, turn).wait_send()
                    share_copy(layer, order, turn).wait_recv()


def finish(grad_zero, one, weights, weight_m, weight_v, small_grad, small, small_m, small_v):
    members, group_count = lax.axis_size("fsdp"), lax.axis_size("group")
    chips = members // 2
    layers, rows, width = weights.shape
    count = chunk_count(rows)
    piece = rows // count
    quarter = piece // group_count
    wire = BF if quarter % 16 == 0 else F32
    small_size = small.shape[1]
    dma = pltpu.SemaphoreType.DMA
    ticks = (chips - 1) * count + chips - 1 + 1
    anywhere = pl.BlockSpec(memory_space=pl.ANY)
    local = pl.BlockSpec(memory_space=pltpu.VMEM)
    crossing = dma((layers * count * group_count,))
    return pl.pallas_call(
        functools.partial(finish_kernel, chips, group_count),
        grid=(ticks,),
        in_specs=[anywhere] * 7 + [local] * 4,
        out_specs=[anywhere, anywhere, local, local] + [anywhere] * 2,
        out_shape=[
            jax.ShapeDtypeStruct((layers, rows, width), BF),
            jax.ShapeDtypeStruct((layers, rows, width), wire),
            jax.ShapeDtypeStruct((1, small_size), F32),
            jax.ShapeDtypeStruct((1, small_size), F32),
        ]
        + reduce_lands(chips, rows, width),
        scratch_shapes=[
            pltpu.VMEM((layers, 2, 4, piece, width), BF),
            pltpu.VMEM((layers, 2, 3, piece, width), F32),
            pltpu.VMEM((layers, count, piece, width), BF),
            pltpu.VMEM((layers, count, piece, width), wire),
            pltpu.VMEM((layers, count, group_count, quarter, width), wire),
            pltpu.VMEM((layers, count, quarter, width), wire),
            pltpu.VMEM((members, 1, small_size), F32),
            pltpu.VMEM((group_count, 1, small_size), F32),
            pltpu.VMEM((1, small_size), F32),
            dma((8 * layers,)),
            dma((6 * layers,)),
            dma((layers * count,)),
            crossing,
            crossing,
            crossing,
            crossing,
            dma((layers * count,)),
            dma((members,)),
            dma((members,)),
            dma((group_count,)),
            dma((group_count,)),
        ]
        + reduce_scratch(chips, rows, width),
        compiler_params=pltpu.CompilerParams(
            vmem_limit_bytes=VMEM_LIMIT, collective_id=3, has_side_effects=True
        ),
        name="finish",
    )(grad_zero, *one, weights, weight_m, weight_v, small_grad, small, small_m, small_v)


def weight_copies(weight_hbm, weight_ref, sems, cuts):
    return [
        pltpu.make_async_copy(
            weight_hbm.at[pl.ds(cuts[index], cuts[index + 1] - cuts[index])],
            weight_ref.at[pl.ds(cuts[index], cuts[index + 1] - cuts[index])],
            sems.at[index],
        )
        for index in range(len(cuts) - 1)
    ]


def ahead_kernel(
    is_first,
    head_count,
    place,
    lengths_ref,
    slopes_ref,
    x_ref,
    gains_ref,
    weight_hbm,
    *rest,
):
    if place is not None:
        shard_ref, rest = rest[0], rest[1:]
        full_ref, rest = rest[11], rest[:11] + rest[12:]
        job_sems = rest[18:]
    (
        query_out,
    key_out,
    value_out,
    lse_out,
    att_out,
    total_one_out,
    hidden_out,
    slope_out,
    total_two_out,
    layer_out,
    low_out,
    weight_ref,
    dist_ref,
    mask_ref,
    query_t,
    value_t,
    att_t,
    sems,
    ) = rest[:18]
    step = pl.program_id(0)
    if place is not None:
        spot = Spot(*place)
        job = Gather(spot, shard_ref, full_ref, job_sems)
        spread = [round(index * 7 / (job.tick_count - 1)) for index in range(job.tick_count)]

    def tick(quarter):
        if place is None:
            return
        for index in range(job.tick_count):
            if spread[index] % 2 == quarter:

                @pl.when(step == spread[index] // 2)
                def _():
                    if index == 0:
                        meet(spot)
                    job.tick(index)

    tick(0)
    width = weight_ref.shape[1]
    inner = (weight_ref.shape[0] - 4 * width) // 2
    queries, keys = query_out.shape[1], key_out.shape[1]
    head = width // head_count
    cuts = [0, width, 3 * width, 4 * width, 4 * width + inner, 4 * width + 2 * inner]
    copies = weight_copies(weight_hbm, weight_ref, sems, cuts)
    key_step = 1 if is_first else 2

    @pl.when(step == 0)
    def _():
        for copy in copies:
            copy.start()
        fill_distance(dist_ref, key_step, 2)

    def need(index):
        @pl.when(step == 0)
        def _():
            copies[index].wait()

    fill_mask(mask_ref, key_step, lengths_ref[step])
    if is_first:
        memory_low = x_ref[0]
        residual = dot_nn(pair_matrix(queries, keys, 0.5, True), memory_low)
        query_low = residual.astype(BF)
    else:
        residual = x_ref[0]
        query_low = residual.astype(BF)
        memory_low = query_low
    low_out[0] = query_low
    need(0)
    query_rows = dot_nn(query_low, weight_ref[0:width]).astype(BF)
    query_out[0] = query_rows
    query_t[...] = (query_rows.astype(F32) * float(head) ** (-0.5)).T.astype(BF)
    need(1)
    key_out[0] = dot_nn(memory_low, weight_ref[width : 2 * width]).astype(BF)
    value_rows = dot_nn(memory_low, weight_ref[2 * width : 3 * width]).astype(BF)
    value_out[0] = value_rows
    value_t[...] = value_rows.astype(F32).T.astype(BF)

    def pair_step(pair, carry):
        start = pl.multiple_of(pair * 2 * head, 2 * head)
        key_pair = key_out[0, :, pl.ds(start, 2 * head)]
        query_pair = query_t[pl.ds(start, 2 * head), :]
        for which in range(2):
            index = 2 * pair + which
            scores = dot_nn(key_pair, pick_rows(query_pair, which))
            scores = scores - slopes_ref[index] * dist_ref[...] + mask_ref[...]
            peak = jnp.max(scores, axis=0, keepdims=True)
            lifted = jnp.exp(scores - peak)
            total = jnp.sum(lifted, axis=0, keepdims=True)
            shares = (lifted * (1.0 / total)).astype(BF)
            rows = pl.ds(start + which * head, head)
            mixed = dot_nn(value_t[rows, :], shares)
            att_t[rows, :] = mixed
            lse_out[0, pl.ds(index, 1), :] = peak + jnp.log(total)
        return carry

    lax.fori_loop(0, head_count // 2, pair_step, 0)
    attended = att_t[...].T.astype(BF)
    att_out[0] = attended
    need(2)
    total_one = residual + dot_nn(attended, weight_ref[3 * width : 4 * width])
    total_one_out[0] = total_one
    unit, _ = norm_parts(total_one)
    normed = unit * gains_ref[0:1] + gains_ref[1:2]
    normed_low = normed.astype(BF)
    need(3)
    need(4)
    total_two = normed
    for chunk in range(inner // width):
        inner_rows = pl.ds(4 * width + chunk * width, width)
        outer_rows = pl.ds(4 * width + inner + chunk * width, width)
        pre = dot_nt(normed_low, weight_ref[inner_rows, :])
        square = pre * pre
        bend = jnp.tanh(pre * (GELU_COEF + (GELU_COEF * GELU_CUBE) * square))
        half = 0.5 + 0.5 * bend
        hidden = (pre * half).astype(BF)
        steep = half + (0.5 * pre) * (1.0 - bend * bend) * (
            GELU_COEF + (3.0 * GELU_COEF * GELU_CUBE) * square
        )
        columns = pl.ds(chunk * width, width)
        hidden_out[0, :, columns] = hidden
        slope_out[0, :, columns] = steep.astype(BF)
        total_two = total_two + dot_nn(hidden, weight_ref[outer_rows, :])
    total_two_out[0] = total_two
    unit_two, _ = norm_parts(total_two)
    result = unit_two * gains_ref[2:3] + gains_ref[3:4]
    layer_out[0] = result.astype(layer_out.dtype)
    tick(1)


def layer_ahead(is_first, x, lengths, slopes, gains, weight_full, out_dtype, shard=None):
    batch, memory_length, width = x.shape
    queries = memory_length // 2 if is_first else memory_length
    keys = memory_length
    head_count = slopes.shape[0]
    rows = weight_full.shape[0]
    inner = (rows - 4 * width) // 2
    head_rows = -(-head_count // 8) * 8

    def block(length, size):
        return pl.BlockSpec((1, length, size), lambda i, *_: (i, 0, 0))

    def shape(length, size, dtype):
        return jax.ShapeDtypeStruct((batch, length, size), dtype)

    outs = [
        (queries, width, BF),
        (keys, width, BF),
        (keys, width, BF),
        (head_rows, queries, F32),
        (queries, width, BF),
        (queries, width, F32),
        (queries, inner, BF),
        (queries, inner, BF),
        (queries, width, F32),
        (queries, width, out_dtype),
        (queries, width, BF),
    ]
    flops = 2 * batch * width * (
        2 * queries * width + 2 * keys * width + 2 * queries * inner + 2 * queries * keys
    )
    hosted = shard is not None
    place = (lax.axis_size("fsdp") // 2, lax.axis_size("group")) if hosted else None
    anywhere = [pl.BlockSpec(memory_space=pl.ANY)] * hosted
    full_shape = [jax.ShapeDtypeStruct((rows, width), BF)] * hosted
    job_sems = gather_sems(*place) if hosted else []
    params = dict(collective_id=1, has_side_effects=True) if hosted else {}
    return pl.pallas_call(
        functools.partial(ahead_kernel, is_first, head_count, place),
        grid_spec=pltpu.PrefetchScalarGridSpec(
            num_scalar_prefetch=2,
            grid=(batch,),
            in_specs=[
                block(memory_length, width),
                pl.BlockSpec((4, width), lambda i, *_: (0, 0)),
                pl.BlockSpec(memory_space=pl.ANY),
            ]
            + anywhere,
            out_specs=[block(length, size) for length, size, _ in outs] + anywhere,
            scratch_shapes=[
                pltpu.VMEM((rows, width), BF),
                pltpu.VMEM((keys, queries), F32),
                pltpu.VMEM((keys, queries), F32),
                pltpu.VMEM((width, queries), BF),
                pltpu.VMEM((width, keys), BF),
                pltpu.VMEM((width, queries), F32),
                pltpu.SemaphoreType.DMA((5,)),
            ]
            + job_sems,
        ),
        out_shape=[shape(*out) for out in outs] + full_shape,
        compiler_params=pltpu.CompilerParams(vmem_limit_bytes=VMEM_LIMIT, **params),
        cost_estimate=pl.CostEstimate(
            flops=flops, bytes_accessed=rows * width * 2 + 30000000, transcendentals=0
        ),
        name="layer_ahead",
    )(lengths, slopes, x, gains, weight_full, *([shard] * hosted))


def back_kernel(
    is_first,
    head_count,
    place,
    query_steps,
    lengths_ref,
    slopes_ref,
    grad_ref,
    total_two_ref,
    total_one_ref,
    slope_ref,
    query_ref,
    key_ref,
    value_ref,
    att_ref,
    lse_ref,
    gains_ref,
    weight_hbm,
    *rest,
):
    if place is not None:
        grad_rows, rest = rest[0], rest[1:]
        landing, rest = rest[10:12], rest[:10] + rest[12:]
        job = rest[20:]
    (
        two_out,
        pre_out,
        normed_out,
        one_out,
        query_grad_out,
        key_grad_out,
        value_grad_out,
        input_out,
        gains_out,
        slopes_out,
        weight_ref,
        dist_ref,
        mask_ref,
        query_t,
        key_t,
        mixed_t,
        mixed_rows,
        delta_ref,
        query_grad_t,
        sems,
    ) = rest[:20]
    step = pl.program_id(0)
    if place is not None:
        spot = Spot(*place)
        engine = Reduce(
            spot,
            chunk_count(grad_rows.shape[0] // (2 * spot.chips)),
            grad_rows,
            landing[0],
            landing[1],
            job[0],
            job[1],
            job[2:],
        )

        early_ticks = engine.items - 2

        @pl.when(step == 0)
        def _():
            meet(spot)
            engine.start()

    pairs = head_count // 2
    sites = pairs + 2

    def reduce_ticks(site):
        if place is None:
            return
        total = sites * query_steps
        here = step * sites + site
        for index in range(-(-early_ticks // total)):
            tick = lax.div(here * early_ticks, total) + index

            @pl.when(tick < lax.div((here + 1) * early_ticks, total))
            def _():
                engine.tick(tick)

    width = weight_ref.shape[1]
    inner = (weight_ref.shape[0] - 4 * width) // 2
    queries, keys = query_ref.shape[1], key_ref.shape[1]
    head = width // head_count
    cuts = [0, 3 * width, 4 * width, 4 * width + inner, 4 * width + 2 * inner]
    copies = weight_copies(weight_hbm, weight_ref, sems, cuts)
    key_step = 1 if is_first else 2
    scale = float(head) ** (-0.5)

    @pl.when(step == 0)
    def _():
        for index in (3, 2, 1, 0):
            copies[index].start()
        fill_distance(dist_ref, key_step, 2)
        gains_out[...] = jnp.zeros_like(gains_out)
        slopes_out[...] = jnp.zeros_like(slopes_out)

    def need(index):
        @pl.when(step == 0)
        def _():
            copies[index].wait()

    fill_mask(mask_ref, key_step, lengths_ref[step])
    query_t[...] = (query_ref[0].astype(F32) * scale).T.astype(BF)
    key_t[...] = key_ref[0].astype(F32).T.astype(BF)

    grad = grad_ref[0].astype(F32)
    unit_two, inverse_two = norm_parts(total_two_ref[0])
    gains_out[2:3] += jnp.sum(grad * unit_two, axis=0, keepdims=True)
    gains_out[3:4] += jnp.sum(grad, axis=0, keepdims=True)
    back_two = norm_back(grad, unit_two, inverse_two, gains_ref[2:3])
    two_low = back_two.astype(BF)
    two_out[0] = two_low
    need(3)
    need(2)
    back_normed = back_two
    for chunk in range(inner // width):
        inner_rows = pl.ds(4 * width + chunk * width, width)
        outer_rows = pl.ds(4 * width + inner + chunk * width, width)
        columns = pl.ds(chunk * width, width)
        back_hidden = dot_nt(two_low, weight_ref[outer_rows, :])
        pre_grad = (back_hidden * slope_ref[0, :, columns].astype(F32)).astype(BF)
        pre_out[0, :, columns] = pre_grad
        back_normed = back_normed + dot_nn(pre_grad, weight_ref[inner_rows, :])
        if chunk % 2 == 1 and chunk < 4:
            reduce_ticks(chunk // 2)
    unit_one, inverse_one = norm_parts(total_one_ref[0])
    normed_out[0] = (unit_one * gains_ref[0:1] + gains_ref[1:2]).astype(BF)
    gains_out[0:1] += jnp.sum(back_normed * unit_one, axis=0, keepdims=True)
    gains_out[1:2] += jnp.sum(back_normed, axis=0, keepdims=True)
    back_one = norm_back(back_normed, unit_one, inverse_one, gains_ref[0:1])
    one_low = back_one.astype(BF)
    one_out[0] = one_low
    need(1)
    back_mixed = dot_nt(one_low, weight_ref[3 * width : 4 * width])
    mixed_low = back_mixed.astype(BF)
    mixed_rows[...] = mixed_low
    mixed_wide = mixed_low.astype(F32).T
    mixed_t[...] = mixed_wide.astype(BF)
    product = mixed_wide * att_ref[0].astype(F32).T
    delta_ref[...] = jnp.sum(product.reshape(head_count, head, queries), axis=1)

    def pair_step(pair, carry):
        start = pl.multiple_of(pair * 2 * head, 2 * head)
        lanes = pl.ds(start, 2 * head)
        key_pair = key_ref[0, :, lanes]
        value_pair = value_ref[0, :, lanes]
        query_pair = query_ref[0, :, lanes]
        mixed_pair = mixed_rows[:, lanes]
        query_pair_t = query_t[lanes, :]
        mixed_pair_t = mixed_t[lanes, :]
        key_grad = jnp.zeros((keys, 2 * head), F32)
        value_grad = jnp.zeros((keys, 2 * head), F32)
        for which in range(2):
            index = 2 * pair + which
            half = lane_half(2 * head, which)
            scores = dot_nn(key_pair, pick_rows(query_pair_t, which))
            scores = scores - slopes_ref[index] * dist_ref[...] + mask_ref[...]
            shares = jnp.exp(scores - lse_ref[0, pl.ds(index, 1), :])
            back_shares = dot_nn(value_pair, pick_rows(mixed_pair_t, which))
            back_scores = shares * (back_shares - delta_ref[pl.ds(index, 1), :])
            slopes_out[pl.ds(index, 1), :] += jnp.sum(
                back_scores * dist_ref[...], axis=0, keepdims=True
            )
            scores_low = back_scores.astype(BF)
            value_grad = value_grad + dot_nn(shares.astype(BF), mixed_pair * half)
            key_grad = key_grad + dot_nn(scores_low, query_pair * half)
            rows = pl.ds(start + which * head, head)
            query_grad_t[rows, :] = dot_nn(key_t[rows, :], scores_low)
        reduce_ticks(pair + 2)
        key_grad_out[0, :, lanes] = (key_grad * scale).astype(BF)
        value_grad_out[0, :, lanes] = value_grad.astype(BF)
        return carry

    lax.fori_loop(0, head_count // 2, pair_step, 0)
    query_grad = (query_grad_t[...] * scale).T.astype(BF)
    query_grad_out[0] = query_grad
    need(0)
    back_query = back_one + dot_nt(query_grad, weight_ref[0:width])
    back_memory = dot_nt(key_grad_out[0], weight_ref[width : 2 * width]) + dot_nt(
        value_grad_out[0], weight_ref[2 * width : 3 * width]
    )
    if is_first:
        spread = pair_matrix(queries, keys, 1.0, False)
        half_grad = back_query * 0.5
        upper = half_grad.astype(BF)
        lower = (half_grad - upper.astype(F32)).astype(BF)
        back_memory = back_memory + dot_nn(spread, upper) + dot_nn(spread, lower)
        input_out[0] = back_memory
    else:
        input_out[0] = back_query + back_memory
    if place is not None:

        @pl.when(step == pl.num_programs(0) - 1)
        def _():
            def late_tick(tick, carry):
                engine.tick(tick)
                return carry

            lax.fori_loop(early_ticks, engine.ticks, late_tick, 0)
            for part in range(engine.count):
                engine.swap_copy(spot.chip, part).wait_recv()
                engine.settle(part)
            engine.drain()


def layer_back(is_first, grad, kept, lengths, slopes, gains, weight_full, grad_rows=None):
    (query_rows, key_rows, value_rows, lse, attended, total_one, steep, total_two) = kept
    batch, queries, width = query_rows.shape
    keys = key_rows.shape[1]
    head_count = slopes.shape[0]
    rows = weight_full.shape[0]
    inner = (rows - 4 * width) // 2
    head_rows = lse.shape[1]

    def block(length, size):
        return pl.BlockSpec((1, length, size), lambda i, *_: (i, 0, 0))

    def shape(length, size, dtype):
        return jax.ShapeDtypeStruct((batch, length, size), dtype)

    outs = [
        (queries, width, BF),
        (queries, inner, BF),
        (queries, width, BF),
        (queries, width, BF),
        (queries, width, BF),
        (keys, width, BF),
        (keys, width, BF),
        (keys, width, F32),
    ]
    flops = 2 * batch * width * (
        2 * queries * width + 2 * keys * width + 2 * queries * inner + 5 * queries * keys
    )
    hosted = grad_rows is not None
    place, job_scratch, lands, params = None, [], [], {}
    if hosted:
        place = (lax.axis_size("fsdp") // 2, lax.axis_size("group"))
        shard_rows = rows // (2 * place[0])
        job_scratch = reduce_scratch(place[0], shard_rows, width)
        lands = reduce_lands(place[0], shard_rows, width)
        params = dict(collective_id=2, has_side_effects=True)
    anywhere = pl.BlockSpec(memory_space=pl.ANY)
    return pl.pallas_call(
        functools.partial(back_kernel, is_first, head_count, place, batch),
        grid_spec=pltpu.PrefetchScalarGridSpec(
            num_scalar_prefetch=2,
            grid=(batch,),
            in_specs=[
                block(queries, width),
                block(queries, width),
                block(queries, width),
                block(queries, inner),
                block(queries, width),
                block(keys, width),
                block(keys, width),
                block(queries, width),
                block(head_rows, queries),
                pl.BlockSpec((4, width), lambda i, *_: (0, 0)),
                anywhere,
            ]
            + [anywhere] * hosted,
            out_specs=[block(length, size) for length, size, _ in outs]
            + [
                pl.BlockSpec((4, width), lambda i, *_: (0, 0)),
                pl.BlockSpec((head_rows, queries), lambda i, *_: (0, 0)),
            ]
            + [anywhere] * len(lands),
            scratch_shapes=[
                pltpu.VMEM((rows, width), BF),
                pltpu.VMEM((keys, queries), F32),
                pltpu.VMEM((keys, queries), F32),
                pltpu.VMEM((width, queries), BF),
                pltpu.VMEM((width, keys), BF),
                pltpu.VMEM((width, queries), BF),
                pltpu.VMEM((queries, width), BF),
                pltpu.VMEM((head_count, queries), F32),
                pltpu.VMEM((width, queries), F32),
                pltpu.SemaphoreType.DMA((4,)),
            ]
            + job_scratch,
        ),
        out_shape=[shape(*out) for out in outs]
        + [
            jax.ShapeDtypeStruct((4, width), F32),
            jax.ShapeDtypeStruct((head_rows, queries), F32),
        ]
        + lands,
        compiler_params=pltpu.CompilerParams(vmem_limit_bytes=VMEM_LIMIT, **params),
        cost_estimate=pl.CostEstimate(
            flops=flops, bytes_accessed=rows * width * 2 + 40000000, transcendentals=0
        ),
        name="layer_back",
    )(
        lengths,
        slopes,
        grad,
        total_two,
        total_one,
        steep,
        query_rows,
        key_rows,
        value_rows,
        attended,
        lse,
        gains,
        weight_full,
        *([grad_rows] * hosted),
    )


def weight_product(left, right):
    return lax.dot_general(
        left, right, (((0, 1), (0, 1)), ((), ())), preferred_element_type=F32
    )


def matrix_gradient(query_low, memory_low, attended, hidden, back):
    (two_low, pre_grad, normed_low, one_low, query_grad, key_grad, value_grad) = back
    return jnp.concatenate(
        [
            weight_product(query_low, query_grad),
            weight_product(memory_low, key_grad),
            weight_product(memory_low, value_grad),
            weight_product(attended, one_low),
            weight_product(pre_grad, normed_low),
            weight_product(hidden, two_low),
        ],
        axis=0,
    )


def adam_step(master, gradient, first_mom, second_mom, rate):
    first_new = BETA_ONE * first_mom + (1.0 - BETA_ONE) * gradient
    second_new = BETA_TWO * second_mom + (1.0 - BETA_TWO) * gradient * gradient
    first_hat = first_new / (1.0 - BETA_ONE**STEP)
    second_hat = second_new / (1.0 - BETA_TWO**STEP)
    inner_move = rate * (first_hat / (jnp.sqrt(second_hat) + ADAM_EPS) + DECAY_RATE * master)
    return (first_new, second_new, inner_move)


def outer_step(master, moves_sum, momentum_old, group_count):
    mean_move = moves_sum / group_count
    momentum_new = MOMENTUM * momentum_old + mean_move
    return (mean_move, momentum_new, master - OUTER_RATE * (mean_move + MOMENTUM * momentum_new))


def shards(
    hidden_in,
    lengths,
    out_grad,
    weights,
    weight_m,
    weight_v,
    outer_mom,
    small,
    small_m,
    small_v,
    small_mom,
):
    width = weights.shape[2]
    part_size = small.shape[0] // 2
    masters_low = weights.astype(BF)

    gains = []
    slopes = []
    for layer in range(2):
        part = small[layer * part_size : (layer + 1) * part_size]
        gains.append(part[: 4 * width].reshape(4, width))
        slopes.append(part[4 * width :])

    matrix_one = gather_rows(masters_low[0])
    (q1, k1, v1, lse1, att1, one1, hid1, steep1, two1, first_out, low1, matrix_two) = layer_ahead(
        True, hidden_in, lengths, slopes[0], gains[0], matrix_one, F32, masters_low[1]
    )
    (q2, k2, v2, lse2, att2, one2, hid2, steep2, two2, block_out, low2) = layer_ahead(
        False, first_out, lengths, slopes[1], gains[1], matrix_two, BF
    )
    back_two = layer_back(
        False,
        out_grad,
        (q2, k2, v2, lse2, att2, one2, steep2, two2),
        lengths,
        slopes[1],
        gains[1],
        matrix_two,
    )
    matrix_grad_two = matrix_gradient(low2, low2, att2, hid2, back_two[:7]).astype(BF)
    back_one = layer_back(
        True,
        back_two[7],
        (q1, k1, v1, lse1, att1, one1, steep1, two1),
        lengths,
        slopes[0],
        gains[0],
        matrix_one,
        matrix_grad_two,
    )
    input_grad = back_one[7]
    matrix_grad_one = matrix_gradient(low1, hidden_in, att1, hid1, back_one[:7]).astype(BF)
    head_count = slopes[0].shape[0]
    small_parts = []
    for back in (back_one, back_two):
        small_parts += [back[8].reshape(-1), -jnp.sum(back[9][:head_count], axis=1)]
    grad_shard, weight_sum, small_grad, small_sum = finish(
        matrix_grad_one,
        (matrix_grad_two, *back_one[10:12]),
        weights,
        weight_m,
        weight_v,
        jnp.concatenate(small_parts)[None],
        small[None],
        small_m,
        small_v,
    )[:4]
    weight_first, weight_second, _ = adam_step(
        weights, grad_shard[None].astype(F32), weight_m, weight_v, INNER_RATE
    )
    small_first, small_second, _ = adam_step(small, small_grad, small_m, small_v, SMALL_RATE)
    weight_sum, small_sum = weight_sum.astype(F32), small_sum[0]
    group_count = lax.axis_size("group")
    weight_mean, weight_mom, weight_new = outer_step(weights, weight_sum, outer_mom, group_count)
    small_mean, small_momentum, small_after = outer_step(small, small_sum, small_mom, group_count)
    return (
        block_out,
        input_grad,
        weight_new,
        weight_new.astype(BF),
        weight_first,
        weight_second,
        weight_mean,
        weight_mom,
        small_after,
        small_first,
        small_second,
        small_mean,
        small_momentum,
    )


def solution(mesh):
    in_specs = (
        P(("group", "fsdp"), None, None),
        P(("group", "fsdp")),
        P(("group", "fsdp"), None, None),
        P(None, "fsdp", None),
        P("group", None, "fsdp", None),
        P("group", None, "fsdp", None),
        P(None, "fsdp", None),
        P(),
        P("group", None),
        P("group", None),
        P(),
    )
    out_specs = (
        P(("group", "fsdp"), None, None),
        P(("group", "fsdp"), None, None),
        P(None, "fsdp", None),
        P(None, "fsdp", None),
        P("group", None, "fsdp", None),
        P("group", None, "fsdp", None),
        P(None, "fsdp", None),
        P(None, "fsdp", None),
        P(),
        P("group", None),
        P("group", None),
        P(),
        P(),
    )
    return jax.shard_map(shards, mesh=mesh, in_specs=in_specs, out_specs=out_specs, check_vma=False)
```

```python
import functools

import jax
import jax.numpy as jnp
from jax import lax
from jax.experimental import pallas as pl
from jax.experimental.pallas import tpu as pltpu
from jax.sharding import PartitionSpec as P

STEP = 10


EPS_NORM = 1e-06
MASK_FILL = -1e30
BETA_ONE = 0.9
BETA_TWO = 0.999
ADAM_EPS = 1e-08
DECAY_RATE = 0.01
INNER_RATE = 0.03
SMALL_RATE = 0.6
OUTER_RATE = 0.7
MOMENTUM = 0.9
GELU_COEF = 0.7978845608028654
GELU_CUBE = 0.044715

BF = jnp.bfloat16
F32 = jnp.float32
VMEM_LIMIT = 60 * 1024 * 1024
MESH_ID = pl.DeviceIdType.MESH


def dot_nn(left, right):
    return lax.dot_general(left, right, (((1,), (0,)), ((), ())), preferred_element_type=F32)


def dot_nt(left, right):
    return lax.dot_general(left, right, (((1,), (1,)), ((), ())), preferred_element_type=F32)


def dot_tn(left, right):
    return lax.dot_general(left, right, (((0,), (0,)), ((), ())), preferred_element_type=F32)


def norm_parts(total):
    center = total - jnp.mean(total, axis=-1, keepdims=True)
    inverse = lax.rsqrt(jnp.mean(center * center, axis=-1, keepdims=True) + EPS_NORM)
    return center * inverse, inverse


def norm_back(grad, unit, inverse, gain):
    scaled = grad * gain
    lead = jnp.mean(scaled, axis=-1, keepdims=True)
    along = jnp.mean(scaled * unit, axis=-1, keepdims=True)
    return inverse * (scaled - lead - unit * along)


def fill_distance(dist_ref, key_step, query_step):
    shape = dist_ref.shape
    keys = lax.broadcasted_iota(jnp.int32, shape, 0) * key_step
    queries = lax.broadcasted_iota(jnp.int32, shape, 1) * query_step
    dist_ref[...] = jnp.abs(queries - keys).astype(F32)


def fill_mask(mask_ref, key_step, length):
    keys = lax.broadcasted_iota(jnp.int32, mask_ref.shape, 0) * key_step
    mask_ref[...] = jnp.where(keys < length, 0.0, MASK_FILL)


def pick_rows(pair_rows, which):
    half = pair_rows.shape[0] // 2
    zero = jnp.zeros((half, pair_rows.shape[1]), pair_rows.dtype)
    if which == 0:
        return jnp.concatenate([pair_rows[:half], zero], axis=0)
    return jnp.concatenate([zero, pair_rows[half:]], axis=0)


def lane_half(width, which):
    lanes = lax.broadcasted_iota(jnp.int32, (1, width), 1)
    inside = lanes < width // 2 if which == 0 else lanes >= width // 2
    return jnp.where(inside, 1.0, 0.0).astype(BF)


def pair_matrix(queries, keys, value, by_query):
    shape = (queries, keys) if by_query else (keys, queries)
    query_index = lax.broadcasted_iota(jnp.int32, shape, 0 if by_query else 1)
    key_index = lax.broadcasted_iota(jnp.int32, shape, 1 if by_query else 0)
    offset = key_index - 2 * query_index
    return jnp.where((offset == 0) | (offset == 1), value, 0.0).astype(BF)


def remote(source, target, send_sem, recv_sem, device):
    return pltpu.make_async_remote_copy(
        src_ref=source,
        dst_ref=target,
        send_sem=send_sem,
        recv_sem=recv_sem,
        device_id=device,
        device_id_type=pl.DeviceIdType.MESH,
    )


class Spot:
    def __init__(self, chips, group_count):
        self.chips = chips
        self.group_count = group_count
        self.group = lax.axis_index("group")
        self.member = lax.axis_index("fsdp")
        self.chip = self.member // 2
        self.core = self.member % 2

    def line(self, chip):
        return {"fsdp": 2 * chip + self.core}

    def partner(self):
        return {"fsdp": 2 * self.chip + 1 - self.core}

    def other(self, turn):
        return {"group": lax.rem(self.group + turn, self.group_count)}

    def back_group(self, turn):
        return lax.rem(self.group + self.group_count - turn, self.group_count)

    def ahead_chip(self, hop):
        return lax.rem(self.chip + hop, self.chips)

    def back_chip(self, hop):
        return lax.rem(self.chip + self.chips - hop, self.chips)


def meet(spot):
    barrier = pltpu.get_barrier_semaphore()
    for hop in range(1, spot.chips):
        pl.semaphore_signal(
            barrier, inc=1, device_id=spot.line(spot.ahead_chip(hop)), device_id_type=MESH_ID
        )
    pl.semaphore_signal(barrier, inc=1, device_id=spot.partner(), device_id_type=MESH_ID)
    for turn in range(1, spot.group_count):
        pl.semaphore_signal(barrier, inc=1, device_id=spot.other(turn), device_id_type=MESH_ID)
    pl.semaphore_wait(barrier, spot.chips - 1 + 1 + spot.group_count - 1)


class Gather:
    def __init__(self, spot, shard_ref, full_ref, sems):
        self.spot = spot
        self.shard = shard_ref
        self.full = full_ref
        self.line_send, self.line_recv, self.cross_send, self.cross_recv = sems[:4]
        self.core_send, self.core_recv, self.own_sem = sems[4:]
        self.rows = shard_ref.shape[0]
        self.part = self.rows // spot.group_count
        self.tick_count = 2 * spot.chips

    def piece(self, chip, core, group):
        start = (2 * chip + core) * self.rows + group * self.part
        return self.full.at[pl.ds(start, self.part)]

    def whole(self, chip, core):
        return self.full.at[pl.ds((2 * chip + core) * self.rows, self.rows)]

    def line_copy(self, hop):
        spot = self.spot
        return remote(
            self.shard.at[pl.ds(spot.group * self.part, self.part)],
            self.piece(spot.chip, spot.core, spot.group),
            self.line_send.at[hop],
            self.line_recv.at[hop],
            spot.line(spot.ahead_chip(hop)),
        )

    def line_arrival(self, hop):
        spot = self.spot
        here = self.piece(spot.back_chip(hop), spot.core, spot.group)
        return remote(
            here, here, self.line_send.at[hop], self.line_recv.at[hop], spot.partner()
        )

    def cross_copy(self, hop, turn):
        spot = self.spot
        here = self.piece(spot.back_chip(hop), spot.core, spot.group)
        slot = hop * spot.group_count + turn
        return remote(
            here, here, self.cross_send.at[slot], self.cross_recv.at[slot], spot.other(turn)
        )

    def cross_arrival(self, hop, turn):
        spot = self.spot
        here = self.piece(spot.back_chip(hop), spot.core, spot.back_group(turn))
        slot = hop * spot.group_count + turn
        return remote(
            here, here, self.cross_send.at[slot], self.cross_recv.at[slot], spot.partner()
        )

    def core_copy(self, hop, turn):
        spot = self.spot
        slot = hop * spot.group_count + turn
        if hop == 0:
            source, target = self.shard, self.whole(spot.chip, spot.core)
        else:
            source = self.piece(spot.back_chip(hop), spot.core, spot.back_group(turn))
            target = source
        return remote(
            source, target, self.core_send.at[slot], self.core_recv.at[slot], spot.partner()
        )

    def core_arrival(self, hop, turn):
        spot = self.spot
        slot = hop * spot.group_count + turn
        if hop == 0:
            here = self.whole(spot.chip, 1 - spot.core)
        else:
            here = self.piece(spot.back_chip(hop), 1 - spot.core, spot.back_group(turn))
        return remote(
            here, here, self.core_send.at[slot], self.core_recv.at[slot], spot.partner()
        )

    def own_copy(self):
        return pltpu.make_async_copy(
            self.shard, self.whole(self.spot.chip, self.spot.core), self.own_sem.at[0]
        )

    def tick(self, index):
        chips, groups = self.spot.chips, self.spot.group_count
        if index == 0:
            for hop in range(1, chips):
                self.line_copy(hop).start()
            self.core_copy(0, 0).start()
            self.own_copy().start()
        elif index < chips:
            hop = index
            self.line_arrival(hop).wait_recv()
            for turn in range(1, groups):
                self.cross_copy(hop, turn).start()
            self.core_copy(hop, 0).start()
        elif index < 2 * chips - 1:
            hop = index - chips + 1
            for turn in range(1, groups):
                self.cross_arrival(hop, turn).wait_recv()
                self.core_copy(hop, turn).start()
        else:
            self.own_copy().wait()
            self.core_copy(0, 0).wait_send()
            self.core_arrival(0, 0).wait_recv()
            for hop in range(1, chips):
                self.line_copy(hop).wait_send()
                self.core_copy(hop, 0).wait_send()
                self.core_arrival(hop, 0).wait_recv()
                for turn in range(1, groups):
                    self.cross_copy(hop, turn).wait_send()
                    self.core_copy(hop, turn).wait_send()
                    self.core_arrival(hop, turn).wait_recv()


def gather_sems(chips, group_count):
    dma = pltpu.SemaphoreType.DMA
    crossing = (chips * group_count,)
    return [dma((chips,)), dma((chips,))] + [dma(crossing)] * 4 + [dma((1,))]


def gather_kernel(chips, group_count, shard_ref, full_ref, *sems):
    spot = Spot(chips, group_count)
    job = Gather(spot, shard_ref, full_ref, sems)
    meet(spot)
    for index in range(job.tick_count):
        job.tick(index)


def gather_rows(shard):
    members, group_count = lax.axis_size("fsdp"), lax.axis_size("group")
    rows, width = shard.shape
    return pl.pallas_call(
        functools.partial(gather_kernel, members // 2, group_count),
        out_shape=jax.ShapeDtypeStruct((rows * members, width), BF),
        in_specs=[pl.BlockSpec(memory_space=pl.ANY)],
        out_specs=pl.BlockSpec(memory_space=pl.ANY),
        scratch_shapes=gather_sems(members // 2, group_count),
        compiler_params=pltpu.CompilerParams(collective_id=0, has_side_effects=True),
        name="gather_rows",
    )(shard)


def chunk_count(rows):
    return max(
        count for count in range(1, 7) if rows % (32 * count) == 0
    )


class Reduce:
    def __init__(self, spot, count, grad, swap, lands, loads, sends, sems):
        self.spot = spot
        self.count = count
        self.grad = grad
        self.swap = swap
        self.lands = lands
        self.loads = loads
        self.sends = sends
        (self.load_sems, self.send_sems, self.recv_sems, self.swap_send, self.swap_recv) = sems
        self.last = spot.chips - 1
        self.rows = grad.shape[0] // (2 * spot.chips)
        self.piece = self.rows // count
        self.items = self.last * count
        self.ticks = self.items + self.last
        self.slots = sends.shape[1]

    def swap_copy(self, chip, part):
        spot = self.spot
        start = part * self.piece
        source = (2 * chip + 1 - spot.core) * self.rows + start
        return remote(
            self.grad.at[pl.ds(pl.multiple_of(source, 8), self.piece)],
            self.swap.at[pl.ds(pl.multiple_of(chip * self.rows + start, 8), self.piece)],
            self.swap_send.at[chip * self.count + part],
            self.swap_recv.at[chip * self.count + part],
            spot.partner(),
        )

    def start(self):
        for chip in range(self.last, -1, -1):
            for part in range(self.count - 1, -1, -1):
                self.swap_copy(chip, part).start()
        self.fetch(0)

    def own_rows(self, chip, part):
        start = (2 * chip + self.spot.core) * self.rows + part * self.piece
        return self.grad.at[pl.ds(pl.multiple_of(start, 8), self.piece)]

    def swap_rows(self, chip, part):
        start = chip * self.rows + part * self.piece
        return self.swap.at[pl.ds(pl.multiple_of(start, 8), self.piece)]

    def land_rows(self, way, item):
        start = (way * self.items + item) * self.piece
        return self.lands.at[pl.ds(pl.multiple_of(start, 8), self.piece)]

    def plan(self, way, tick):
        spot, count, last = self.spot, self.count, self.last
        distance = spot.chip + way * (last - 2 * spot.chip)
        item = tick - distance
        raised = item + count * spot.chips
        chip = last - way - (lax.div(raised, count) - spot.chips)
        part = count - 1 - lax.rem(raised, count)
        inside = (item >= 0) & (item < self.items)
        ahead = (1 - 2 * way) * (chip - spot.chip)
        passes = inside & (ahead > 0)
        takes = distance > 0
        return item, chip, part, passes, takes

    def near_loads(self, way, tick, chip, part):
        turn = lax.rem(tick, 2)
        return [
            pltpu.make_async_copy(
                source,
                self.loads.at[way, 2 * turn + which],
                self.load_sems.at[way * 5 + 2 * turn + which],
            )
            for which, source in enumerate((self.own_rows(chip, part), self.swap_rows(chip, part)))
        ]

    def land_load(self, way, item):
        return pltpu.make_async_copy(
            self.land_rows(way, item), self.loads.at[way, 4], self.load_sems.at[way * 5 + 4]
        )

    def fetch(self, tick):
        for way in range(2):
            item, chip, part, passes, takes = self.plan(way, tick)

            @pl.when(passes)
            def _():
                self.swap_copy(chip, part).wait_recv()
                for copy in self.near_loads(way, tick, chip, part):
                    copy.start()

    def hop(self, way, item):
        spot = self.spot
        return remote(
            self.sends.at[way, lax.rem(item, self.slots)],
            self.land_rows(way, item),
            self.send_sems.at[way * self.items + item],
            self.recv_sems.at[way * self.items + item],
            spot.line(spot.chip + 1 - 2 * way),
        )

    def arrival(self, way, item):
        here = self.land_rows(way, item)
        sem = way * self.items + item
        return remote(
            here, here, self.send_sems.at[sem], self.recv_sems.at[sem], self.spot.partner()
        )

    def tick(self, tick):
        spot = self.spot
        nearer = jnp.where(2 * spot.chip > self.last, 1, 0)
        for turn in range(2):
            way = nearer if turn == 0 else 1 - nearer
            item, chip, part, passes, takes = self.plan(way, tick)

            @pl.when(passes)
            def _():
                @pl.when(takes)
                def _():
                    self.arrival(way, item).wait_recv()
                    self.land_load(way, item).start()

                slot = lax.rem(item, self.slots)
                first = way * (self.last - spot.chip) * self.count

                @pl.when(item - first >= self.slots)
                def _():
                    self.hop(way, item - self.slots).wait_send()

                for copy in self.near_loads(way, tick, chip, part):
                    copy.wait()

                @pl.when(takes)
                def _():
                    self.land_load(way, item).wait()
                    self.add(way, tick, slot, True)

                @pl.when(jnp.logical_not(takes))
                def _():
                    self.add(way, tick, slot, False)

                self.hop(way, item).start()

        self.fetch(tick + 1)

    def settle(self, order):
        spot = self.spot

        @pl.when(spot.chip > 0)
        def _():
            self.arrival(0, (self.last - spot.chip) * self.count + order).wait_recv()

        @pl.when(spot.chip < self.last)
        def _():
            self.arrival(1, (self.last - 1 - spot.chip) * self.count + order).wait_recv()

    def add(self, way, tick, slot, landed):
        block = 32
        near = 2 * lax.rem(tick, 2)

        def step(index, carry):
            rows = pl.ds(pl.multiple_of(index * block, block), block)
            total = self.loads[way, near, rows, :].astype(F32)
            total = total + self.loads[way, near + 1, rows, :].astype(F32)
            if landed:
                total = total + self.loads[way, 4, rows, :].astype(F32)
            self.sends[way, slot, rows, :] = total.astype(BF)
            return carry

        lax.fori_loop(0, self.piece // block, step, 0)

    def drain(self):
        spot = self.spot
        for way in range(2):
            begin = 0 if way == 0 else (self.last - spot.chip) * self.count
            end = (self.last - spot.chip) * self.count if way == 0 else self.items
            for back in range(1, self.slots + 1):

                @pl.when(end - back >= begin)
                def _():
                    self.hop(way, end - back).wait_send()

        for chip in range(spot.chips):
            for part in range(self.count):
                self.swap_copy(chip, part).wait_send()


def reduce_scratch(chips, rows, width):
    count = chunk_count(rows)
    dma = pltpu.SemaphoreType.DMA
    items = (chips - 1) * count
    return [
        pltpu.VMEM((2, 5, rows // count, width), BF),
        pltpu.VMEM((2, 4, rows // count, width), BF),
        dma((10,)),
        dma((2 * items,)),
        dma((2 * items,)),
        dma((chips * count,)),
        dma((chips * count,)),
    ]


def reduce_lands(chips, rows, width):
    return [
        jax.ShapeDtypeStruct((chips * rows, width), BF),
        jax.ShapeDtypeStruct((2 * (chips - 1) * rows, width), BF),
    ]


def move_of(master, gradient, first_mom, second_mom, rate):
    return adam_step(master, gradient, first_mom, second_mom, rate)[2]


def finish_kernel(
    chips,
    group_count,
    grad_zero,
    shard_one,
    weight_hbm,
    first_hbm,
    second_hbm,
    small_grad,
    small_ref,
    small_first,
    small_second,
    grad_out,
    sum_out,
    small_grad_out,
    small_sum_out,
    swap_zero,
    lands_zero,
    parts,
    states,
    grads,
    moves,
    quarters,
    sums,
    small_land,
    small_moves,
    small_move,
    part_sems,
    state_sems,
    grad_sems,
    cross_send,
    cross_recv,
    share_send,
    share_recv,
    share_own,
    small_send,
    small_recv,
    small_cross_send,
    small_cross_recv,
    *engine_scratch,
):
    tick = pl.program_id(0)
    spot = Spot(chips, group_count)
    rows = sum_out.shape[1]
    count = moves.shape[1]
    piece = rows // count
    quarter = piece // group_count
    engine = Reduce(
        spot,
        count,
        grad_zero,
        swap_zero,
        lands_zero,
        engine_scratch[0],
        engine_scratch[1],
        engine_scratch[2:],
    )
    members = 2 * chips
    last = chips - 1

    def small_send_copy(hop):
        target = lax.rem(spot.member + hop, members)
        return remote(
            small_grad,
            small_land.at[spot.member],
            small_send.at[hop],
            small_recv.at[hop],
            {"fsdp": target},
        )

    def small_cross_copy(turn):
        return remote(
            small_move,
            small_moves.at[spot.group],
            small_cross_send.at[turn],
            small_cross_recv.at[turn],
            spot.other(turn),
        )

    @pl.when(tick == 0)
    def _():
        barrier = pltpu.get_barrier_semaphore()
        for hop in range(1, members):
            pl.semaphore_signal(
                barrier,
                inc=1,
                device_id={"fsdp": lax.rem(spot.member + hop, members)},
                device_id_type=MESH_ID,
            )
        for turn in range(1, group_count):
            pl.semaphore_signal(barrier, inc=1, device_id=spot.other(turn), device_id_type=MESH_ID)
        pl.semaphore_wait(barrier, members - 1 + group_count - 1)
        engine.start()
        for hop in range(1, members):
            small_send_copy(hop).start()
        parts[...] = jnp.zeros_like(parts)

    bases = (engine.ticks - count, 1)

    def part_loads(layer, order):
        part, slot = count - 1 - order, lax.rem(order, 2)
        here = pl.multiple_of(part * piece, 8)
        start = (2 * spot.chip + spot.core) * rows + here
        sources = (shard_one.at[pl.ds(here, piece)],) if layer == 1 else (
            grad_zero.at[pl.ds(pl.multiple_of(start, 8), piece)],
            swap_zero.at[pl.ds(pl.multiple_of(spot.chip * rows + here, 8), piece)],
            lands_zero.at[
                pl.ds(pl.multiple_of(((last - spot.chip) * count + order) * piece, 8), piece)
            ],
            lands_zero.at[
                pl.ds(
                    pl.multiple_of(
                        ((2 * last - 1 - spot.chip) * count + order) * piece, 8
                    ),
                    piece,
                )
            ],
        )
        return [
            pltpu.make_async_copy(
                source,
                parts.at[layer, slot, which],
                part_sems.at[(2 * layer + slot) * 4 + which],
            )
            for which, source in enumerate(sources)
        ]

    def state_loads(layer, order):
        part, slot = count - 1 - order, lax.rem(order, 2)
        window = pl.ds(pl.multiple_of(part * piece, 8), piece)
        sources = (
            weight_hbm.at[layer, window],
            first_hbm.at[0, layer, window],
            second_hbm.at[0, layer, window],
        )
        return [
            pltpu.make_async_copy(
                source,
                states.at[layer, slot, which],
                state_sems.at[(2 * layer + slot) * 3 + which],
            )
            for which, source in enumerate(sources)
        ]

    def each_near(layer, order, act):
        copies = part_loads(layer, order)
        for copy in copies[:2]:
            act(copy)

    def each_landed(layer, order, act):
        if layer == 1:
            return
        copies = part_loads(layer, order)

        @pl.when(spot.chip > 0)
        def _():
            act(copies[2])

        @pl.when(spot.chip < last)
        def _():
            act(copies[3])

    def grad_store(layer, order):
        part = count - 1 - order
        return pltpu.make_async_copy(
            grads.at[layer, part],
            grad_out.at[layer, pl.ds(pl.multiple_of(part * piece, 8), piece)],
            grad_sems.at[layer * count + part],
        )

    def cross_copy(layer, order, turn):
        part = count - 1 - order
        target = lax.rem(spot.group + turn, group_count)
        sem = (layer * count + part) * group_count + turn
        return remote(
            moves.at[layer, part, pl.ds(pl.multiple_of(target * quarter, 8), quarter)],
            quarters.at[layer, part, turn],
            cross_send.at[sem],
            cross_recv.at[sem],
            spot.other(turn),
        )

    def share_rows(layer, part, group):
        start = pl.multiple_of(part * piece + group * quarter, 8)
        return sum_out.at[layer, pl.ds(start, quarter)]

    def share_copy(layer, order, turn):
        part = count - 1 - order
        sem = (layer * count + part) * group_count + turn
        return remote(
            sums.at[layer, part],
            share_rows(layer, part, spot.group),
            share_send.at[sem],
            share_recv.at[sem],
            spot.other(turn),
        )

    def share_local(layer, order):
        part = count - 1 - order
        return pltpu.make_async_copy(
            sums.at[layer, part],
            share_rows(layer, part, spot.group),
            share_own.at[layer * count + part],
        )

    def prepare(tick):
        for layer in range(2):
            order = tick - bases[layer]

            @pl.when((order >= 0) & (order < count))
            def _():
                if layer == 0:
                    engine.swap_copy(spot.chip, count - 1 - order).wait_recv()
                each_near(layer, order, lambda copy: copy.start())
                for copy in state_loads(layer, order):
                    copy.start()

    engine.tick(tick)
    prepare(tick + 1)
    landed = tick - bases[0]

    @pl.when((landed >= 0) & (landed < count))
    def _():
        engine.settle(landed)
        each_landed(0, landed, lambda copy: copy.start())

    for layer in range(2):
        later = tick - bases[layer] - 1

        @pl.when((later >= 0) & (later < count))
        def _():
            part = count - 1 - later
            for turn in range(1, group_count):
                cross_copy(layer, later, turn).wait_recv()
            total = moves[
                layer, part, pl.ds(pl.multiple_of(spot.group * quarter, 8), quarter), :
            ].astype(F32)
            for turn in range(1, group_count):
                total = total + quarters[layer, part, turn].astype(F32)
            sums[layer, part] = total.astype(sums.dtype)
            for turn in range(1, group_count):
                share_copy(layer, later, turn).start()
            share_local(layer, later).start()

        order = tick - bases[layer]

        @pl.when((order >= 0) & (order < count))
        def _():
            part, slot = count - 1 - order, lax.rem(order, 2)
            each_near(layer, order, lambda copy: copy.wait())
            each_landed(layer, order, lambda copy: copy.wait())
            for copy in state_loads(layer, order):
                copy.wait()

            def step(index, carry):
                window = pl.ds(pl.multiple_of(index * 32, 32), 32)
                total = parts[layer, slot, 0, window, :].astype(F32)
                for which in range(1, 4):
                    total = total + parts[layer, slot, which, window, :].astype(F32)
                low = total.astype(BF)
                grads[layer, part, window, :] = low
                move = move_of(
                    states[layer, slot, 0, window, :],
                    low.astype(F32),
                    states[layer, slot, 1, window, :],
                    states[layer, slot, 2, window, :],
                    INNER_RATE,
                )
                moves[layer, part, window, :] = move.astype(moves.dtype)
                return carry

            lax.fori_loop(0, piece // 32, step, 0)
            for turn in range(1, group_count):
                cross_copy(layer, order, turn).start()
            grad_store(layer, order).start()

    @pl.when(tick == 2)
    def _():
        small_land[spot.member] = small_grad[...]
        for hop in range(1, members):
            small_send_copy(hop).wait_recv()
        total = small_land[0]
        for member in range(1, members):
            total = total + small_land[member]
        small_grad_out[...] = total
        move = move_of(small_ref[...], total, small_first[...], small_second[...], SMALL_RATE)
        small_move[...] = move
        small_moves[spot.group] = move
        for turn in range(1, group_count):
            small_cross_copy(turn).start()

    @pl.when(tick == 4)
    def _():
        for turn in range(1, group_count):
            small_cross_copy(turn).wait_recv()
        total = small_moves[0]
        for group in range(1, group_count):
            total = total + small_moves[group]
        small_sum_out[...] = total

    @pl.when(tick == pl.num_programs(0) - 1)
    def _():
        engine.drain()
        for hop in range(1, members):
            small_send_copy(hop).wait_send()
        for turn in range(1, group_count):
            small_cross_copy(turn).wait_send()
        for layer in range(2):
            for order in range(count):
                grad_store(layer, order).wait()
                share_local(layer, order).wait()
                for turn in range(1, group_count):
                    cross_copy(layer, order, turn).wait_send()
                    share_copy(layer, order, turn).wait_send()
                    share_copy(layer, order, turn).wait_recv()


def finish(grad_zero, shard_one, weights, weight_m, weight_v, small_grad, small, small_m, small_v):
    members, group_count = lax.axis_size("fsdp"), lax.axis_size("group")
    chips = members // 2
    layers, rows, width = weights.shape
    count = chunk_count(rows)
    piece = rows // count
    quarter = piece // group_count
    wire = BF if quarter % 16 == 0 else F32
    small_size = small.shape[1]
    dma = pltpu.SemaphoreType.DMA
    ticks = (chips - 1) * count + chips - 1 + 1
    anywhere = pl.BlockSpec(memory_space=pl.ANY)
    local = pl.BlockSpec(memory_space=pltpu.VMEM)
    crossing = dma((layers * count * group_count,))
    return pl.pallas_call(
        functools.partial(finish_kernel, chips, group_count),
        grid=(ticks,),
        in_specs=[anywhere] * 5 + [local] * 4,
        out_specs=[anywhere, anywhere, local, local] + [anywhere] * 2,
        out_shape=[
            jax.ShapeDtypeStruct((layers, rows, width), BF),
            jax.ShapeDtypeStruct((layers, rows, width), wire),
            jax.ShapeDtypeStruct((1, small_size), F32),
            jax.ShapeDtypeStruct((1, small_size), F32),
        ]
        + reduce_lands(chips, rows, width),
        scratch_shapes=[
            pltpu.VMEM((layers, 2, 4, piece, width), BF),
            pltpu.VMEM((layers, 2, 3, piece, width), F32),
            pltpu.VMEM((layers, count, piece, width), BF),
            pltpu.VMEM((layers, count, piece, width), wire),
            pltpu.VMEM((layers, count, group_count, quarter, width), wire),
            pltpu.VMEM((layers, count, quarter, width), wire),
            pltpu.VMEM((members, 1, small_size), F32),
            pltpu.VMEM((group_count, 1, small_size), F32),
            pltpu.VMEM((1, small_size), F32),
            dma((8 * layers,)),
            dma((6 * layers,)),
            dma((layers * count,)),
            crossing,
            crossing,
            crossing,
            crossing,
            dma((layers * count,)),
            dma((members,)),
            dma((members,)),
            dma((group_count,)),
            dma((group_count,)),
        ]
        + reduce_scratch(chips, rows, width),
        compiler_params=pltpu.CompilerParams(
            vmem_limit_bytes=VMEM_LIMIT, collective_id=3, has_side_effects=True
        ),
        name="finish",
    )(grad_zero, shard_one, weights, weight_m, weight_v, small_grad, small, small_m, small_v)


def weight_copies(weight_hbm, weight_ref, sems, cuts):
    return [
        pltpu.make_async_copy(
            weight_hbm.at[pl.ds(cuts[index], cuts[index + 1] - cuts[index])],
            weight_ref.at[pl.ds(cuts[index], cuts[index + 1] - cuts[index])],
            sems.at[index],
        )
        for index in range(len(cuts) - 1)
    ]


def ahead_kernel(
    is_first,
    head_count,
    place,
    lengths_ref,
    slopes_ref,
    x_ref,
    gains_ref,
    weight_hbm,
    *rest,
):
    if place is not None:
        shard_ref, rest = rest[0], rest[1:]
        full_ref, rest = rest[11], rest[:11] + rest[12:]
        job_sems = rest[18:]
    (
        query_out,
    key_out,
    value_out,
    lse_out,
    att_out,
    total_one_out,
    hidden_out,
    slope_out,
    total_two_out,
    layer_out,
    low_out,
    weight_ref,
    dist_ref,
    mask_ref,
    query_t,
    value_t,
    att_t,
    sems,
    ) = rest[:18]
    step = pl.program_id(0)
    if place is not None:
        spot = Spot(*place)
        job = Gather(spot, shard_ref, full_ref, job_sems)
        spread = [round(index * 7 / (job.tick_count - 1)) for index in range(job.tick_count)]

    def tick(quarter):
        if place is None:
            return
        for index in range(job.tick_count):
            if spread[index] % 2 == quarter:

                @pl.when(step == spread[index] // 2)
                def _():
                    if index == 0:
                        meet(spot)
                    job.tick(index)

    tick(0)
    width = weight_ref.shape[1]
    inner = (weight_ref.shape[0] - 4 * width) // 2
    queries, keys = query_out.shape[1], key_out.shape[1]
    head = width // head_count
    cuts = [0, width, 3 * width, 4 * width, 4 * width + inner, 4 * width + 2 * inner]
    copies = weight_copies(weight_hbm, weight_ref, sems, cuts)
    key_step = 1 if is_first else 2

    @pl.when(step == 0)
    def _():
        for copy in copies:
            copy.start()
        fill_distance(dist_ref, key_step, 2)

    def need(index):
        @pl.when(step == 0)
        def _():
            copies[index].wait()

    fill_mask(mask_ref, key_step, lengths_ref[step])
    if is_first:
        memory_low = x_ref[0]
        residual = dot_nn(pair_matrix(queries, keys, 0.5, True), memory_low)
        query_low = residual.astype(BF)
    else:
        residual = x_ref[0]
        query_low = residual.astype(BF)
        memory_low = query_low
    low_out[0] = query_low
    need(0)
    query_rows = dot_nn(query_low, weight_ref[0:width]).astype(BF)
    query_out[0] = query_rows
    query_t[...] = (query_rows.astype(F32) * float(head) ** (-0.5)).T.astype(BF)
    need(1)
    key_out[0] = dot_nn(memory_low, weight_ref[width : 2 * width]).astype(BF)
    value_rows = dot_nn(memory_low, weight_ref[2 * width : 3 * width]).astype(BF)
    value_out[0] = value_rows
    value_t[...] = value_rows.astype(F32).T.astype(BF)

    def pair_step(pair, carry):
        start = pl.multiple_of(pair * 2 * head, 2 * head)
        key_pair = key_out[0, :, pl.ds(start, 2 * head)]
        query_pair = query_t[pl.ds(start, 2 * head), :]
        for which in range(2):
            index = 2 * pair + which
            scores = dot_nn(key_pair, pick_rows(query_pair, which))
            scores = scores - slopes_ref[index] * dist_ref[...] + mask_ref[...]
            peak = jnp.max(scores, axis=0, keepdims=True)
            lifted = jnp.exp(scores - peak)
            total = jnp.sum(lifted, axis=0, keepdims=True)
            shares = (lifted * (1.0 / total)).astype(BF)
            rows = pl.ds(start + which * head, head)
            mixed = dot_nn(value_t[rows, :], shares)
            att_t[rows, :] = mixed
            lse_out[0, pl.ds(index, 1), :] = peak + jnp.log(total)
        return carry

    lax.fori_loop(0, head_count // 2, pair_step, 0)
    attended = att_t[...].T.astype(BF)
    att_out[0] = attended
    need(2)
    total_one = residual + dot_nn(attended, weight_ref[3 * width : 4 * width])
    total_one_out[0] = total_one
    unit, _ = norm_parts(total_one)
    normed = unit * gains_ref[0:1] + gains_ref[1:2]
    normed_low = normed.astype(BF)
    need(3)
    need(4)
    total_two = normed
    for chunk in range(inner // width):
        inner_rows = pl.ds(4 * width + chunk * width, width)
        outer_rows = pl.ds(4 * width + inner + chunk * width, width)
        pre = dot_nt(normed_low, weight_ref[inner_rows, :])
        square = pre * pre
        bend = jnp.tanh(pre * (GELU_COEF + (GELU_COEF * GELU_CUBE) * square))
        half = 0.5 + 0.5 * bend
        hidden = (pre * half).astype(BF)
        steep = half + (0.5 * pre) * (1.0 - bend * bend) * (
            GELU_COEF + (3.0 * GELU_COEF * GELU_CUBE) * square
        )
        columns = pl.ds(chunk * width, width)
        hidden_out[0, :, columns] = hidden
        slope_out[0, :, columns] = steep.astype(BF)
        total_two = total_two + dot_nn(hidden, weight_ref[outer_rows, :])
    total_two_out[0] = total_two
    unit_two, _ = norm_parts(total_two)
    result = unit_two * gains_ref[2:3] + gains_ref[3:4]
    layer_out[0] = result.astype(layer_out.dtype)
    tick(1)


def layer_ahead(is_first, x, lengths, slopes, gains, weight_full, out_dtype, shard=None):
    batch, memory_length, width = x.shape
    queries = memory_length // 2 if is_first else memory_length
    keys = memory_length
    head_count = slopes.shape[0]
    rows = weight_full.shape[0]
    inner = (rows - 4 * width) // 2
    head_rows = -(-head_count // 8) * 8

    def block(length, size):
        return pl.BlockSpec((1, length, size), lambda i, *_: (i, 0, 0))

    def shape(length, size, dtype):
        return jax.ShapeDtypeStruct((batch, length, size), dtype)

    outs = [
        (queries, width, BF),
        (keys, width, BF),
        (keys, width, BF),
        (head_rows, queries, F32),
        (queries, width, BF),
        (queries, width, F32),
        (queries, inner, BF),
        (queries, inner, BF),
        (queries, width, F32),
        (queries, width, out_dtype),
        (queries, width, BF),
    ]
    flops = 2 * batch * width * (
        2 * queries * width + 2 * keys * width + 2 * queries * inner + 2 * queries * keys
    )
    hosted = shard is not None
    place = (lax.axis_size("fsdp") // 2, lax.axis_size("group")) if hosted else None
    anywhere = [pl.BlockSpec(memory_space=pl.ANY)] * hosted
    full_shape = [jax.ShapeDtypeStruct((rows, width), BF)] * hosted
    job_sems = gather_sems(*place) if hosted else []
    params = dict(collective_id=1, has_side_effects=True) if hosted else {}
    return pl.pallas_call(
        functools.partial(ahead_kernel, is_first, head_count, place),
        grid_spec=pltpu.PrefetchScalarGridSpec(
            num_scalar_prefetch=2,
            grid=(batch,),
            in_specs=[
                block(memory_length, width),
                pl.BlockSpec((4, width), lambda i, *_: (0, 0)),
                pl.BlockSpec(memory_space=pl.ANY),
            ]
            + anywhere,
            out_specs=[block(length, size) for length, size, _ in outs] + anywhere,
            scratch_shapes=[
                pltpu.VMEM((rows, width), BF),
                pltpu.VMEM((keys, queries), F32),
                pltpu.VMEM((keys, queries), F32),
                pltpu.VMEM((width, queries), BF),
                pltpu.VMEM((width, keys), BF),
                pltpu.VMEM((width, queries), F32),
                pltpu.SemaphoreType.DMA((5,)),
            ]
            + job_sems,
        ),
        out_shape=[shape(*out) for out in outs] + full_shape,
        compiler_params=pltpu.CompilerParams(vmem_limit_bytes=VMEM_LIMIT, **params),
        cost_estimate=pl.CostEstimate(
            flops=flops, bytes_accessed=rows * width * 2 + 30000000, transcendentals=0
        ),
        name="layer_ahead",
    )(lengths, slopes, x, gains, weight_full, *([shard] * hosted))


def back_kernel(
    is_first,
    head_count,
    place,
    query_steps,
    lengths_ref,
    slopes_ref,
    grad_ref,
    total_two_ref,
    total_one_ref,
    slope_ref,
    query_ref,
    key_ref,
    value_ref,
    att_ref,
    lse_ref,
    gains_ref,
    weight_hbm,
    *rest,
):
    if place is not None:
        grad_rows, rest = rest[0], rest[1:]
        landing, rest = rest[10:12], rest[:10] + rest[12:]
        job = rest[20:]
    (
        two_out,
        pre_out,
        normed_out,
        one_out,
        query_grad_out,
        key_grad_out,
        value_grad_out,
        input_out,
        gains_out,
        slopes_out,
        weight_ref,
        dist_ref,
        mask_ref,
        query_t,
        key_t,
        mixed_t,
        mixed_rows,
        delta_ref,
        query_grad_t,
        sems,
    ) = rest[:20]
    step = pl.program_id(0)
    if place is not None:
        spot = Spot(*place)
        engine = Reduce(
            spot,
            chunk_count(grad_rows.shape[0] // (2 * spot.chips)),
            grad_rows,
            landing[0],
            landing[1],
            job[0],
            job[1],
            job[2:],
        )

        early_ticks = engine.ticks - 1

        @pl.when(step == 0)
        def _():
            meet(spot)
            engine.start()
            engine.tick(0)

    pairs = head_count // 2
    sites = pairs + 2

    def reduce_ticks(site):
        if place is None:
            return
        total = sites * query_steps
        here = step * sites + site
        for index in range(-(-early_ticks // total)):
            tick = lax.div(here * early_ticks, total) + index + 1

            @pl.when(tick <= lax.div((here + 1) * early_ticks, total))
            def _():
                engine.tick(tick)

    width = weight_ref.shape[1]
    inner = (weight_ref.shape[0] - 4 * width) // 2
    queries, keys = query_ref.shape[1], key_ref.shape[1]
    head = width // head_count
    cuts = [0, 3 * width, 4 * width, 4 * width + inner, 4 * width + 2 * inner]
    copies = weight_copies(weight_hbm, weight_ref, sems, cuts)
    key_step = 1 if is_first else 2
    scale = float(head) ** (-0.5)

    @pl.when(step == 0)
    def _():
        for index in (3, 2, 1, 0):
            copies[index].start()
        fill_distance(dist_ref, key_step, 2)
        gains_out[...] = jnp.zeros_like(gains_out)
        slopes_out[...] = jnp.zeros_like(slopes_out)

    def need(index):
        @pl.when(step == 0)
        def _():
            copies[index].wait()

    fill_mask(mask_ref, key_step, lengths_ref[step])
    query_t[...] = (query_ref[0].astype(F32) * scale).T.astype(BF)
    key_t[...] = key_ref[0].astype(F32).T.astype(BF)

    grad = grad_ref[0].astype(F32)
    unit_two, inverse_two = norm_parts(total_two_ref[0])
    gains_out[2:3] += jnp.sum(grad * unit_two, axis=0, keepdims=True)
    gains_out[3:4] += jnp.sum(grad, axis=0, keepdims=True)
    back_two = norm_back(grad, unit_two, inverse_two, gains_ref[2:3])
    two_low = back_two.astype(BF)
    two_out[0] = two_low
    need(3)
    need(2)
    back_normed = back_two
    for chunk in range(inner // width):
        inner_rows = pl.ds(4 * width + chunk * width, width)
        outer_rows = pl.ds(4 * width + inner + chunk * width, width)
        columns = pl.ds(chunk * width, width)
        back_hidden = dot_nt(two_low, weight_ref[outer_rows, :])
        pre_grad = (back_hidden * slope_ref[0, :, columns].astype(F32)).astype(BF)
        pre_out[0, :, columns] = pre_grad
        back_normed = back_normed + dot_nn(pre_grad, weight_ref[inner_rows, :])
        if chunk % 2 == 1 and chunk < 4:
            reduce_ticks(chunk // 2)
    unit_one, inverse_one = norm_parts(total_one_ref[0])
    normed_out[0] = (unit_one * gains_ref[0:1] + gains_ref[1:2]).astype(BF)
    gains_out[0:1] += jnp.sum(back_normed * unit_one, axis=0, keepdims=True)
    gains_out[1:2] += jnp.sum(back_normed, axis=0, keepdims=True)
    back_one = norm_back(back_normed, unit_one, inverse_one, gains_ref[0:1])
    one_low = back_one.astype(BF)
    one_out[0] = one_low
    need(1)
    back_mixed = dot_nt(one_low, weight_ref[3 * width : 4 * width])
    mixed_low = back_mixed.astype(BF)
    mixed_rows[...] = mixed_low
    mixed_wide = mixed_low.astype(F32).T
    mixed_t[...] = mixed_wide.astype(BF)
    product = mixed_wide * att_ref[0].astype(F32).T
    delta_ref[...] = jnp.sum(product.reshape(head_count, head, queries), axis=1)

    def pair_step(pair, carry):
        start = pl.multiple_of(pair * 2 * head, 2 * head)
        lanes = pl.ds(start, 2 * head)
        key_pair = key_ref[0, :, lanes]
        value_pair = value_ref[0, :, lanes]
        query_pair = query_ref[0, :, lanes]
        mixed_pair = mixed_rows[:, lanes]
        query_pair_t = query_t[lanes, :]
        mixed_pair_t = mixed_t[lanes, :]
        key_grad = jnp.zeros((keys, 2 * head), F32)
        value_grad = jnp.zeros((keys, 2 * head), F32)
        for which in range(2):
            index = 2 * pair + which
            half = lane_half(2 * head, which)
            scores = dot_nn(key_pair, pick_rows(query_pair_t, which))
            scores = scores - slopes_ref[index] * dist_ref[...] + mask_ref[...]
            shares = jnp.exp(scores - lse_ref[0, pl.ds(index, 1), :])
            back_shares = dot_nn(value_pair, pick_rows(mixed_pair_t, which))
            back_scores = shares * (back_shares - delta_ref[pl.ds(index, 1), :])
            slopes_out[pl.ds(index, 1), :] += jnp.sum(
                back_scores * dist_ref[...], axis=0, keepdims=True
            )
            scores_low = back_scores.astype(BF)
            value_grad = value_grad + dot_nn(shares.astype(BF), mixed_pair * half)
            key_grad = key_grad + dot_nn(scores_low, query_pair * half)
            rows = pl.ds(start + which * head, head)
            query_grad_t[rows, :] = dot_nn(key_t[rows, :], scores_low)
        reduce_ticks(pair + 2)
        key_grad_out[0, :, lanes] = (key_grad * scale).astype(BF)
        value_grad_out[0, :, lanes] = value_grad.astype(BF)
        return carry

    lax.fori_loop(0, head_count // 2, pair_step, 0)
    query_grad = (query_grad_t[...] * scale).T.astype(BF)
    query_grad_out[0] = query_grad
    need(0)
    back_query = back_one + dot_nt(query_grad, weight_ref[0:width])
    back_memory = dot_nt(key_grad_out[0], weight_ref[width : 2 * width]) + dot_nt(
        value_grad_out[0], weight_ref[2 * width : 3 * width]
    )
    if is_first:
        spread = pair_matrix(queries, keys, 1.0, False)
        half_grad = back_query * 0.5
        upper = half_grad.astype(BF)
        lower = (half_grad - upper.astype(F32)).astype(BF)
        back_memory = back_memory + dot_nn(spread, upper) + dot_nn(spread, lower)
        input_out[0] = back_memory
    else:
        input_out[0] = back_query + back_memory
    if place is not None:

        @pl.when(step == pl.num_programs(0) - 1)
        def _():
            def late_tick(tick, carry):
                engine.tick(tick)
                return carry

            lax.fori_loop(early_ticks + 1, engine.ticks, late_tick, 0)
            for part in range(engine.count):
                engine.swap_copy(spot.chip, part).wait_recv()
                engine.settle(part)
            engine.drain()


def layer_back(is_first, grad, kept, lengths, slopes, gains, weight_full, grad_rows=None):
    (query_rows, key_rows, value_rows, lse, attended, total_one, steep, total_two) = kept
    batch, queries, width = query_rows.shape
    keys = key_rows.shape[1]
    head_count = slopes.shape[0]
    rows = weight_full.shape[0]
    inner = (rows - 4 * width) // 2
    head_rows = lse.shape[1]

    def block(length, size):
        return pl.BlockSpec((1, length, size), lambda i, *_: (i, 0, 0))

    def shape(length, size, dtype):
        return jax.ShapeDtypeStruct((batch, length, size), dtype)

    outs = [
        (queries, width, BF),
        (queries, inner, BF),
        (queries, width, BF),
        (queries, width, BF),
        (queries, width, BF),
        (keys, width, BF),
        (keys, width, BF),
        (keys, width, F32),
    ]
    flops = 2 * batch * width * (
        2 * queries * width + 2 * keys * width + 2 * queries * inner + 5 * queries * keys
    )
    hosted = grad_rows is not None
    place, job_scratch, lands, params = None, [], [], {}
    if hosted:
        place = (lax.axis_size("fsdp") // 2, lax.axis_size("group"))
        shard_rows = rows // (2 * place[0])
        job_scratch = reduce_scratch(place[0], shard_rows, width)
        lands = reduce_lands(place[0], shard_rows, width)
        params = dict(collective_id=2, has_side_effects=True)
    anywhere = pl.BlockSpec(memory_space=pl.ANY)
    return pl.pallas_call(
        functools.partial(back_kernel, is_first, head_count, place, batch),
        grid_spec=pltpu.PrefetchScalarGridSpec(
            num_scalar_prefetch=2,
            grid=(batch,),
            in_specs=[
                block(queries, width),
                block(queries, width),
                block(queries, width),
                block(queries, inner),
                block(queries, width),
                block(keys, width),
                block(keys, width),
                block(queries, width),
                block(head_rows, queries),
                pl.BlockSpec((4, width), lambda i, *_: (0, 0)),
                anywhere,
            ]
            + [anywhere] * hosted,
            out_specs=[block(length, size) for length, size, _ in outs]
            + [
                pl.BlockSpec((4, width), lambda i, *_: (0, 0)),
                pl.BlockSpec((head_rows, queries), lambda i, *_: (0, 0)),
            ]
            + [anywhere] * len(lands),
            scratch_shapes=[
                pltpu.VMEM((rows, width), BF),
                pltpu.VMEM((keys, queries), F32),
                pltpu.VMEM((keys, queries), F32),
                pltpu.VMEM((width, queries), BF),
                pltpu.VMEM((width, keys), BF),
                pltpu.VMEM((width, queries), BF),
                pltpu.VMEM((queries, width), BF),
                pltpu.VMEM((head_count, queries), F32),
                pltpu.VMEM((width, queries), F32),
                pltpu.SemaphoreType.DMA((4,)),
            ]
            + job_scratch,
        ),
        out_shape=[shape(*out) for out in outs]
        + [
            jax.ShapeDtypeStruct((4, width), F32),
            jax.ShapeDtypeStruct((head_rows, queries), F32),
        ]
        + lands,
        compiler_params=pltpu.CompilerParams(vmem_limit_bytes=VMEM_LIMIT, **params),
        cost_estimate=pl.CostEstimate(
            flops=flops, bytes_accessed=rows * width * 2 + 40000000, transcendentals=0
        ),
        name="layer_back",
    )(
        lengths,
        slopes,
        grad,
        total_two,
        total_one,
        steep,
        query_rows,
        key_rows,
        value_rows,
        attended,
        lse,
        gains,
        weight_full,
        *([grad_rows] * hosted),
    )


def weight_product(left, right):
    return lax.dot_general(
        left, right, (((0, 1), (0, 1)), ((), ())), preferred_element_type=F32
    )


def matrix_gradient(query_low, memory_low, attended, hidden, back):
    (two_low, pre_grad, normed_low, one_low, query_grad, key_grad, value_grad) = back
    return jnp.concatenate(
        [
            weight_product(query_low, query_grad),
            weight_product(memory_low, key_grad),
            weight_product(memory_low, value_grad),
            weight_product(attended, one_low),
            weight_product(pre_grad, normed_low),
            weight_product(hidden, two_low),
        ],
        axis=0,
    )


def adam_step(master, gradient, first_mom, second_mom, rate):
    first_new = BETA_ONE * first_mom + (1.0 - BETA_ONE) * gradient
    second_new = BETA_TWO * second_mom + (1.0 - BETA_TWO) * gradient * gradient
    first_hat = first_new / (1.0 - BETA_ONE**STEP)
    second_hat = second_new / (1.0 - BETA_TWO**STEP)
    inner_move = rate * (first_hat / (jnp.sqrt(second_hat) + ADAM_EPS) + DECAY_RATE * master)
    return (first_new, second_new, inner_move)


def outer_step(master, moves_sum, momentum_old, group_count):
    mean_move = moves_sum / group_count
    momentum_new = MOMENTUM * momentum_old + mean_move
    return (mean_move, momentum_new, master - OUTER_RATE * (mean_move + MOMENTUM * momentum_new))


def shards(
    hidden_in,
    lengths,
    out_grad,
    weights,
    weight_m,
    weight_v,
    outer_mom,
    small,
    small_m,
    small_v,
    small_mom,
):
    width = weights.shape[2]
    part_size = small.shape[0] // 2
    masters_low = [weights[layer].astype(BF) for layer in range(2)]

    gains = []
    slopes = []
    for layer in range(2):
        part = small[layer * part_size : (layer + 1) * part_size]
        gains.append(part[: 4 * width].reshape(4, width))
        slopes.append(part[4 * width :])

    matrix_two = lax.all_gather(masters_low[1], "fsdp", axis=0, tiled=True)
    matrix_one = gather_rows(masters_low[0])
    (q1, k1, v1, lse1, att1, one1, hid1, steep1, two1, first_out, low1) = layer_ahead(
        True, hidden_in, lengths, slopes[0], gains[0], matrix_one, F32
    )
    (q2, k2, v2, lse2, att2, one2, hid2, steep2, two2, block_out, low2) = layer_ahead(
        False, first_out, lengths, slopes[1], gains[1], matrix_two, BF
    )
    back_two = layer_back(
        False,
        out_grad,
        (q2, k2, v2, lse2, att2, one2, steep2, two2),
        lengths,
        slopes[1],
        gains[1],
        matrix_two,
    )
    matrix_grad_two = matrix_gradient(low2, low2, att2, hid2, back_two[:7]).astype(BF)
    first_grad, matrix_grad_two = lax.optimization_barrier((back_two[7], matrix_grad_two))
    shard_two = lax.psum_scatter(matrix_grad_two, "fsdp", scatter_dimension=0, tiled=True)
    back_one = layer_back(
        True,
        first_grad,
        (q1, k1, v1, lse1, att1, one1, steep1, two1),
        lengths,
        slopes[0],
        gains[0],
        matrix_one,
    )
    input_grad = back_one[7]
    matrix_grad_one = matrix_gradient(low1, hidden_in, att1, hid1, back_one[:7]).astype(BF)
    head_count = slopes[0].shape[0]
    small_parts = []
    for back in (back_one, back_two):
        small_parts += [back[8].reshape(-1), -jnp.sum(back[9][:head_count], axis=1)]
    grad_shard, weight_sum, small_grad, small_sum = finish(
        matrix_grad_one,
        shard_two,
        weights,
        weight_m,
        weight_v,
        jnp.concatenate(small_parts)[None],
        small[None],
        small_m,
        small_v,
    )[:4]
    weight_first, weight_second, _ = adam_step(
        weights, grad_shard[None].astype(F32), weight_m, weight_v, INNER_RATE
    )
    small_first, small_second, _ = adam_step(small, small_grad, small_m, small_v, SMALL_RATE)
    weight_sum, small_sum = weight_sum.astype(F32), small_sum[0]
    group_count = lax.axis_size("group")
    weight_mean, weight_mom, weight_new = outer_step(weights, weight_sum, outer_mom, group_count)
    small_mean, small_momentum, small_after = outer_step(small, small_sum, small_mom, group_count)
    return (
        block_out,
        input_grad,
        weight_new,
        weight_new.astype(BF),
        weight_first,
        weight_second,
        weight_mean,
        weight_mom,
        small_after,
        small_first,
        small_second,
        small_mean,
        small_momentum,
    )


def solution(mesh):
    in_specs = (
        P(("group", "fsdp"), None, None),
        P(("group", "fsdp")),
        P(("group", "fsdp"), None, None),
        P(None, "fsdp", None),
        P("group", None, "fsdp", None),
        P("group", None, "fsdp", None),
        P(None, "fsdp", None),
        P(),
        P("group", None),
        P("group", None),
        P(),
    )
    out_specs = (
        P(("group", "fsdp"), None, None),
        P(("group", "fsdp"), None, None),
        P(None, "fsdp", None),
        P(None, "fsdp", None),
        P("group", None, "fsdp", None),
        P("group", None, "fsdp", None),
        P(None, "fsdp", None),
        P(None, "fsdp", None),
        P(),
        P("group", None),
        P("group", None),
        P(),
        P(),
    )
    return jax.shard_map(shards, mesh=mesh, in_specs=in_specs, out_specs=out_specs, check_vma=False)
```

```python
import functools

import jax
import jax.numpy as jnp
from jax import lax
from jax.experimental import pallas as pl
from jax.experimental.pallas import tpu as pltpu
from jax.sharding import PartitionSpec as P

STEP = 10


EPS_NORM = 1e-06
MASK_FILL = -1e30
BETA_ONE = 0.9
BETA_TWO = 0.999
ADAM_EPS = 1e-08
DECAY_RATE = 0.01
INNER_RATE = 0.03
SMALL_RATE = 0.6
OUTER_RATE = 0.7
MOMENTUM = 0.9
GELU_COEF = 0.7978845608028654
GELU_CUBE = 0.044715

BF = jnp.bfloat16
F32 = jnp.float32
VMEM_LIMIT = 60 * 1024 * 1024
MESH_ID = pl.DeviceIdType.MESH


def dot_nn(left, right):
    return lax.dot_general(left, right, (((1,), (0,)), ((), ())), preferred_element_type=F32)


def dot_nt(left, right):
    return lax.dot_general(left, right, (((1,), (1,)), ((), ())), preferred_element_type=F32)


def dot_tn(left, right):
    return lax.dot_general(left, right, (((0,), (0,)), ((), ())), preferred_element_type=F32)


def norm_parts(total):
    center = total - jnp.mean(total, axis=-1, keepdims=True)
    inverse = lax.rsqrt(jnp.mean(center * center, axis=-1, keepdims=True) + EPS_NORM)
    return center * inverse, inverse


def norm_back(grad, unit, inverse, gain):
    scaled = grad * gain
    lead = jnp.mean(scaled, axis=-1, keepdims=True)
    along = jnp.mean(scaled * unit, axis=-1, keepdims=True)
    return inverse * (scaled - lead - unit * along)


def fill_distance(dist_ref, key_step, query_step):
    shape = dist_ref.shape
    keys = lax.broadcasted_iota(jnp.int32, shape, 0) * key_step
    queries = lax.broadcasted_iota(jnp.int32, shape, 1) * query_step
    dist_ref[...] = jnp.abs(queries - keys).astype(F32)


def fill_mask(mask_ref, key_step, length):
    keys = lax.broadcasted_iota(jnp.int32, mask_ref.shape, 0) * key_step
    mask_ref[...] = jnp.where(keys < length, 0.0, MASK_FILL)


def pick_rows(pair_rows, which):
    half = pair_rows.shape[0] // 2
    zero = jnp.zeros((half, pair_rows.shape[1]), pair_rows.dtype)
    if which == 0:
        return jnp.concatenate([pair_rows[:half], zero], axis=0)
    return jnp.concatenate([zero, pair_rows[half:]], axis=0)


def lane_half(width, which):
    lanes = lax.broadcasted_iota(jnp.int32, (1, width), 1)
    inside = lanes < width // 2 if which == 0 else lanes >= width // 2
    return jnp.where(inside, 1.0, 0.0).astype(BF)


def pair_matrix(queries, keys, value, by_query):
    shape = (queries, keys) if by_query else (keys, queries)
    query_index = lax.broadcasted_iota(jnp.int32, shape, 0 if by_query else 1)
    key_index = lax.broadcasted_iota(jnp.int32, shape, 1 if by_query else 0)
    offset = key_index - 2 * query_index
    return jnp.where((offset == 0) | (offset == 1), value, 0.0).astype(BF)


def remote(source, target, send_sem, recv_sem, device):
    return pltpu.make_async_remote_copy(
        src_ref=source,
        dst_ref=target,
        send_sem=send_sem,
        recv_sem=recv_sem,
        device_id=device,
        device_id_type=pl.DeviceIdType.MESH,
    )


class Spot:
    def __init__(self, chips, group_count):
        self.chips = chips
        self.group_count = group_count
        self.group = lax.axis_index("group")
        self.member = lax.axis_index("fsdp")
        self.chip = self.member // 2
        self.core = self.member % 2

    def line(self, chip):
        return {"fsdp": 2 * chip + self.core}

    def partner(self):
        return {"fsdp": 2 * self.chip + 1 - self.core}

    def other(self, turn):
        return {"group": lax.rem(self.group + turn, self.group_count)}

    def back_group(self, turn):
        return lax.rem(self.group + self.group_count - turn, self.group_count)

    def ahead_chip(self, hop):
        return lax.rem(self.chip + hop, self.chips)

    def back_chip(self, hop):
        return lax.rem(self.chip + self.chips - hop, self.chips)


def meet(spot):
    barrier = pltpu.get_barrier_semaphore()
    for hop in range(1, spot.chips):
        pl.semaphore_signal(
            barrier, inc=1, device_id=spot.line(spot.ahead_chip(hop)), device_id_type=MESH_ID
        )
    pl.semaphore_signal(barrier, inc=1, device_id=spot.partner(), device_id_type=MESH_ID)
    for turn in range(1, spot.group_count):
        pl.semaphore_signal(barrier, inc=1, device_id=spot.other(turn), device_id_type=MESH_ID)
    pl.semaphore_wait(barrier, spot.chips - 1 + 1 + spot.group_count - 1)


class Gather:
    def __init__(self, spot, shard_ref, full_ref, sems):
        self.spot = spot
        self.shard = shard_ref
        self.full = full_ref
        self.line_send, self.line_recv, self.cross_send, self.cross_recv = sems[:4]
        self.core_send, self.core_recv, self.own_sem = sems[4:]
        self.rows = shard_ref.shape[0]
        self.part = self.rows // spot.group_count
        self.tick_count = 2 * spot.chips

    def piece(self, chip, core, group):
        start = (2 * chip + core) * self.rows + group * self.part
        return self.full.at[pl.ds(start, self.part)]

    def whole(self, chip, core):
        return self.full.at[pl.ds((2 * chip + core) * self.rows, self.rows)]

    def line_copy(self, hop):
        spot = self.spot
        return remote(
            self.shard.at[pl.ds(spot.group * self.part, self.part)],
            self.piece(spot.chip, spot.core, spot.group),
            self.line_send.at[hop],
            self.line_recv.at[hop],
            spot.line(spot.ahead_chip(hop)),
        )

    def line_arrival(self, hop):
        spot = self.spot
        here = self.piece(spot.back_chip(hop), spot.core, spot.group)
        return remote(
            here, here, self.line_send.at[hop], self.line_recv.at[hop], spot.partner()
        )

    def cross_copy(self, hop, turn):
        spot = self.spot
        here = self.piece(spot.back_chip(hop), spot.core, spot.group)
        slot = hop * spot.group_count + turn
        return remote(
            here, here, self.cross_send.at[slot], self.cross_recv.at[slot], spot.other(turn)
        )

    def cross_arrival(self, hop, turn):
        spot = self.spot
        here = self.piece(spot.back_chip(hop), spot.core, spot.back_group(turn))
        slot = hop * spot.group_count + turn
        return remote(
            here, here, self.cross_send.at[slot], self.cross_recv.at[slot], spot.partner()
        )

    def core_copy(self, hop, turn):
        spot = self.spot
        slot = hop * spot.group_count + turn
        if hop == 0:
            source, target = self.shard, self.whole(spot.chip, spot.core)
        else:
            source = self.piece(spot.back_chip(hop), spot.core, spot.back_group(turn))
            target = source
        return remote(
            source, target, self.core_send.at[slot], self.core_recv.at[slot], spot.partner()
        )

    def core_arrival(self, hop, turn):
        spot = self.spot
        slot = hop * spot.group_count + turn
        if hop == 0:
            here = self.whole(spot.chip, 1 - spot.core)
        else:
            here = self.piece(spot.back_chip(hop), 1 - spot.core, spot.back_group(turn))
        return remote(
            here, here, self.core_send.at[slot], self.core_recv.at[slot], spot.partner()
        )

    def own_copy(self):
        return pltpu.make_async_copy(
            self.shard, self.whole(self.spot.chip, self.spot.core), self.own_sem.at[0]
        )

    def tick(self, index):
        chips, groups = self.spot.chips, self.spot.group_count
        if index == 0:
            for hop in range(1, chips):
                self.line_copy(hop).start()
            self.core_copy(0, 0).start()
            self.own_copy().start()
        elif index < chips:
            hop = index
            self.line_arrival(hop).wait_recv()
            for turn in range(1, groups):
                self.cross_copy(hop, turn).start()
            self.core_copy(hop, 0).start()
        elif index < 2 * chips - 1:
            hop = index - chips + 1
            for turn in range(1, groups):
                self.cross_arrival(hop, turn).wait_recv()
                self.core_copy(hop, turn).start()
        else:
            self.own_copy().wait()
            self.core_copy(0, 0).wait_send()
            self.core_arrival(0, 0).wait_recv()
            for hop in range(1, chips):
                self.line_copy(hop).wait_send()
                self.core_copy(hop, 0).wait_send()
                self.core_arrival(hop, 0).wait_recv()
                for turn in range(1, groups):
                    self.cross_copy(hop, turn).wait_send()
                    self.core_copy(hop, turn).wait_send()
                    self.core_arrival(hop, turn).wait_recv()


def gather_sems(chips, group_count):
    dma = pltpu.SemaphoreType.DMA
    crossing = (chips * group_count,)
    return [dma((chips,)), dma((chips,))] + [dma(crossing)] * 4 + [dma((1,))]


def gather_kernel(chips, group_count, shard_ref, full_ref, *sems):
    spot = Spot(chips, group_count)
    job = Gather(spot, shard_ref, full_ref, sems)
    meet(spot)
    for index in range(job.tick_count):
        job.tick(index)


def gather_rows(shard):
    members, group_count = lax.axis_size("fsdp"), lax.axis_size("group")
    rows, width = shard.shape
    return pl.pallas_call(
        functools.partial(gather_kernel, members // 2, group_count),
        out_shape=jax.ShapeDtypeStruct((rows * members, width), BF),
        in_specs=[pl.BlockSpec(memory_space=pl.ANY)],
        out_specs=pl.BlockSpec(memory_space=pl.ANY),
        scratch_shapes=gather_sems(members // 2, group_count),
        compiler_params=pltpu.CompilerParams(collective_id=0, has_side_effects=True),
        name="gather_rows",
    )(shard)


def chunk_count(rows):
    return max(
        count for count in range(1, 7) if rows % (32 * count) == 0
    )


class Reduce:
    def __init__(self, spot, count, grad, swap, lands, loads, sends, sems):
        self.spot = spot
        self.count = count
        self.grad = grad
        self.swap = swap
        self.lands = lands
        self.loads = loads
        self.sends = sends
        (self.load_sems, self.send_sems, self.recv_sems, self.swap_send, self.swap_recv) = sems
        self.last = spot.chips - 1
        self.rows = grad.shape[0] // (2 * spot.chips)
        self.piece = self.rows // count
        self.items = self.last * count
        self.ticks = self.items + self.last
        self.slots = sends.shape[1]

    def swap_copy(self, chip, part):
        spot = self.spot
        start = part * self.piece
        source = (2 * chip + 1 - spot.core) * self.rows + start
        return remote(
            self.grad.at[pl.ds(pl.multiple_of(source, 8), self.piece)],
            self.swap.at[pl.ds(pl.multiple_of(chip * self.rows + start, 8), self.piece)],
            self.swap_send.at[chip * self.count + part],
            self.swap_recv.at[chip * self.count + part],
            spot.partner(),
        )

    def start(self):
        for chip in range(self.last, -1, -1):
            for part in range(self.count - 1, -1, -1):
                self.swap_copy(chip, part).start()
        self.fetch(0)

    def own_rows(self, chip, part):
        start = (2 * chip + self.spot.core) * self.rows + part * self.piece
        return self.grad.at[pl.ds(pl.multiple_of(start, 8), self.piece)]

    def swap_rows(self, chip, part):
        start = chip * self.rows + part * self.piece
        return self.swap.at[pl.ds(pl.multiple_of(start, 8), self.piece)]

    def land_rows(self, way, item):
        start = (way * self.items + item) * self.piece
        return self.lands.at[pl.ds(pl.multiple_of(start, 8), self.piece)]

    def plan(self, way, tick):
        spot, count, last = self.spot, self.count, self.last
        distance = spot.chip + way * (last - 2 * spot.chip)
        item = tick - distance
        raised = item + count * spot.chips
        chip = last - way - (lax.div(raised, count) - spot.chips)
        part = count - 1 - lax.rem(raised, count)
        inside = (item >= 0) & (item < self.items)
        ahead = (1 - 2 * way) * (chip - spot.chip)
        passes = inside & (ahead > 0)
        takes = distance > 0
        return item, chip, part, passes, takes

    def near_loads(self, way, tick, chip, part):
        turn = lax.rem(tick, 2)
        return [
            pltpu.make_async_copy(
                source,
                self.loads.at[way, 2 * turn + which],
                self.load_sems.at[way * 5 + 2 * turn + which],
            )
            for which, source in enumerate((self.own_rows(chip, part), self.swap_rows(chip, part)))
        ]

    def land_load(self, way, item):
        return pltpu.make_async_copy(
            self.land_rows(way, item), self.loads.at[way, 4], self.load_sems.at[way * 5 + 4]
        )

    def fetch(self, tick):
        for way in range(2):
            item, chip, part, passes, takes = self.plan(way, tick)

            @pl.when(passes)
            def _():
                self.swap_copy(chip, part).wait_recv()
                for copy in self.near_loads(way, tick, chip, part):
                    copy.start()

    def hop(self, way, item):
        spot = self.spot
        return remote(
            self.sends.at[way, lax.rem(item, self.slots)],
            self.land_rows(way, item),
            self.send_sems.at[way * self.items + item],
            self.recv_sems.at[way * self.items + item],
            spot.line(spot.chip + 1 - 2 * way),
        )

    def arrival(self, way, item):
        here = self.land_rows(way, item)
        sem = way * self.items + item
        return remote(
            here, here, self.send_sems.at[sem], self.recv_sems.at[sem], self.spot.partner()
        )

    def tick(self, tick):
        spot = self.spot
        nearer = jnp.where(2 * spot.chip > self.last, 1, 0)
        for turn in range(2):
            way = nearer if turn == 0 else 1 - nearer
            item, chip, part, passes, takes = self.plan(way, tick)

            @pl.when(passes)
            def _():
                @pl.when(takes)
                def _():
                    self.arrival(way, item).wait_recv()
                    self.land_load(way, item).start()

                slot = lax.rem(item, self.slots)
                first = way * (self.last - spot.chip) * self.count

                @pl.when(item - first >= self.slots)
                def _():
                    self.hop(way, item - self.slots).wait_send()

                for copy in self.near_loads(way, tick, chip, part):
                    copy.wait()

                @pl.when(takes)
                def _():
                    self.land_load(way, item).wait()
                    self.add(way, tick, slot, True)

                @pl.when(jnp.logical_not(takes))
                def _():
                    self.add(way, tick, slot, False)

                self.hop(way, item).start()

        self.fetch(tick + 1)

    def settle(self, order):
        spot = self.spot

        @pl.when(spot.chip > 0)
        def _():
            self.arrival(0, (self.last - spot.chip) * self.count + order).wait_recv()

        @pl.when(spot.chip < self.last)
        def _():
            self.arrival(1, (self.last - 1 - spot.chip) * self.count + order).wait_recv()

    def add(self, way, tick, slot, landed):
        block = 32
        near = 2 * lax.rem(tick, 2)

        def step(index, carry):
            rows = pl.ds(pl.multiple_of(index * block, block), block)
            total = self.loads[way, near, rows, :].astype(F32)
            total = total + self.loads[way, near + 1, rows, :].astype(F32)
            if landed:
                total = total + self.loads[way, 4, rows, :].astype(F32)
            self.sends[way, slot, rows, :] = total.astype(BF)
            return carry

        lax.fori_loop(0, self.piece // block, step, 0)

    def drain(self):
        spot = self.spot
        for way in range(2):
            begin = 0 if way == 0 else (self.last - spot.chip) * self.count
            end = (self.last - spot.chip) * self.count if way == 0 else self.items
            for back in range(1, self.slots + 1):

                @pl.when(end - back >= begin)
                def _():
                    self.hop(way, end - back).wait_send()

        for chip in range(spot.chips):
            for part in range(self.count):
                self.swap_copy(chip, part).wait_send()


def reduce_scratch(chips, rows, width):
    count = chunk_count(rows)
    dma = pltpu.SemaphoreType.DMA
    items = (chips - 1) * count
    return [
        pltpu.VMEM((2, 5, rows // count, width), BF),
        pltpu.VMEM((2, 4, rows // count, width), BF),
        dma((10,)),
        dma((2 * items,)),
        dma((2 * items,)),
        dma((chips * count,)),
        dma((chips * count,)),
    ]


def reduce_lands(chips, rows, width):
    return [
        jax.ShapeDtypeStruct((chips * rows, width), BF),
        jax.ShapeDtypeStruct((2 * (chips - 1) * rows, width), BF),
    ]


def move_of(master, gradient, first_mom, second_mom, rate):
    return adam_step(master, gradient, first_mom, second_mom, rate)[2]


def finish_kernel(
    chips,
    group_count,
    grad_zero,
    shard_one,
    weight_hbm,
    first_hbm,
    second_hbm,
    small_grad,
    small_ref,
    small_first,
    small_second,
    grad_out,
    sum_out,
    small_grad_out,
    small_sum_out,
    swap_zero,
    lands_zero,
    parts,
    states,
    grads,
    moves,
    quarters,
    sums,
    small_land,
    small_moves,
    small_move,
    part_sems,
    state_sems,
    grad_sems,
    cross_send,
    cross_recv,
    share_send,
    share_recv,
    share_own,
    small_send,
    small_recv,
    small_cross_send,
    small_cross_recv,
    *engine_scratch,
):
    tick = pl.program_id(0)
    spot = Spot(chips, group_count)
    rows = sum_out.shape[1]
    count = moves.shape[1]
    piece = rows // count
    quarter = piece // group_count
    engine = Reduce(
        spot,
        count,
        grad_zero,
        swap_zero,
        lands_zero,
        engine_scratch[0],
        engine_scratch[1],
        engine_scratch[2:],
    )
    members = 2 * chips
    last = chips - 1

    def small_send_copy(hop):
        target = lax.rem(spot.member + hop, members)
        return remote(
            small_grad,
            small_land.at[spot.member],
            small_send.at[hop],
            small_recv.at[hop],
            {"fsdp": target},
        )

    def small_cross_copy(turn):
        return remote(
            small_move,
            small_moves.at[spot.group],
            small_cross_send.at[turn],
            small_cross_recv.at[turn],
            spot.other(turn),
        )

    @pl.when(tick == 0)
    def _():
        barrier = pltpu.get_barrier_semaphore()
        for hop in range(1, members):
            pl.semaphore_signal(
                barrier,
                inc=1,
                device_id={"fsdp": lax.rem(spot.member + hop, members)},
                device_id_type=MESH_ID,
            )
        for turn in range(1, group_count):
            pl.semaphore_signal(barrier, inc=1, device_id=spot.other(turn), device_id_type=MESH_ID)
        pl.semaphore_wait(barrier, members - 1 + group_count - 1)
        engine.start()
        for hop in range(1, members):
            small_send_copy(hop).start()
        parts[...] = jnp.zeros_like(parts)

    bases = (engine.ticks - count, 1)

    def part_loads(layer, order):
        part, slot = count - 1 - order, lax.rem(order, 2)
        here = pl.multiple_of(part * piece, 8)
        start = (2 * spot.chip + spot.core) * rows + here
        sources = (shard_one.at[pl.ds(here, piece)],) if layer == 1 else (
            grad_zero.at[pl.ds(pl.multiple_of(start, 8), piece)],
            swap_zero.at[pl.ds(pl.multiple_of(spot.chip * rows + here, 8), piece)],
            lands_zero.at[
                pl.ds(pl.multiple_of(((last - spot.chip) * count + order) * piece, 8), piece)
            ],
            lands_zero.at[
                pl.ds(
                    pl.multiple_of(
                        ((2 * last - 1 - spot.chip) * count + order) * piece, 8
                    ),
                    piece,
                )
            ],
        )
        return [
            pltpu.make_async_copy(
                source,
                parts.at[layer, slot, which],
                part_sems.at[(2 * layer + slot) * 4 + which],
            )
            for which, source in enumerate(sources)
        ]

    def state_loads(layer, order):
        part, slot = count - 1 - order, lax.rem(order, 2)
        window = pl.ds(pl.multiple_of(part * piece, 8), piece)
        sources = (
            weight_hbm.at[layer, window],
            first_hbm.at[0, layer, window],
            second_hbm.at[0, layer, window],
        )
        return [
            pltpu.make_async_copy(
                source,
                states.at[layer, slot, which],
                state_sems.at[(2 * layer + slot) * 3 + which],
            )
            for which, source in enumerate(sources)
        ]

    def each_near(layer, order, act):
        copies = part_loads(layer, order)
        for copy in copies[:2]:
            act(copy)

    def each_landed(layer, order, act):
        if layer == 1:
            return
        copies = part_loads(layer, order)

        @pl.when(spot.chip > 0)
        def _():
            act(copies[2])

        @pl.when(spot.chip < last)
        def _():
            act(copies[3])

    def grad_store(layer, order):
        part = count - 1 - order
        return pltpu.make_async_copy(
            grads.at[layer, part],
            grad_out.at[layer, pl.ds(pl.multiple_of(part * piece, 8), piece)],
            grad_sems.at[layer * count + part],
        )

    def cross_copy(layer, order, turn):
        part = count - 1 - order
        target = lax.rem(spot.group + turn, group_count)
        sem = (layer * count + part) * group_count + turn
        return remote(
            moves.at[layer, part, pl.ds(pl.multiple_of(target * quarter, 8), quarter)],
            quarters.at[layer, part, turn],
            cross_send.at[sem],
            cross_recv.at[sem],
            spot.other(turn),
        )

    def share_rows(layer, part, group):
        start = pl.multiple_of(part * piece + group * quarter, 8)
        return sum_out.at[layer, pl.ds(start, quarter)]

    def share_copy(layer, order, turn):
        part = count - 1 - order
        sem = (layer * count + part) * group_count + turn
        return remote(
            sums.at[layer, part],
            share_rows(layer, part, spot.group),
            share_send.at[sem],
            share_recv.at[sem],
            spot.other(turn),
        )

    def share_local(layer, order):
        part = count - 1 - order
        return pltpu.make_async_copy(
            sums.at[layer, part],
            share_rows(layer, part, spot.group),
            share_own.at[layer * count + part],
        )

    def prepare(tick):
        for layer in range(2):
            order = tick - bases[layer]

            @pl.when((order >= 0) & (order < count))
            def _():
                if layer == 0:
                    engine.swap_copy(spot.chip, count - 1 - order).wait_recv()
                each_near(layer, order, lambda copy: copy.start())
                for copy in state_loads(layer, order):
                    copy.start()

    engine.tick(tick)
    prepare(tick + 1)
    landed = tick - bases[0]

    @pl.when((landed >= 0) & (landed < count))
    def _():
        engine.settle(landed)
        each_landed(0, landed, lambda copy: copy.start())

    for layer in range(2):
        later = tick - bases[layer] - 1

        @pl.when((later >= 0) & (later < count))
        def _():
            part = count - 1 - later
            for turn in range(1, group_count):
                cross_copy(layer, later, turn).wait_recv()
            total = moves[
                layer, part, pl.ds(pl.multiple_of(spot.group * quarter, 8), quarter), :
            ].astype(F32)
            for turn in range(1, group_count):
                total = total + quarters[layer, part, turn].astype(F32)
            sums[layer, part] = total.astype(sums.dtype)
            for turn in range(1, group_count):
                share_copy(layer, later, turn).start()
            share_local(layer, later).start()

        order = tick - bases[layer]

        @pl.when((order >= 0) & (order < count))
        def _():
            part, slot = count - 1 - order, lax.rem(order, 2)
            each_near(layer, order, lambda copy: copy.wait())
            each_landed(layer, order, lambda copy: copy.wait())
            for copy in state_loads(layer, order):
                copy.wait()

            def step(index, carry):
                window = pl.ds(pl.multiple_of(index * 32, 32), 32)
                total = parts[layer, slot, 0, window, :].astype(F32)
                for which in range(1, 4):
                    total = total + parts[layer, slot, which, window, :].astype(F32)
                low = total.astype(BF)
                grads[layer, part, window, :] = low
                move = move_of(
                    states[layer, slot, 0, window, :],
                    low.astype(F32),
                    states[layer, slot, 1, window, :],
                    states[layer, slot, 2, window, :],
                    INNER_RATE,
                )
                moves[layer, part, window, :] = move.astype(moves.dtype)
                return carry

            lax.fori_loop(0, piece // 32, step, 0)
            for turn in range(1, group_count):
                cross_copy(layer, order, turn).start()
            grad_store(layer, order).start()

    @pl.when(tick == 2)
    def _():
        small_land[spot.member] = small_grad[...]
        for hop in range(1, members):
            small_send_copy(hop).wait_recv()
        total = small_land[0]
        for member in range(1, members):
            total = total + small_land[member]
        small_grad_out[...] = total
        move = move_of(small_ref[...], total, small_first[...], small_second[...], SMALL_RATE)
        small_move[...] = move
        small_moves[spot.group] = move
        for turn in range(1, group_count):
            small_cross_copy(turn).start()

    @pl.when(tick == 4)
    def _():
        for turn in range(1, group_count):
            small_cross_copy(turn).wait_recv()
        total = small_moves[0]
        for group in range(1, group_count):
            total = total + small_moves[group]
        small_sum_out[...] = total

    @pl.when(tick == pl.num_programs(0) - 1)
    def _():
        engine.drain()
        for hop in range(1, members):
            small_send_copy(hop).wait_send()
        for turn in range(1, group_count):
            small_cross_copy(turn).wait_send()
        for layer in range(2):
            for order in range(count):
                grad_store(layer, order).wait()
                share_local(layer, order).wait()
                for turn in range(1, group_count):
                    cross_copy(layer, order, turn).wait_send()
                    share_copy(layer, order, turn).wait_send()
                    share_copy(layer, order, turn).wait_recv()


def finish(grad_zero, shard_one, weights, weight_m, weight_v, small_grad, small, small_m, small_v):
    members, group_count = lax.axis_size("fsdp"), lax.axis_size("group")
    chips = members // 2
    layers, rows, width = weights.shape
    count = chunk_count(rows)
    piece = rows // count
    quarter = piece // group_count
    wire = BF if quarter % 16 == 0 else F32
    small_size = small.shape[1]
    dma = pltpu.SemaphoreType.DMA
    ticks = (chips - 1) * count + chips - 1 + 1
    anywhere = pl.BlockSpec(memory_space=pl.ANY)
    local = pl.BlockSpec(memory_space=pltpu.VMEM)
    crossing = dma((layers * count * group_count,))
    return pl.pallas_call(
        functools.partial(finish_kernel, chips, group_count),
        grid=(ticks,),
        in_specs=[anywhere] * 5 + [local] * 4,
        out_specs=[anywhere, anywhere, local, local] + [anywhere] * 2,
        out_shape=[
            jax.ShapeDtypeStruct((layers, rows, width), BF),
            jax.ShapeDtypeStruct((layers, rows, width), wire),
            jax.ShapeDtypeStruct((1, small_size), F32),
            jax.ShapeDtypeStruct((1, small_size), F32),
        ]
        + reduce_lands(chips, rows, width),
        scratch_shapes=[
            pltpu.VMEM((layers, 2, 4, piece, width), BF),
            pltpu.VMEM((layers, 2, 3, piece, width), F32),
            pltpu.VMEM((layers, count, piece, width), BF),
            pltpu.VMEM((layers, count, piece, width), wire),
            pltpu.VMEM((layers, count, group_count, quarter, width), wire),
            pltpu.VMEM((layers, count, quarter, width), wire),
            pltpu.VMEM((members, 1, small_size), F32),
            pltpu.VMEM((group_count, 1, small_size), F32),
            pltpu.VMEM((1, small_size), F32),
            dma((8 * layers,)),
            dma((6 * layers,)),
            dma((layers * count,)),
            crossing,
            crossing,
            crossing,
            crossing,
            dma((layers * count,)),
            dma((members,)),
            dma((members,)),
            dma((group_count,)),
            dma((group_count,)),
        ]
        + reduce_scratch(chips, rows, width),
        compiler_params=pltpu.CompilerParams(
            vmem_limit_bytes=VMEM_LIMIT, collective_id=3, has_side_effects=True
        ),
        name="finish",
    )(grad_zero, shard_one, weights, weight_m, weight_v, small_grad, small, small_m, small_v)


def weight_copies(weight_hbm, weight_ref, sems, ranges):
    return [
        pltpu.make_async_copy(
            weight_hbm.at[pl.ds(start, size)], weight_ref.at[pl.ds(start, size)], sems.at[index]
        )
        for index, (start, size) in enumerate(ranges)
    ]


class Rolling:
    def __init__(self, copies, active, depth=2):
        self.copies = copies
        self.active = active
        self.depth = depth

    def start(self):
        for copy in self.copies[: self.depth]:
            copy.start()

    def need(self, index):
        @pl.when(self.active)
        def _():
            self.copies[index].wait()
            if index + self.depth < len(self.copies):
                self.copies[index + self.depth].start()


def feed_cuts(width, inner):
    ranges = [(0, width), (width, 2 * width), (3 * width, width)]
    return ranges + [(4 * width, inner), (4 * width + inner, inner)]


def ahead_kernel(
    is_first,
    head_count,
    place,
    lengths_ref,
    slopes_ref,
    x_ref,
    gains_ref,
    weight_hbm,
    *rest,
):
    if place is not None:
        shard_ref, rest = rest[0], rest[1:]
        full_ref, rest = rest[11], rest[:11] + rest[12:]
        job_sems = rest[18:]
    (
        query_out,
    key_out,
    value_out,
    lse_out,
    att_out,
    total_one_out,
    hidden_out,
    slope_out,
    total_two_out,
    layer_out,
    low_out,
    weight_ref,
    dist_ref,
    mask_ref,
    query_t,
    value_t,
    att_t,
    sems,
    ) = rest[:18]
    step = pl.program_id(0)
    if place is not None:
        spot = Spot(*place)
        job = Gather(spot, shard_ref, full_ref, job_sems)
        spread = [round(index * 7 / (job.tick_count - 1)) for index in range(job.tick_count)]

    def tick(quarter):
        if place is None:
            return
        for index in range(job.tick_count):
            if spread[index] % 2 == quarter:

                @pl.when(step == spread[index] // 2)
                def _():
                    if index == 0:
                        meet(spot)
                    job.tick(index)

    tick(0)
    width = weight_ref.shape[1]
    inner = (weight_ref.shape[0] - 4 * width) // 2
    queries, keys = query_out.shape[1], key_out.shape[1]
    head = width // head_count
    copies = weight_copies(weight_hbm, weight_ref, sems, feed_cuts(width, inner))
    rolling = Rolling(copies, step == 0)
    key_step = 1 if is_first else 2

    @pl.when(step == 0)
    def _():
        rolling.start()
        fill_distance(dist_ref, key_step, 2)

    fill_mask(mask_ref, key_step, lengths_ref[step])
    if is_first:
        memory_low = x_ref[0]
        residual = dot_nn(pair_matrix(queries, keys, 0.5, True), memory_low)
        query_low = residual.astype(BF)
    else:
        residual = x_ref[0]
        query_low = residual.astype(BF)
        memory_low = query_low
    low_out[0] = query_low
    rolling.need(0)
    query_rows = dot_nn(query_low, weight_ref[0:width]).astype(BF)
    query_out[0] = query_rows
    query_t[...] = (query_rows.astype(F32) * float(head) ** (-0.5)).T.astype(BF)
    rolling.need(1)
    key_out[0] = dot_nn(memory_low, weight_ref[width : 2 * width]).astype(BF)
    value_rows = dot_nn(memory_low, weight_ref[2 * width : 3 * width]).astype(BF)
    value_out[0] = value_rows
    value_t[...] = value_rows.astype(F32).T.astype(BF)

    def pair_step(pair, carry):
        start = pl.multiple_of(pair * 2 * head, 2 * head)
        key_pair = key_out[0, :, pl.ds(start, 2 * head)]
        query_pair = query_t[pl.ds(start, 2 * head), :]
        for which in range(2):
            index = 2 * pair + which
            scores = dot_nn(key_pair, pick_rows(query_pair, which))
            scores = scores - slopes_ref[index] * dist_ref[...] + mask_ref[...]
            peak = jnp.max(scores, axis=0, keepdims=True)
            lifted = jnp.exp(scores - peak)
            total = jnp.sum(lifted, axis=0, keepdims=True)
            shares = lifted.astype(BF)
            rows = pl.ds(start + which * head, head)
            mixed = dot_nn(value_t[rows, :], shares)
            att_t[rows, :] = mixed * (1.0 / total)
            lse_out[0, pl.ds(index, 1), :] = peak + jnp.log(total)
        return carry

    lax.fori_loop(0, head_count // 2, pair_step, 0, unroll=True)
    attended = att_t[...].T.astype(BF)
    att_out[0] = attended
    rolling.need(2)
    total_one = residual + dot_nn(attended, weight_ref[3 * width : 4 * width])
    total_one_out[0] = total_one
    unit, _ = norm_parts(total_one)
    normed = unit * gains_ref[0:1] + gains_ref[1:2]
    normed_low = normed.astype(BF)
    rolling.need(3)
    rolling.need(4)
    total_two = normed
    for chunk in range(inner // width):
        inner_rows = pl.ds(4 * width + chunk * width, width)
        outer_rows = pl.ds(4 * width + inner + chunk * width, width)
        pre = dot_nt(normed_low, weight_ref[inner_rows, :])
        square = pre * pre
        bend = jnp.tanh(pre * (GELU_COEF + (GELU_COEF * GELU_CUBE) * square))
        half = 0.5 + 0.5 * bend
        hidden = (pre * half).astype(BF)
        steep = half + (0.5 * pre) * (1.0 - bend * bend) * (
            GELU_COEF + (3.0 * GELU_COEF * GELU_CUBE) * square
        )
        columns = pl.ds(chunk * width, width)
        hidden_out[0, :, columns] = hidden
        slope_out[0, :, columns] = steep.astype(BF)
        total_two = total_two + dot_nn(hidden, weight_ref[outer_rows, :])
    total_two_out[0] = total_two
    unit_two, _ = norm_parts(total_two)
    result = unit_two * gains_ref[2:3] + gains_ref[3:4]
    layer_out[0] = result.astype(layer_out.dtype)
    tick(1)


def layer_ahead(is_first, x, lengths, slopes, gains, weight_full, out_dtype, shard=None):
    batch, memory_length, width = x.shape
    queries = memory_length // 2 if is_first else memory_length
    keys = memory_length
    head_count = slopes.shape[0]
    rows = weight_full.shape[0]
    inner = (rows - 4 * width) // 2
    head_rows = -(-head_count // 8) * 8

    def block(length, size):
        return pl.BlockSpec((1, length, size), lambda i, *_: (i, 0, 0))

    def shape(length, size, dtype):
        return jax.ShapeDtypeStruct((batch, length, size), dtype)

    outs = [
        (queries, width, BF),
        (keys, width, BF),
        (keys, width, BF),
        (head_rows, queries, F32),
        (queries, width, BF),
        (queries, width, F32),
        (queries, inner, BF),
        (queries, inner, BF),
        (queries, width, F32),
        (queries, width, out_dtype),
        (queries, width, BF),
    ]
    flops = 2 * batch * width * (
        2 * queries * width + 2 * keys * width + 2 * queries * inner + 2 * queries * keys
    )
    hosted = shard is not None
    place = (lax.axis_size("fsdp") // 2, lax.axis_size("group")) if hosted else None
    anywhere = [pl.BlockSpec(memory_space=pl.ANY)] * hosted
    full_shape = [jax.ShapeDtypeStruct((rows, width), BF)] * hosted
    job_sems = gather_sems(*place) if hosted else []
    params = dict(collective_id=1, has_side_effects=True) if hosted else {}
    return pl.pallas_call(
        functools.partial(ahead_kernel, is_first, head_count, place),
        grid_spec=pltpu.PrefetchScalarGridSpec(
            num_scalar_prefetch=2,
            grid=(batch,),
            in_specs=[
                block(memory_length, width),
                pl.BlockSpec((4, width), lambda i, *_: (0, 0)),
                pl.BlockSpec(memory_space=pl.ANY),
            ]
            + anywhere,
            out_specs=[block(length, size) for length, size, _ in outs] + anywhere,
            scratch_shapes=[
                pltpu.VMEM((rows, width), BF),
                pltpu.VMEM((keys, queries), F32),
                pltpu.VMEM((keys, queries), F32),
                pltpu.VMEM((width, queries), BF),
                pltpu.VMEM((width, keys), BF),
                pltpu.VMEM((width, queries), F32),
                pltpu.SemaphoreType.DMA((5,)),
            ]
            + job_sems,
        ),
        out_shape=[shape(*out) for out in outs] + full_shape,
        compiler_params=pltpu.CompilerParams(vmem_limit_bytes=VMEM_LIMIT, **params),
        cost_estimate=pl.CostEstimate(
            flops=flops, bytes_accessed=rows * width * 2 + 30000000, transcendentals=0
        ),
        name="layer_ahead",
    )(lengths, slopes, x, gains, weight_full, *([shard] * hosted))


def back_kernel(
    is_first,
    head_count,
    place,
    query_steps,
    lengths_ref,
    slopes_ref,
    grad_ref,
    total_two_ref,
    total_one_ref,
    slope_ref,
    query_ref,
    key_ref,
    value_ref,
    att_ref,
    lse_ref,
    gains_ref,
    weight_hbm,
    *rest,
):
    if place is not None:
        grad_rows, rest = rest[0], rest[1:]
        landing, rest = rest[10:12], rest[:10] + rest[12:]
        job = rest[20:]
    (
        two_out,
        pre_out,
        normed_out,
        one_out,
        query_grad_out,
        key_grad_out,
        value_grad_out,
        input_out,
        gains_out,
        slopes_out,
        weight_ref,
        dist_ref,
        mask_ref,
        query_t,
        key_t,
        mixed_t,
        mixed_rows,
        delta_ref,
        query_grad_t,
        sems,
    ) = rest[:20]
    step = pl.program_id(0)
    if place is not None:
        spot = Spot(*place)
        engine = Reduce(
            spot,
            chunk_count(grad_rows.shape[0] // (2 * spot.chips)),
            grad_rows,
            landing[0],
            landing[1],
            job[0],
            job[1],
            job[2:],
        )

        early_ticks = engine.ticks - 1

        @pl.when(step == 0)
        def _():
            meet(spot)
            engine.start()
            engine.tick(0)

    pairs = head_count // 2
    sites = pairs + 2

    def reduce_ticks(site):
        if place is None:
            return
        total = sites * query_steps
        here = step * sites + site
        for index in range(-(-early_ticks // total)):
            tick = lax.div(here * early_ticks, total) + index + 1

            @pl.when(tick <= lax.div((here + 1) * early_ticks, total))
            def _():
                engine.tick(tick)

    width = weight_ref.shape[1]
    inner = (weight_ref.shape[0] - 4 * width) // 2
    queries, keys = query_ref.shape[1], key_ref.shape[1]
    head = width // head_count
    ranges = [
        (0, 3 * width),
        (3 * width, width),
        (4 * width, inner),
        (4 * width + inner, inner),
    ]
    copies = weight_copies(weight_hbm, weight_ref, sems, ranges)
    key_step = 1 if is_first else 2
    scale = float(head) ** (-0.5)

    @pl.when(step == 0)
    def _():
        for index in (3, 2, 1, 0):
            copies[index].start()
        fill_distance(dist_ref, key_step, 2)
        gains_out[...] = jnp.zeros_like(gains_out)
        slopes_out[...] = jnp.zeros_like(slopes_out)

    def need(index):
        @pl.when(step == 0)
        def _():
            copies[index].wait()

    fill_mask(mask_ref, key_step, lengths_ref[step])
    query_t[...] = (query_ref[0].astype(F32) * scale).T.astype(BF)
    key_t[...] = key_ref[0].astype(F32).T.astype(BF)

    grad = grad_ref[0].astype(F32)
    unit_two, inverse_two = norm_parts(total_two_ref[0])
    gains_out[2:3] += jnp.sum(grad * unit_two, axis=0, keepdims=True)
    gains_out[3:4] += jnp.sum(grad, axis=0, keepdims=True)
    back_two = norm_back(grad, unit_two, inverse_two, gains_ref[2:3])
    two_low = back_two.astype(BF)
    two_out[0] = two_low
    need(3)
    need(2)
    back_normed = back_two
    for chunk in range(inner // width):
        inner_rows = pl.ds(4 * width + chunk * width, width)
        outer_rows = pl.ds(4 * width + inner + chunk * width, width)
        columns = pl.ds(chunk * width, width)
        back_hidden = dot_nt(two_low, weight_ref[outer_rows, :])
        pre_grad = (back_hidden * slope_ref[0, :, columns].astype(F32)).astype(BF)
        pre_out[0, :, columns] = pre_grad
        back_normed = back_normed + dot_nn(pre_grad, weight_ref[inner_rows, :])
        if chunk % 2 == 1 and chunk < 4:
            reduce_ticks(chunk // 2)
    unit_one, inverse_one = norm_parts(total_one_ref[0])
    normed_out[0] = (unit_one * gains_ref[0:1] + gains_ref[1:2]).astype(BF)
    gains_out[0:1] += jnp.sum(back_normed * unit_one, axis=0, keepdims=True)
    gains_out[1:2] += jnp.sum(back_normed, axis=0, keepdims=True)
    back_one = norm_back(back_normed, unit_one, inverse_one, gains_ref[0:1])
    one_low = back_one.astype(BF)
    one_out[0] = one_low
    need(1)
    back_mixed = dot_nt(one_low, weight_ref[3 * width : 4 * width])
    mixed_low = back_mixed.astype(BF)
    mixed_rows[...] = mixed_low
    mixed_wide = mixed_low.astype(F32).T
    mixed_t[...] = mixed_wide.astype(BF)
    product = mixed_wide * att_ref[0].astype(F32).T
    delta_ref[...] = jnp.sum(product.reshape(head_count, head, queries), axis=1)

    def pair_step(pair, carry):
        start = pl.multiple_of(pair * 2 * head, 2 * head)
        lanes = pl.ds(start, 2 * head)
        key_pair = key_ref[0, :, lanes]
        value_pair = value_ref[0, :, lanes]
        query_pair = query_ref[0, :, lanes]
        mixed_pair = mixed_rows[:, lanes]
        query_pair_t = query_t[lanes, :]
        mixed_pair_t = mixed_t[lanes, :]
        key_grad = jnp.zeros((keys, 2 * head), F32)
        value_grad = jnp.zeros((keys, 2 * head), F32)
        for which in range(2):
            index = 2 * pair + which
            half = lane_half(2 * head, which)
            scores = dot_nn(key_pair, pick_rows(query_pair_t, which))
            scores = scores - slopes_ref[index] * dist_ref[...] + mask_ref[...]
            shares = jnp.exp(scores - lse_ref[0, pl.ds(index, 1), :])
            back_shares = dot_nn(value_pair, pick_rows(mixed_pair_t, which))
            back_scores = shares * (back_shares - delta_ref[pl.ds(index, 1), :])
            slopes_out[pl.ds(index, 1), :] += jnp.sum(
                back_scores * dist_ref[...], axis=0, keepdims=True
            )
            scores_low = back_scores.astype(BF)
            value_grad = value_grad + dot_nn(shares.astype(BF), mixed_pair * half)
            key_grad = key_grad + dot_nn(scores_low, query_pair * half)
            rows = pl.ds(start + which * head, head)
            query_grad_t[rows, :] = dot_nn(key_t[rows, :], scores_low)
        reduce_ticks(pair + 2)
        key_grad_out[0, :, lanes] = (key_grad * scale).astype(BF)
        value_grad_out[0, :, lanes] = value_grad.astype(BF)
        return carry

    lax.fori_loop(0, head_count // 2, pair_step, 0, unroll=True)
    query_grad = (query_grad_t[...] * scale).T.astype(BF)
    query_grad_out[0] = query_grad
    need(0)
    back_query = back_one + dot_nt(query_grad, weight_ref[0:width])
    back_memory = dot_nt(key_grad_out[0], weight_ref[width : 2 * width]) + dot_nt(
        value_grad_out[0], weight_ref[2 * width : 3 * width]
    )
    if is_first:
        spread = pair_matrix(queries, keys, 1.0, False)
        half_grad = back_query * 0.5
        upper = half_grad.astype(BF)
        lower = (half_grad - upper.astype(F32)).astype(BF)
        back_memory = back_memory + dot_nn(spread, upper) + dot_nn(spread, lower)
        input_out[0] = back_memory
    else:
        input_out[0] = back_query + back_memory
    if place is not None:

        @pl.when(step == pl.num_programs(0) - 1)
        def _():
            def late_tick(tick, carry):
                engine.tick(tick)
                return carry

            lax.fori_loop(early_ticks + 1, engine.ticks, late_tick, 0)
            for part in range(engine.count):
                engine.swap_copy(spot.chip, part).wait_recv()
                engine.settle(part)
            engine.drain()


def layer_back(is_first, grad, kept, lengths, slopes, gains, weight_full, grad_rows=None):
    (query_rows, key_rows, value_rows, lse, attended, total_one, steep, total_two) = kept
    batch, queries, width = query_rows.shape
    keys = key_rows.shape[1]
    head_count = slopes.shape[0]
    rows = weight_full.shape[0]
    inner = (rows - 4 * width) // 2
    head_rows = lse.shape[1]

    def block(length, size):
        return pl.BlockSpec((1, length, size), lambda i, *_: (i, 0, 0))

    def shape(length, size, dtype):
        return jax.ShapeDtypeStruct((batch, length, size), dtype)

    outs = [
        (queries, width, BF),
        (queries, inner, BF),
        (queries, width, BF),
        (queries, width, BF),
        (queries, width, BF),
        (keys, width, BF),
        (keys, width, BF),
        (keys, width, F32),
    ]
    flops = 2 * batch * width * (
        2 * queries * width + 2 * keys * width + 2 * queries * inner + 5 * queries * keys
    )
    hosted = grad_rows is not None
    place, job_scratch, lands, params = None, [], [], {}
    if hosted:
        place = (lax.axis_size("fsdp") // 2, lax.axis_size("group"))
        shard_rows = rows // (2 * place[0])
        job_scratch = reduce_scratch(place[0], shard_rows, width)
        lands = reduce_lands(place[0], shard_rows, width)
        params = dict(collective_id=2, has_side_effects=True)
    anywhere = pl.BlockSpec(memory_space=pl.ANY)
    return pl.pallas_call(
        functools.partial(back_kernel, is_first, head_count, place, batch),
        grid_spec=pltpu.PrefetchScalarGridSpec(
            num_scalar_prefetch=2,
            grid=(batch,),
            in_specs=[
                block(queries, width),
                block(queries, width),
                block(queries, width),
                block(queries, inner),
                block(queries, width),
                block(keys, width),
                block(keys, width),
                block(queries, width),
                block(head_rows, queries),
                pl.BlockSpec((4, width), lambda i, *_: (0, 0)),
                anywhere,
            ]
            + [anywhere] * hosted,
            out_specs=[block(length, size) for length, size, _ in outs]
            + [
                pl.BlockSpec((4, width), lambda i, *_: (0, 0)),
                pl.BlockSpec((head_rows, queries), lambda i, *_: (0, 0)),
            ]
            + [anywhere] * len(lands),
            scratch_shapes=[
                pltpu.VMEM((rows, width), BF),
                pltpu.VMEM((keys, queries), F32),
                pltpu.VMEM((keys, queries), F32),
                pltpu.VMEM((width, queries), BF),
                pltpu.VMEM((width, keys), BF),
                pltpu.VMEM((width, queries), BF),
                pltpu.VMEM((queries, width), BF),
                pltpu.VMEM((head_count, queries), F32),
                pltpu.VMEM((width, queries), F32),
                pltpu.SemaphoreType.DMA((4,)),
            ]
            + job_scratch,
        ),
        out_shape=[shape(*out) for out in outs]
        + [
            jax.ShapeDtypeStruct((4, width), F32),
            jax.ShapeDtypeStruct((head_rows, queries), F32),
        ]
        + lands,
        compiler_params=pltpu.CompilerParams(vmem_limit_bytes=VMEM_LIMIT, **params),
        cost_estimate=pl.CostEstimate(
            flops=flops, bytes_accessed=rows * width * 2 + 40000000, transcendentals=0
        ),
        name="layer_back",
    )(
        lengths,
        slopes,
        grad,
        total_two,
        total_one,
        steep,
        query_rows,
        key_rows,
        value_rows,
        attended,
        lse,
        gains,
        weight_full,
        *([grad_rows] * hosted),
    )


def last_kernel(
    head_count,
    lengths_ref,
    slopes_ref,
    x_ref,
    grad_ref,
    gains_ref,
    weight_hbm,
    layer_out,
    low_out,
    att_out,
    hidden_out,
    two_out,
    pre_out,
    normed_out,
    one_out,
    query_grad_out,
    key_grad_out,
    value_grad_out,
    back_out,
    gains_out,
    slopes_out,
    weight_ref,
    dist_ref,
    mask_ref,
    query_rows,
    key_rows,
    value_rows,
    query_t,
    key_t,
    value_t,
    att_t,
    shares_ref,
    steep_ref,
    mixed_rows,
    mixed_t,
    delta_ref,
    query_grad_t,
    sems,
):
    step = pl.program_id(0)
    width = weight_ref.shape[1]
    inner = (weight_ref.shape[0] - 4 * width) // 2
    chunks = inner // width
    length = low_out.shape[1]
    head = width // head_count
    scale = float(head) ** (-0.5)
    rolling = Rolling(
        weight_copies(weight_hbm, weight_ref, sems, feed_cuts(width, inner)), step == 0
    )

    @pl.when(step == 0)
    def _():
        rolling.start()
        fill_distance(dist_ref, 2, 2)
        gains_out[...] = jnp.zeros_like(gains_out)
        slopes_out[...] = jnp.zeros_like(slopes_out)

    fill_mask(mask_ref, 2, lengths_ref[step])
    residual = x_ref[0]
    low = residual.astype(BF)
    low_out[0] = low
    rolling.need(0)
    queries = dot_nn(low, weight_ref[0:width]).astype(BF)
    query_rows[...] = queries
    query_t[...] = (queries.astype(F32) * scale).T.astype(BF)
    rolling.need(1)
    keys = dot_nn(low, weight_ref[width : 2 * width]).astype(BF)
    key_rows[...] = keys
    key_t[...] = keys.astype(F32).T.astype(BF)
    values = dot_nn(low, weight_ref[2 * width : 3 * width]).astype(BF)
    value_rows[...] = values
    value_t[...] = values.astype(F32).T.astype(BF)

    def ahead_pair(pair, carry):
        start = pl.multiple_of(pair * 2 * head, 2 * head)
        key_pair = key_rows[:, pl.ds(start, 2 * head)]
        query_pair = query_t[pl.ds(start, 2 * head), :]
        for which in range(2):
            index = 2 * pair + which
            scores = dot_nn(key_pair, pick_rows(query_pair, which))
            scores = scores - slopes_ref[index] * dist_ref[...] + mask_ref[...]
            peak = jnp.max(scores, axis=0, keepdims=True)
            lifted = jnp.exp(scores - peak)
            total = jnp.sum(lifted, axis=0, keepdims=True)
            shares = lifted * (1.0 / total)
            shares_ref[index] = shares
            rows = pl.ds(start + which * head, head)
            att_t[rows, :] = dot_nn(value_t[rows, :], shares.astype(BF))
        return carry

    lax.fori_loop(0, head_count // 2, ahead_pair, 0, unroll=True)
    attended = att_t[...].T.astype(BF)
    att_out[0] = attended
    rolling.need(2)
    total_one = residual + dot_nn(attended, weight_ref[3 * width : 4 * width])
    unit_one, inverse_one = norm_parts(total_one)
    normed = unit_one * gains_ref[0:1] + gains_ref[1:2]
    normed_low = normed.astype(BF)
    normed_out[0] = normed_low
    rolling.need(3)
    rolling.need(4)
    total_two = normed
    for chunk in range(chunks):
        inner_rows = pl.ds(4 * width + chunk * width, width)
        outer_rows = pl.ds(4 * width + inner + chunk * width, width)
        pre = dot_nt(normed_low, weight_ref[inner_rows, :])
        square = pre * pre
        bend = jnp.tanh(pre * (GELU_COEF + (GELU_COEF * GELU_CUBE) * square))
        half = 0.5 + 0.5 * bend
        hidden = (pre * half).astype(BF)
        steep = half + (0.5 * pre) * (1.0 - bend * bend) * (
            GELU_COEF + (3.0 * GELU_COEF * GELU_CUBE) * square
        )
        columns = pl.ds(chunk * width, width)
        hidden_out[0, :, columns] = hidden
        steep_ref[:, columns] = steep.astype(BF)
        total_two = total_two + dot_nn(hidden, weight_ref[outer_rows, :])
    unit_two, inverse_two = norm_parts(total_two)
    layer_out[0] = (unit_two * gains_ref[2:3] + gains_ref[3:4]).astype(layer_out.dtype)

    grad = grad_ref[0].astype(F32)
    gains_out[2:3] += jnp.sum(grad * unit_two, axis=0, keepdims=True)
    gains_out[3:4] += jnp.sum(grad, axis=0, keepdims=True)
    back_two = norm_back(grad, unit_two, inverse_two, gains_ref[2:3])
    two_low = back_two.astype(BF)
    two_out[0] = two_low
    back_normed = back_two
    for chunk in range(chunks):
        inner_rows = pl.ds(4 * width + chunk * width, width)
        outer_rows = pl.ds(4 * width + inner + chunk * width, width)
        columns = pl.ds(chunk * width, width)
        back_hidden = dot_nt(two_low, weight_ref[outer_rows, :])
        pre_grad = (back_hidden * steep_ref[:, columns].astype(F32)).astype(BF)
        pre_out[0, :, columns] = pre_grad
        back_normed = back_normed + dot_nn(pre_grad, weight_ref[inner_rows, :])
    gains_out[0:1] += jnp.sum(back_normed * unit_one, axis=0, keepdims=True)
    gains_out[1:2] += jnp.sum(back_normed, axis=0, keepdims=True)
    back_one = norm_back(back_normed, unit_one, inverse_one, gains_ref[0:1])
    back_out[0] = back_one
    one_low = back_one.astype(BF)
    one_out[0] = one_low
    mixed_low = dot_nt(one_low, weight_ref[3 * width : 4 * width]).astype(BF)
    mixed_rows[...] = mixed_low
    mixed_wide = mixed_low.astype(F32).T
    mixed_t[...] = mixed_wide.astype(BF)
    delta_ref[...] = jnp.sum((mixed_wide * att_t[...]).reshape(head_count, head, length), axis=1)

    def back_pair(pair, carry):
        start = pl.multiple_of(pair * 2 * head, 2 * head)
        lanes = pl.ds(start, 2 * head)
        value_pair = value_rows[:, lanes]
        query_pair = query_rows[:, lanes]
        mixed_pair = mixed_rows[:, lanes]
        mixed_pair_t = mixed_t[lanes, :]
        key_grad = jnp.zeros((length, 2 * head), F32)
        value_grad = jnp.zeros((length, 2 * head), F32)
        for which in range(2):
            index = 2 * pair + which
            half = lane_half(2 * head, which)
            shares = shares_ref[index]
            back_shares = dot_nn(value_pair, pick_rows(mixed_pair_t, which))
            back_scores = shares * (back_shares - delta_ref[pl.ds(index, 1), :])
            slopes_out[pl.ds(index, 1), :] += jnp.sum(
                back_scores * dist_ref[...], axis=0, keepdims=True
            )
            scores_low = back_scores.astype(BF)
            value_grad = value_grad + dot_nn(shares.astype(BF), mixed_pair * half)
            key_grad = key_grad + dot_nn(scores_low, query_pair * half)
            rows = pl.ds(start + which * head, head)
            query_grad_t[rows, :] = dot_nn(key_t[rows, :], scores_low)
        key_grad_out[0, :, lanes] = (key_grad * scale).astype(BF)
        value_grad_out[0, :, lanes] = value_grad.astype(BF)
        return carry

    lax.fori_loop(0, head_count // 2, back_pair, 0, unroll=True)
    query_grad_out[0] = (query_grad_t[...] * scale).T.astype(BF)


def layer_last(x, grad, lengths, slopes, gains, weight_full):
    batch, length, width = x.shape
    head_count = slopes.shape[0]
    rows = weight_full.shape[0]
    inner = (rows - 4 * width) // 2
    head_rows = -(-head_count // 8) * 8

    def block(size):
        return pl.BlockSpec((1, length, size), lambda i, *_: (i, 0, 0))

    def shape(size, dtype):
        return jax.ShapeDtypeStruct((batch, length, size), dtype)

    outs = [(width, BF)] * 3 + [(inner, BF), (width, BF), (inner, BF)] + [(width, BF)] * 5
    outs = outs + [(width, F32)]
    fixed = [
        pl.BlockSpec((4, width), lambda i, *_: (0, 0)),
        pl.BlockSpec((head_rows, length), lambda i, *_: (0, 0)),
    ]
    return pl.pallas_call(
        functools.partial(last_kernel, head_count),
        grid_spec=pltpu.PrefetchScalarGridSpec(
            num_scalar_prefetch=2,
            grid=(batch,),
            in_specs=[block(width), block(width), fixed[0], pl.BlockSpec(memory_space=pl.ANY)],
            out_specs=[block(size) for size, _ in outs] + fixed,
            scratch_shapes=[
                pltpu.VMEM((rows, width), BF),
                pltpu.VMEM((length, length), F32),
                pltpu.VMEM((length, length), F32),
                pltpu.VMEM((length, width), BF),
                pltpu.VMEM((length, width), BF),
                pltpu.VMEM((length, width), BF),
                pltpu.VMEM((width, length), BF),
                pltpu.VMEM((width, length), BF),
                pltpu.VMEM((width, length), BF),
                pltpu.VMEM((width, length), F32),
                pltpu.VMEM((head_count, length, length), F32),
                pltpu.VMEM((length, inner), BF),
                pltpu.VMEM((length, width), BF),
                pltpu.VMEM((width, length), BF),
                pltpu.VMEM((head_count, length), F32),
                pltpu.VMEM((width, length), F32),
                pltpu.SemaphoreType.DMA((5,)),
            ],
        ),
        out_shape=[shape(size, dtype) for size, dtype in outs]
        + [
            jax.ShapeDtypeStruct((4, width), F32),
            jax.ShapeDtypeStruct((head_rows, length), F32),
        ],
        compiler_params=pltpu.CompilerParams(vmem_limit_bytes=VMEM_LIMIT),
        cost_estimate=pl.CostEstimate(
            flops=60000000000, bytes_accessed=80000000, transcendentals=0
        ),
        name="layer_last",
    )(lengths, slopes, x, grad, gains, weight_full)


def weight_product(left, right):
    return lax.dot_general(
        left, right, (((0, 1), (0, 1)), ((), ())), preferred_element_type=F32
    )


def matrix_gradient(query_low, memory_low, attended, hidden, back):
    (two_low, pre_grad, normed_low, one_low, query_grad, key_grad, value_grad) = back
    return jnp.concatenate(
        [
            weight_product(query_low, query_grad),
            weight_product(memory_low, key_grad),
            weight_product(memory_low, value_grad),
            weight_product(attended, one_low),
            weight_product(pre_grad, normed_low),
            weight_product(hidden, two_low),
        ],
        axis=0,
    )


def adam_step(master, gradient, first_mom, second_mom, rate):
    first_new = BETA_ONE * first_mom + (1.0 - BETA_ONE) * gradient
    second_new = BETA_TWO * second_mom + (1.0 - BETA_TWO) * gradient * gradient
    first_hat = first_new / (1.0 - BETA_ONE**STEP)
    second_hat = second_new / (1.0 - BETA_TWO**STEP)
    inner_move = rate * (first_hat / (jnp.sqrt(second_hat) + ADAM_EPS) + DECAY_RATE * master)
    return (first_new, second_new, inner_move)


def outer_step(master, moves_sum, momentum_old, group_count):
    mean_move = moves_sum / group_count
    momentum_new = MOMENTUM * momentum_old + mean_move
    return (mean_move, momentum_new, master - OUTER_RATE * (mean_move + MOMENTUM * momentum_new))


def shards(
    hidden_in,
    lengths,
    out_grad,
    weights,
    weight_m,
    weight_v,
    outer_mom,
    small,
    small_m,
    small_v,
    small_mom,
):
    width = weights.shape[2]
    part_size = small.shape[0] // 2
    masters_low = [weights[layer].astype(BF) for layer in range(2)]

    gains = []
    slopes = []
    for layer in range(2):
        part = small[layer * part_size : (layer + 1) * part_size]
        gains.append(part[: 4 * width].reshape(4, width))
        slopes.append(part[4 * width :])

    matrix_two = lax.all_gather(masters_low[1], "fsdp", axis=0, tiled=True)
    matrix_one = gather_rows(masters_low[0])
    (q1, k1, v1, lse1, att1, one1, hid1, steep1, two1, first_out, low1) = layer_ahead(
        True, hidden_in, lengths, slopes[0], gains[0], matrix_one, F32
    )
    (block_out, low2, att2, hid2, *back_two) = layer_last(
        first_out, out_grad, lengths, slopes[1], gains[1], matrix_two
    )
    matrix_grad_two = matrix_gradient(low2, low2, att2, hid2, back_two[:7]).astype(BF)
    rest_two, matrix_grad_two = lax.optimization_barrier(
        ((back_two[4], back_two[5], back_two[6], back_two[7]), matrix_grad_two)
    )
    first_grad = rest_two[3]
    for index in range(3):
        first_grad = first_grad + jnp.einsum(
            "btn,an->bta",
            rest_two[index],
            matrix_two[index * width : (index + 1) * width],
            preferred_element_type=F32,
        )
    shard_two = lax.psum_scatter(matrix_grad_two, "fsdp", scatter_dimension=0, tiled=True)
    back_one = layer_back(
        True,
        first_grad,
        (q1, k1, v1, lse1, att1, one1, steep1, two1),
        lengths,
        slopes[0],
        gains[0],
        matrix_one,
    )
    input_grad = back_one[7]
    matrix_grad_one = matrix_gradient(low1, hidden_in, att1, hid1, back_one[:7]).astype(BF)
    head_count = slopes[0].shape[0]
    small_parts = []
    for back in (back_one, back_two):
        small_parts += [back[8].reshape(-1), -jnp.sum(back[9][:head_count], axis=1)]
    grad_shard, weight_sum, small_grad, small_sum = finish(
        matrix_grad_one,
        shard_two,
        weights,
        weight_m,
        weight_v,
        jnp.concatenate(small_parts)[None],
        small[None],
        small_m,
        small_v,
    )[:4]
    weight_first, weight_second, _ = adam_step(
        weights, grad_shard[None].astype(F32), weight_m, weight_v, INNER_RATE
    )
    small_first, small_second, _ = adam_step(small, small_grad, small_m, small_v, SMALL_RATE)
    weight_sum, small_sum = weight_sum.astype(F32), small_sum[0]
    group_count = lax.axis_size("group")
    weight_mean, weight_mom, weight_new = outer_step(weights, weight_sum, outer_mom, group_count)
    small_mean, small_momentum, small_after = outer_step(small, small_sum, small_mom, group_count)
    return (
        block_out,
        input_grad,
        weight_new,
        weight_new.astype(BF),
        weight_first,
        weight_second,
        weight_mean,
        weight_mom,
        small_after,
        small_first,
        small_second,
        small_mean,
        small_momentum,
    )


def solution(mesh):
    in_specs = (
        P(("group", "fsdp"), None, None),
        P(("group", "fsdp")),
        P(("group", "fsdp"), None, None),
        P(None, "fsdp", None),
        P("group", None, "fsdp", None),
        P("group", None, "fsdp", None),
        P(None, "fsdp", None),
        P(),
        P("group", None),
        P("group", None),
        P(),
    )
    out_specs = (
        P(("group", "fsdp"), None, None),
        P(("group", "fsdp"), None, None),
        P(None, "fsdp", None),
        P(None, "fsdp", None),
        P("group", None, "fsdp", None),
        P("group", None, "fsdp", None),
        P(None, "fsdp", None),
        P(None, "fsdp", None),
        P(),
        P("group", None),
        P("group", None),
        P(),
        P(),
    )
    return jax.shard_map(shards, mesh=mesh, in_specs=in_specs, out_specs=out_specs, check_vma=False)
```

```python
import functools

import jax
import jax.numpy as jnp
from jax import lax
from jax.experimental import pallas as pl
from jax.experimental.pallas import tpu as pltpu
from jax.sharding import PartitionSpec as P

STEP = 10


EPS_NORM = 1e-06
MASK_FILL = -1e30
BETA_ONE = 0.9
BETA_TWO = 0.999
ADAM_EPS = 1e-08
DECAY_RATE = 0.01
INNER_RATE = 0.03
SMALL_RATE = 0.6
OUTER_RATE = 0.7
MOMENTUM = 0.9
GELU_COEF = 0.7978845608028654
GELU_CUBE = 0.044715

BF = jnp.bfloat16
F32 = jnp.float32
VMEM_LIMIT = 60 * 1024 * 1024
MESH_ID = pl.DeviceIdType.MESH


def dot_nn(left, right):
    return lax.dot_general(left, right, (((1,), (0,)), ((), ())), preferred_element_type=F32)


def dot_nt(left, right):
    return lax.dot_general(left, right, (((1,), (1,)), ((), ())), preferred_element_type=F32)


def dot_tn(left, right):
    return lax.dot_general(left, right, (((0,), (0,)), ((), ())), preferred_element_type=F32)


def norm_parts(total):
    center = total - jnp.mean(total, axis=-1, keepdims=True)
    inverse = lax.rsqrt(jnp.mean(center * center, axis=-1, keepdims=True) + EPS_NORM)
    return center * inverse, inverse


def norm_back(grad, unit, inverse, gain):
    scaled = grad * gain
    lead = jnp.mean(scaled, axis=-1, keepdims=True)
    along = jnp.mean(scaled * unit, axis=-1, keepdims=True)
    return inverse * (scaled - lead - unit * along)


def fill_distance(dist_ref, key_step, query_step):
    shape = dist_ref.shape
    keys = lax.broadcasted_iota(jnp.int32, shape, 0) * key_step
    queries = lax.broadcasted_iota(jnp.int32, shape, 1) * query_step
    dist_ref[...] = jnp.abs(queries - keys).astype(F32)


def fill_mask(mask_ref, key_step, length):
    keys = lax.broadcasted_iota(jnp.int32, mask_ref.shape, 0) * key_step
    mask_ref[...] = jnp.where(keys < length, 0.0, MASK_FILL)


def pick_rows(pair_rows, which):
    half = pair_rows.shape[0] // 2
    zero = jnp.zeros((half, pair_rows.shape[1]), pair_rows.dtype)
    if which == 0:
        return jnp.concatenate([pair_rows[:half], zero], axis=0)
    return jnp.concatenate([zero, pair_rows[half:]], axis=0)


def lane_half(width, which):
    lanes = lax.broadcasted_iota(jnp.int32, (1, width), 1)
    inside = lanes < width // 2 if which == 0 else lanes >= width // 2
    return jnp.where(inside, 1.0, 0.0).astype(BF)


def pair_matrix(queries, keys, value, by_query):
    shape = (queries, keys) if by_query else (keys, queries)
    query_index = lax.broadcasted_iota(jnp.int32, shape, 0 if by_query else 1)
    key_index = lax.broadcasted_iota(jnp.int32, shape, 1 if by_query else 0)
    offset = key_index - 2 * query_index
    return jnp.where((offset == 0) | (offset == 1), value, 0.0).astype(BF)


def remote(source, target, send_sem, recv_sem, device):
    return pltpu.make_async_remote_copy(
        src_ref=source,
        dst_ref=target,
        send_sem=send_sem,
        recv_sem=recv_sem,
        device_id=device,
        device_id_type=pl.DeviceIdType.MESH,
    )


class Spot:
    def __init__(self, chips, group_count):
        self.chips = chips
        self.group_count = group_count
        self.group = lax.axis_index("group")
        self.member = lax.axis_index("fsdp")
        self.chip = self.member // 2
        self.core = self.member % 2

    def line(self, chip):
        return {"fsdp": 2 * chip + self.core}

    def partner(self):
        return {"fsdp": 2 * self.chip + 1 - self.core}

    def other(self, turn):
        return {"group": lax.rem(self.group + turn, self.group_count)}

    def back_group(self, turn):
        return lax.rem(self.group + self.group_count - turn, self.group_count)

    def ahead_chip(self, hop):
        return lax.rem(self.chip + hop, self.chips)

    def back_chip(self, hop):
        return lax.rem(self.chip + self.chips - hop, self.chips)


def meet(spot):
    barrier = pltpu.get_barrier_semaphore()
    for hop in range(1, spot.chips):
        pl.semaphore_signal(
            barrier, inc=1, device_id=spot.line(spot.ahead_chip(hop)), device_id_type=MESH_ID
        )
    pl.semaphore_signal(barrier, inc=1, device_id=spot.partner(), device_id_type=MESH_ID)
    for turn in range(1, spot.group_count):
        pl.semaphore_signal(barrier, inc=1, device_id=spot.other(turn), device_id_type=MESH_ID)
    pl.semaphore_wait(barrier, spot.chips - 1 + 1 + spot.group_count - 1)


class Gather:
    def __init__(self, spot, shard_ref, full_ref, sems):
        self.spot = spot
        self.shard = shard_ref
        self.full = full_ref
        self.line_send, self.line_recv, self.cross_send, self.cross_recv = sems[:4]
        self.core_send, self.core_recv, self.own_sem = sems[4:]
        self.rows = shard_ref.shape[0]
        self.part = self.rows // spot.group_count
        self.last = spot.chips - 1

    def piece(self, chip, core, group):
        start = (2 * chip + core) * self.rows + group * self.part
        return self.full.at[pl.ds(start, self.part)]

    def whole(self, chip, core):
        return self.full.at[pl.ds((2 * chip + core) * self.rows, self.rows)]

    def line_own(self, side):
        spot = self.spot
        return remote(
            self.shard.at[pl.ds(spot.group * self.part, self.part)],
            self.piece(spot.chip, spot.core, spot.group),
            self.line_send.at[spot.chips + side],
            self.line_recv.at[spot.chip],
            spot.line(spot.chip + 1 - 2 * side),
        )

    def line_pass(self, source, chip):
        here = self.piece(source, self.spot.core, self.spot.group)
        return remote(
            here, here, self.line_send.at[source], self.line_recv.at[source], self.spot.line(chip)
        )

    def cross_copy(self, source, turn):
        here = self.piece(source, self.spot.core, self.spot.group)
        slot = source * self.spot.group_count + turn
        return remote(
            here, here, self.cross_send.at[slot], self.cross_recv.at[slot], self.spot.other(turn)
        )

    def cross_arrival(self, source, turn):
        here = self.piece(source, self.spot.core, self.spot.back_group(turn))
        slot = source * self.spot.group_count + turn
        return remote(
            here, here, self.cross_send.at[slot], self.cross_recv.at[slot], self.spot.partner()
        )

    def core_copy(self, source, turn):
        here = self.piece(source, self.spot.core, self.spot.back_group(turn))
        slot = source * self.spot.group_count + turn
        return remote(
            here, here, self.core_send.at[slot], self.core_recv.at[slot], self.spot.partner()
        )

    def core_arrival(self, source, turn):
        here = self.piece(source, 1 - self.spot.core, self.spot.back_group(turn))
        slot = source * self.spot.group_count + turn
        return remote(
            here, here, self.core_send.at[slot], self.core_recv.at[slot], self.spot.partner()
        )

    def core_own(self):
        slot = self.spot.chip * self.spot.group_count
        return remote(
            self.shard,
            self.whole(self.spot.chip, self.spot.core),
            self.core_send.at[slot],
            self.core_recv.at[slot],
            self.spot.partner(),
        )

    def core_own_arrival(self):
        slot = self.spot.chip * self.spot.group_count
        here = self.whole(self.spot.chip, 1 - self.spot.core)
        return remote(
            here, here, self.core_send.at[slot], self.core_recv.at[slot], self.spot.partner()
        )

    def own_copy(self):
        return pltpu.make_async_copy(
            self.shard, self.whole(self.spot.chip, self.spot.core), self.own_sem.at[0]
        )

    def each_side(self, distance, act):
        spot = self.spot
        for side in range(2):
            source = spot.chip - distance if side == 0 else spot.chip + distance
            target = spot.chip + 1 - 2 * side

            @pl.when((source >= 0) & (source <= self.last))
            def _():
                act(source, target, (target >= 0) & (target <= self.last))

    def start(self):
        spot = self.spot

        @pl.when(spot.chip < self.last)
        def _():
            self.line_own(0).start()

        @pl.when(spot.chip > 0)
        def _():
            self.line_own(1).start()

        self.core_own().start()
        self.own_copy().start()

    def line_stage(self, source, target, inside):
        self.line_pass(source, self.spot.chip).wait_recv()

        @pl.when(inside)
        def _():
            self.line_pass(source, target).start()

        for turn in range(1, self.spot.group_count):
            self.cross_copy(source, turn).start()
        self.core_copy(source, 0).start()

    def cross_stage(self, source, target, inside):
        for turn in range(1, self.spot.group_count):
            self.cross_arrival(source, turn).wait_recv()
            self.core_copy(source, turn).start()

    def end_stage(self, source, target, inside):
        @pl.when(inside)
        def _():
            self.line_pass(source, target).wait_send()

        for turn in range(self.spot.group_count):
            if turn > 0:
                self.cross_copy(source, turn).wait_send()
            self.core_copy(source, turn).wait_send()
            self.core_arrival(source, turn).wait_recv()

    def run(self):
        spot = self.spot
        self.start()
        for distance in range(1, spot.chips):
            self.each_side(distance, self.line_stage)
            if distance > 1:
                self.each_side(distance - 1, self.cross_stage)
        self.each_side(spot.chips - 1, self.cross_stage)
        for distance in range(1, spot.chips):
            self.each_side(distance, self.end_stage)
        self.own_copy().wait()
        self.core_own().wait_send()
        self.core_own_arrival().wait_recv()

        @pl.when(spot.chip < self.last)
        def _():
            self.line_own(0).wait_send()

        @pl.when(spot.chip > 0)
        def _():
            self.line_own(1).wait_send()


def gather_sems(chips, group_count):
    dma = pltpu.SemaphoreType.DMA
    crossing = (chips * group_count,)
    return [dma((chips + 2,)), dma((chips,))] + [dma(crossing)] * 4 + [dma((1,))]


def gather_kernel(chips, group_count, shard_ref, full_ref, *sems):
    spot = Spot(chips, group_count)
    meet(spot)
    Gather(spot, shard_ref, full_ref, sems).run()


def gather_rows(shard):
    members, group_count = lax.axis_size("fsdp"), lax.axis_size("group")
    rows, width = shard.shape
    return pl.pallas_call(
        functools.partial(gather_kernel, members // 2, group_count),
        out_shape=jax.ShapeDtypeStruct((rows * members, width), BF),
        in_specs=[pl.BlockSpec(memory_space=pl.ANY)],
        out_specs=pl.BlockSpec(memory_space=pl.ANY),
        scratch_shapes=gather_sems(members // 2, group_count),
        compiler_params=pltpu.CompilerParams(collective_id=0, has_side_effects=True),
        name="gather_rows",
    )(shard)


def chunk_count(rows):
    return max(
        count for count in range(1, 7) if rows % (32 * count) == 0
    )


class Reduce:
    def __init__(self, spot, count, grad, swap, lands, loads, sends, sems):
        self.spot = spot
        self.count = count
        self.grad = grad
        self.swap = swap
        self.lands = lands
        self.loads = loads
        self.sends = sends
        (self.load_sems, self.send_sems, self.recv_sems, self.swap_send, self.swap_recv) = sems
        self.last = spot.chips - 1
        self.rows = grad.shape[0] // (2 * spot.chips)
        self.piece = self.rows // count
        self.items = self.last * count
        self.ticks = self.items + self.last
        self.slots = sends.shape[1]

    def swap_copy(self, chip, part):
        spot = self.spot
        start = part * self.piece
        source = (2 * chip + 1 - spot.core) * self.rows + start
        return remote(
            self.grad.at[pl.ds(pl.multiple_of(source, 8), self.piece)],
            self.swap.at[pl.ds(pl.multiple_of(chip * self.rows + start, 8), self.piece)],
            self.swap_send.at[chip * self.count + part],
            self.swap_recv.at[chip * self.count + part],
            spot.partner(),
        )

    def start(self):
        for chip in range(self.last, -1, -1):
            for part in range(self.count - 1, -1, -1):
                self.swap_copy(chip, part).start()
        self.fetch(0)

    def own_rows(self, chip, part):
        start = (2 * chip + self.spot.core) * self.rows + part * self.piece
        return self.grad.at[pl.ds(pl.multiple_of(start, 8), self.piece)]

    def swap_rows(self, chip, part):
        start = chip * self.rows + part * self.piece
        return self.swap.at[pl.ds(pl.multiple_of(start, 8), self.piece)]

    def land_rows(self, way, item):
        start = (way * self.items + item) * self.piece
        return self.lands.at[pl.ds(pl.multiple_of(start, 8), self.piece)]

    def plan(self, way, tick):
        spot, count, last = self.spot, self.count, self.last
        distance = spot.chip + way * (last - 2 * spot.chip)
        item = tick - distance
        raised = item + count * spot.chips
        chip = last - way - (lax.div(raised, count) - spot.chips)
        part = count - 1 - lax.rem(raised, count)
        inside = (item >= 0) & (item < self.items)
        ahead = (1 - 2 * way) * (chip - spot.chip)
        passes = inside & (ahead > 0)
        takes = distance > 0
        return item, chip, part, passes, takes

    def near_loads(self, way, tick, chip, part):
        turn = lax.rem(tick, 2)
        return [
            pltpu.make_async_copy(
                source,
                self.loads.at[way, 2 * turn + which],
                self.load_sems.at[way * 5 + 2 * turn + which],
            )
            for which, source in enumerate((self.own_rows(chip, part), self.swap_rows(chip, part)))
        ]

    def land_load(self, way, item):
        return pltpu.make_async_copy(
            self.land_rows(way, item), self.loads.at[way, 4], self.load_sems.at[way * 5 + 4]
        )

    def fetch(self, tick):
        for way in range(2):
            item, chip, part, passes, takes = self.plan(way, tick)

            @pl.when(passes)
            def _():
                self.swap_copy(chip, part).wait_recv()
                for copy in self.near_loads(way, tick, chip, part):
                    copy.start()

    def hop(self, way, item):
        spot = self.spot
        return remote(
            self.sends.at[way, lax.rem(item, self.slots)],
            self.land_rows(way, item),
            self.send_sems.at[way * self.items + item],
            self.recv_sems.at[way * self.items + item],
            spot.line(spot.chip + 1 - 2 * way),
        )

    def arrival(self, way, item):
        here = self.land_rows(way, item)
        sem = way * self.items + item
        return remote(
            here, here, self.send_sems.at[sem], self.recv_sems.at[sem], self.spot.partner()
        )

    def tick(self, tick):
        spot = self.spot
        nearer = jnp.where(2 * spot.chip > self.last, 1, 0)
        for turn in range(2):
            way = nearer if turn == 0 else 1 - nearer
            item, chip, part, passes, takes = self.plan(way, tick)

            @pl.when(passes)
            def _():
                @pl.when(takes)
                def _():
                    self.arrival(way, item).wait_recv()
                    self.land_load(way, item).start()

                slot = lax.rem(item, self.slots)
                first = way * (self.last - spot.chip) * self.count

                @pl.when(item - first >= self.slots)
                def _():
                    self.hop(way, item - self.slots).wait_send()

                for copy in self.near_loads(way, tick, chip, part):
                    copy.wait()

                @pl.when(takes)
                def _():
                    self.land_load(way, item).wait()
                    self.add(way, tick, slot, True)

                @pl.when(jnp.logical_not(takes))
                def _():
                    self.add(way, tick, slot, False)

                self.hop(way, item).start()

        self.fetch(tick + 1)

    def settle(self, order):
        spot = self.spot

        @pl.when(spot.chip > 0)
        def _():
            self.arrival(0, (self.last - spot.chip) * self.count + order).wait_recv()

        @pl.when(spot.chip < self.last)
        def _():
            self.arrival(1, (self.last - 1 - spot.chip) * self.count + order).wait_recv()

    def add(self, way, tick, slot, landed):
        block = 32
        near = 2 * lax.rem(tick, 2)

        def step(index, carry):
            rows = pl.ds(pl.multiple_of(index * block, block), block)
            total = self.loads[way, near, rows, :].astype(F32)
            total = total + self.loads[way, near + 1, rows, :].astype(F32)
            if landed:
                total = total + self.loads[way, 4, rows, :].astype(F32)
            self.sends[way, slot, rows, :] = total.astype(BF)
            return carry

        lax.fori_loop(0, self.piece // block, step, 0)

    def drain(self):
        spot = self.spot
        for way in range(2):
            begin = 0 if way == 0 else (self.last - spot.chip) * self.count
            end = (self.last - spot.chip) * self.count if way == 0 else self.items
            for back in range(1, self.slots + 1):

                @pl.when(end - back >= begin)
                def _():
                    self.hop(way, end - back).wait_send()

        for chip in range(spot.chips):
            for part in range(self.count):
                self.swap_copy(chip, part).wait_send()


def reduce_scratch(chips, rows, width):
    count = chunk_count(rows)
    dma = pltpu.SemaphoreType.DMA
    items = (chips - 1) * count
    return [
        pltpu.VMEM((2, 5, rows // count, width), BF),
        pltpu.VMEM((2, 4, rows // count, width), BF),
        dma((10,)),
        dma((2 * items,)),
        dma((2 * items,)),
        dma((chips * count,)),
        dma((chips * count,)),
    ]


def reduce_lands(chips, rows, width):
    return [
        jax.ShapeDtypeStruct((chips * rows, width), BF),
        jax.ShapeDtypeStruct((2 * (chips - 1) * rows, width), BF),
    ]


def move_of(master, gradient, first_mom, second_mom, rate):
    return adam_step(master, gradient, first_mom, second_mom, rate)[2]


def finish_kernel(
    chips,
    group_count,
    grad_zero,
    shard_one,
    weight_hbm,
    first_hbm,
    second_hbm,
    small_grad,
    small_ref,
    small_first,
    small_second,
    grad_out,
    sum_out,
    small_grad_out,
    small_sum_out,
    swap_zero,
    lands_zero,
    parts,
    states,
    grads,
    moves,
    quarters,
    sums,
    small_land,
    small_moves,
    small_move,
    part_sems,
    state_sems,
    grad_sems,
    cross_send,
    cross_recv,
    share_send,
    share_recv,
    share_own,
    small_send,
    small_recv,
    small_cross_send,
    small_cross_recv,
    *engine_scratch,
):
    tick = pl.program_id(0)
    spot = Spot(chips, group_count)
    rows = sum_out.shape[1]
    count = moves.shape[1]
    piece = rows // count
    quarter = piece // group_count
    engine = Reduce(
        spot,
        count,
        grad_zero,
        swap_zero,
        lands_zero,
        engine_scratch[0],
        engine_scratch[1],
        engine_scratch[2:],
    )
    members = 2 * chips
    last = chips - 1

    def small_send_copy(hop):
        target = lax.rem(spot.member + hop, members)
        return remote(
            small_grad,
            small_land.at[spot.member],
            small_send.at[hop],
            small_recv.at[hop],
            {"fsdp": target},
        )

    def small_cross_copy(turn):
        return remote(
            small_move,
            small_moves.at[spot.group],
            small_cross_send.at[turn],
            small_cross_recv.at[turn],
            spot.other(turn),
        )

    @pl.when(tick == 0)
    def _():
        barrier = pltpu.get_barrier_semaphore()
        for hop in range(1, members):
            pl.semaphore_signal(
                barrier,
                inc=1,
                device_id={"fsdp": lax.rem(spot.member + hop, members)},
                device_id_type=MESH_ID,
            )
        for turn in range(1, group_count):
            pl.semaphore_signal(barrier, inc=1, device_id=spot.other(turn), device_id_type=MESH_ID)
        pl.semaphore_wait(barrier, members - 1 + group_count - 1)
        engine.start()
        for hop in range(1, members):
            small_send_copy(hop).start()
        parts[...] = jnp.zeros_like(parts)

    bases = (engine.ticks - count, 1)

    def part_loads(layer, order):
        part, slot = count - 1 - order, lax.rem(order, 2)
        here = pl.multiple_of(part * piece, 8)
        start = (2 * spot.chip + spot.core) * rows + here
        sources = (shard_one.at[pl.ds(here, piece)],) if layer == 1 else (
            grad_zero.at[pl.ds(pl.multiple_of(start, 8), piece)],
            swap_zero.at[pl.ds(pl.multiple_of(spot.chip * rows + here, 8), piece)],
            lands_zero.at[
                pl.ds(pl.multiple_of(((last - spot.chip) * count + order) * piece, 8), piece)
            ],
            lands_zero.at[
                pl.ds(
                    pl.multiple_of(
                        ((2 * last - 1 - spot.chip) * count + order) * piece, 8
                    ),
                    piece,
                )
            ],
        )
        return [
            pltpu.make_async_copy(
                source,
                parts.at[layer, slot, which],
                part_sems.at[(2 * layer + slot) * 4 + which],
            )
            for which, source in enumerate(sources)
        ]

    def state_loads(layer, order):
        part, slot = count - 1 - order, lax.rem(order, 2)
        window = pl.ds(pl.multiple_of(part * piece, 8), piece)
        sources = (
            weight_hbm.at[layer, window],
            first_hbm.at[0, layer, window],
            second_hbm.at[0, layer, window],
        )
        return [
            pltpu.make_async_copy(
                source,
                states.at[layer, slot, which],
                state_sems.at[(2 * layer + slot) * 3 + which],
            )
            for which, source in enumerate(sources)
        ]

    def each_near(layer, order, act):
        copies = part_loads(layer, order)
        for copy in copies[:2]:
            act(copy)

    def each_landed(layer, order, act):
        if layer == 1:
            return
        copies = part_loads(layer, order)

        @pl.when(spot.chip > 0)
        def _():
            act(copies[2])

        @pl.when(spot.chip < last)
        def _():
            act(copies[3])

    def grad_store(layer, order):
        part = count - 1 - order
        return pltpu.make_async_copy(
            grads.at[layer, part],
            grad_out.at[layer, pl.ds(pl.multiple_of(part * piece, 8), piece)],
            grad_sems.at[layer * count + part],
        )

    def cross_copy(layer, order, turn):
        part = count - 1 - order
        target = lax.rem(spot.group + turn, group_count)
        sem = (layer * count + part) * group_count + turn
        return remote(
            moves.at[layer, part, pl.ds(pl.multiple_of(target * quarter, 8), quarter)],
            quarters.at[layer, part, turn],
            cross_send.at[sem],
            cross_recv.at[sem],
            spot.other(turn),
        )

    def share_rows(layer, part, group):
        start = pl.multiple_of(part * piece + group * quarter, 8)
        return sum_out.at[layer, pl.ds(start, quarter)]

    def share_copy(layer, order, turn):
        part = count - 1 - order
        sem = (layer * count + part) * group_count + turn
        return remote(
            sums.at[layer, part],
            share_rows(layer, part, spot.group),
            share_send.at[sem],
            share_recv.at[sem],
            spot.other(turn),
        )

    def share_local(layer, order):
        part = count - 1 - order
        return pltpu.make_async_copy(
            sums.at[layer, part],
            share_rows(layer, part, spot.group),
            share_own.at[layer * count + part],
        )

    def prepare(tick):
        for layer in range(2):
            order = tick - bases[layer]

            @pl.when((order >= 0) & (order < count))
            def _():
                if layer == 0:
                    engine.swap_copy(spot.chip, count - 1 - order).wait_recv()
                each_near(layer, order, lambda copy: copy.start())
                for copy in state_loads(layer, order):
                    copy.start()

    engine.tick(tick)
    prepare(tick + 1)
    landed = tick - bases[0]

    @pl.when((landed >= 0) & (landed < count))
    def _():
        engine.settle(landed)
        each_landed(0, landed, lambda copy: copy.start())

    for layer in range(2):
        later = tick - bases[layer] - 1

        @pl.when((later >= 0) & (later < count))
        def _():
            part = count - 1 - later
            for turn in range(1, group_count):
                cross_copy(layer, later, turn).wait_recv()
            total = moves[
                layer, part, pl.ds(pl.multiple_of(spot.group * quarter, 8), quarter), :
            ].astype(F32)
            for turn in range(1, group_count):
                total = total + quarters[layer, part, turn].astype(F32)
            sums[layer, part] = total.astype(sums.dtype)
            for turn in range(1, group_count):
                share_copy(layer, later, turn).start()
            share_local(layer, later).start()

        order = tick - bases[layer]

        @pl.when((order >= 0) & (order < count))
        def _():
            part, slot = count - 1 - order, lax.rem(order, 2)
            each_near(layer, order, lambda copy: copy.wait())
            each_landed(layer, order, lambda copy: copy.wait())
            for copy in state_loads(layer, order):
                copy.wait()

            def step(index, carry):
                window = pl.ds(pl.multiple_of(index * 32, 32), 32)
                total = parts[layer, slot, 0, window, :].astype(F32)
                for which in range(1, 4):
                    total = total + parts[layer, slot, which, window, :].astype(F32)
                low = total.astype(BF)
                grads[layer, part, window, :] = low
                move = move_of(
                    states[layer, slot, 0, window, :],
                    low.astype(F32),
                    states[layer, slot, 1, window, :],
                    states[layer, slot, 2, window, :],
                    INNER_RATE,
                )
                moves[layer, part, window, :] = move.astype(moves.dtype)
                return carry

            lax.fori_loop(0, piece // 32, step, 0)
            for turn in range(1, group_count):
                cross_copy(layer, order, turn).start()
            grad_store(layer, order).start()

    @pl.when(tick == 2)
    def _():
        small_land[spot.member] = small_grad[...]
        for hop in range(1, members):
            small_send_copy(hop).wait_recv()
        total = small_land[0]
        for member in range(1, members):
            total = total + small_land[member]
        small_grad_out[...] = total
        move = move_of(small_ref[...], total, small_first[...], small_second[...], SMALL_RATE)
        small_move[...] = move
        small_moves[spot.group] = move
        for turn in range(1, group_count):
            small_cross_copy(turn).start()

    @pl.when(tick == 4)
    def _():
        for turn in range(1, group_count):
            small_cross_copy(turn).wait_recv()
        total = small_moves[0]
        for group in range(1, group_count):
            total = total + small_moves[group]
        small_sum_out[...] = total

    @pl.when(tick == pl.num_programs(0) - 1)
    def _():
        engine.drain()
        for hop in range(1, members):
            small_send_copy(hop).wait_send()
        for turn in range(1, group_count):
            small_cross_copy(turn).wait_send()
        for layer in range(2):
            for order in range(count):
                grad_store(layer, order).wait()
                share_local(layer, order).wait()
                for turn in range(1, group_count):
                    cross_copy(layer, order, turn).wait_send()
                    share_copy(layer, order, turn).wait_send()
                    share_copy(layer, order, turn).wait_recv()


def finish(grad_zero, shard_one, weights, weight_m, weight_v, small_grad, small, small_m, small_v):
    members, group_count = lax.axis_size("fsdp"), lax.axis_size("group")
    chips = members // 2
    layers, rows, width = weights.shape
    count = chunk_count(rows)
    piece = rows // count
    quarter = piece // group_count
    wire = BF if quarter % 16 == 0 else F32
    small_size = small.shape[1]
    dma = pltpu.SemaphoreType.DMA
    ticks = (chips - 1) * count + chips - 1 + 1
    anywhere = pl.BlockSpec(memory_space=pl.ANY)
    local = pl.BlockSpec(memory_space=pltpu.VMEM)
    crossing = dma((layers * count * group_count,))
    return pl.pallas_call(
        functools.partial(finish_kernel, chips, group_count),
        grid=(ticks,),
        in_specs=[anywhere] * 5 + [local] * 4,
        out_specs=[anywhere, anywhere, local, local] + [anywhere] * 2,
        out_shape=[
            jax.ShapeDtypeStruct((layers, rows, width), BF),
            jax.ShapeDtypeStruct((layers, rows, width), wire),
            jax.ShapeDtypeStruct((1, small_size), F32),
            jax.ShapeDtypeStruct((1, small_size), F32),
        ]
        + reduce_lands(chips, rows, width),
        scratch_shapes=[
            pltpu.VMEM((layers, 2, 4, piece, width), BF),
            pltpu.VMEM((layers, 2, 3, piece, width), F32),
            pltpu.VMEM((layers, count, piece, width), BF),
            pltpu.VMEM((layers, count, piece, width), wire),
            pltpu.VMEM((layers, count, group_count, quarter, width), wire),
            pltpu.VMEM((layers, count, quarter, width), wire),
            pltpu.VMEM((members, 1, small_size), F32),
            pltpu.VMEM((group_count, 1, small_size), F32),
            pltpu.VMEM((1, small_size), F32),
            dma((8 * layers,)),
            dma((6 * layers,)),
            dma((layers * count,)),
            crossing,
            crossing,
            crossing,
            crossing,
            dma((layers * count,)),
            dma((members,)),
            dma((members,)),
            dma((group_count,)),
            dma((group_count,)),
        ]
        + reduce_scratch(chips, rows, width),
        compiler_params=pltpu.CompilerParams(
            vmem_limit_bytes=VMEM_LIMIT, collective_id=3, has_side_effects=True
        ),
        name="finish",
    )(grad_zero, shard_one, weights, weight_m, weight_v, small_grad, small, small_m, small_v)


def weight_copies(weight_hbm, weight_ref, sems, ranges):
    return [
        pltpu.make_async_copy(
            weight_hbm.at[pl.ds(start, size)], weight_ref.at[pl.ds(start, size)], sems.at[index]
        )
        for index, (start, size) in enumerate(ranges)
    ]


class Rolling:
    def __init__(self, copies, active, depth=2):
        self.copies = copies
        self.active = active
        self.depth = depth

    def start(self):
        for copy in self.copies[: self.depth]:
            copy.start()

    def need(self, index):
        @pl.when(self.active)
        def _():
            self.copies[index].wait()
            if index + self.depth < len(self.copies):
                self.copies[index + self.depth].start()


def feed_cuts(width, inner):
    ranges = [(0, width), (width, 2 * width), (3 * width, width)]
    return ranges + [(4 * width, inner), (4 * width + inner, inner)]


def ahead_kernel(
    is_first,
    head_count,
    place,
    lengths_ref,
    slopes_ref,
    x_ref,
    gains_ref,
    weight_hbm,
    *rest,
):
    if place is not None:
        shard_ref, rest = rest[0], rest[1:]
        full_ref, rest = rest[11], rest[:11] + rest[12:]
        job_sems = rest[18:]
    (
        query_out,
    key_out,
    value_out,
    lse_out,
    att_out,
    total_one_out,
    hidden_out,
    slope_out,
    total_two_out,
    layer_out,
    low_out,
    weight_ref,
    dist_ref,
    mask_ref,
    query_t,
    value_t,
    att_t,
    sems,
    ) = rest[:18]
    step = pl.program_id(0)
    if place is not None:
        spot = Spot(*place)
        job = Gather(spot, shard_ref, full_ref, job_sems)
        spread = [round(index * 7 / (job.tick_count - 1)) for index in range(job.tick_count)]

    def tick(quarter):
        if place is None:
            return
        for index in range(job.tick_count):
            if spread[index] % 2 == quarter:

                @pl.when(step == spread[index] // 2)
                def _():
                    if index == 0:
                        meet(spot)
                    job.tick(index)

    tick(0)
    width = weight_ref.shape[1]
    inner = (weight_ref.shape[0] - 4 * width) // 2
    queries, keys = query_out.shape[1], key_out.shape[1]
    head = width // head_count
    copies = weight_copies(weight_hbm, weight_ref, sems, feed_cuts(width, inner))
    rolling = Rolling(copies, step == 0)
    key_step = 1 if is_first else 2

    @pl.when(step == 0)
    def _():
        rolling.start()
        fill_distance(dist_ref, key_step, 2)

    fill_mask(mask_ref, key_step, lengths_ref[step])
    if is_first:
        memory_low = x_ref[0]
        residual = dot_nn(pair_matrix(queries, keys, 0.5, True), memory_low)
        query_low = residual.astype(BF)
    else:
        residual = x_ref[0]
        query_low = residual.astype(BF)
        memory_low = query_low
    low_out[0] = query_low
    rolling.need(0)
    query_rows = dot_nn(query_low, weight_ref[0:width]).astype(BF)
    query_out[0] = query_rows
    query_t[...] = (query_rows.astype(F32) * float(head) ** (-0.5)).T.astype(BF)
    rolling.need(1)
    key_out[0] = dot_nn(memory_low, weight_ref[width : 2 * width]).astype(BF)
    value_rows = dot_nn(memory_low, weight_ref[2 * width : 3 * width]).astype(BF)
    value_out[0] = value_rows
    value_t[...] = value_rows.astype(F32).T.astype(BF)

    def pair_step(pair, carry):
        start = pl.multiple_of(pair * 2 * head, 2 * head)
        key_pair = key_out[0, :, pl.ds(start, 2 * head)]
        query_pair = query_t[pl.ds(start, 2 * head), :]
        for which in range(2):
            index = 2 * pair + which
            scores = dot_nn(key_pair, pick_rows(query_pair, which))
            scores = scores - slopes_ref[index] * dist_ref[...] + mask_ref[...]
            peak = jnp.max(scores, axis=0, keepdims=True)
            lifted = jnp.exp(scores - peak)
            total = jnp.sum(lifted, axis=0, keepdims=True)
            shares = lifted.astype(BF)
            rows = pl.ds(start + which * head, head)
            mixed = dot_nn(value_t[rows, :], shares)
            att_t[rows, :] = mixed * (1.0 / total)
            lse_out[0, pl.ds(index, 1), :] = peak + jnp.log(total)
        return carry

    lax.fori_loop(0, head_count // 2, pair_step, 0, unroll=True)
    attended = att_t[...].T.astype(BF)
    att_out[0] = attended
    rolling.need(2)
    total_one = residual + dot_nn(attended, weight_ref[3 * width : 4 * width])
    total_one_out[0] = total_one
    unit, _ = norm_parts(total_one)
    normed = unit * gains_ref[0:1] + gains_ref[1:2]
    normed_low = normed.astype(BF)
    rolling.need(3)
    rolling.need(4)
    total_two = normed
    for chunk in range(inner // width):
        inner_rows = pl.ds(4 * width + chunk * width, width)
        outer_rows = pl.ds(4 * width + inner + chunk * width, width)
        pre = dot_nt(normed_low, weight_ref[inner_rows, :])
        square = pre * pre
        bend = jnp.tanh(pre * (GELU_COEF + (GELU_COEF * GELU_CUBE) * square))
        half = 0.5 + 0.5 * bend
        hidden = (pre * half).astype(BF)
        steep = half + (0.5 * pre) * (1.0 - bend * bend) * (
            GELU_COEF + (3.0 * GELU_COEF * GELU_CUBE) * square
        )
        columns = pl.ds(chunk * width, width)
        hidden_out[0, :, columns] = hidden
        slope_out[0, :, columns] = steep.astype(BF)
        total_two = total_two + dot_nn(hidden, weight_ref[outer_rows, :])
    total_two_out[0] = total_two
    unit_two, _ = norm_parts(total_two)
    result = unit_two * gains_ref[2:3] + gains_ref[3:4]
    layer_out[0] = result.astype(layer_out.dtype)
    tick(1)


def layer_ahead(is_first, x, lengths, slopes, gains, weight_full, out_dtype, shard=None):
    batch, memory_length, width = x.shape
    queries = memory_length // 2 if is_first else memory_length
    keys = memory_length
    head_count = slopes.shape[0]
    rows = weight_full.shape[0]
    inner = (rows - 4 * width) // 2
    head_rows = -(-head_count // 8) * 8

    def block(length, size):
        return pl.BlockSpec((1, length, size), lambda i, *_: (i, 0, 0))

    def shape(length, size, dtype):
        return jax.ShapeDtypeStruct((batch, length, size), dtype)

    outs = [
        (queries, width, BF),
        (keys, width, BF),
        (keys, width, BF),
        (head_rows, queries, F32),
        (queries, width, BF),
        (queries, width, F32),
        (queries, inner, BF),
        (queries, inner, BF),
        (queries, width, F32),
        (queries, width, out_dtype),
        (queries, width, BF),
    ]
    flops = 2 * batch * width * (
        2 * queries * width + 2 * keys * width + 2 * queries * inner + 2 * queries * keys
    )
    hosted = shard is not None
    place = (lax.axis_size("fsdp") // 2, lax.axis_size("group")) if hosted else None
    anywhere = [pl.BlockSpec(memory_space=pl.ANY)] * hosted
    full_shape = [jax.ShapeDtypeStruct((rows, width), BF)] * hosted
    job_sems = gather_sems(*place) if hosted else []
    params = dict(collective_id=1, has_side_effects=True) if hosted else {}
    return pl.pallas_call(
        functools.partial(ahead_kernel, is_first, head_count, place),
        grid_spec=pltpu.PrefetchScalarGridSpec(
            num_scalar_prefetch=2,
            grid=(batch,),
            in_specs=[
                block(memory_length, width),
                pl.BlockSpec((4, width), lambda i, *_: (0, 0)),
                pl.BlockSpec(memory_space=pl.ANY),
            ]
            + anywhere,
            out_specs=[block(length, size) for length, size, _ in outs] + anywhere,
            scratch_shapes=[
                pltpu.VMEM((rows, width), BF),
                pltpu.VMEM((keys, queries), F32),
                pltpu.VMEM((keys, queries), F32),
                pltpu.VMEM((width, queries), BF),
                pltpu.VMEM((width, keys), BF),
                pltpu.VMEM((width, queries), F32),
                pltpu.SemaphoreType.DMA((5,)),
            ]
            + job_sems,
        ),
        out_shape=[shape(*out) for out in outs] + full_shape,
        compiler_params=pltpu.CompilerParams(vmem_limit_bytes=VMEM_LIMIT, **params),
        cost_estimate=pl.CostEstimate(
            flops=flops, bytes_accessed=rows * width * 2 + 30000000, transcendentals=0
        ),
        name="layer_ahead",
    )(lengths, slopes, x, gains, weight_full, *([shard] * hosted))


def back_kernel(
    is_first,
    head_count,
    place,
    query_steps,
    lengths_ref,
    slopes_ref,
    grad_ref,
    total_two_ref,
    total_one_ref,
    slope_ref,
    query_ref,
    key_ref,
    value_ref,
    att_ref,
    lse_ref,
    gains_ref,
    weight_hbm,
    *rest,
):
    if place is not None:
        grad_rows, rest = rest[0], rest[1:]
        landing, rest = rest[10:12], rest[:10] + rest[12:]
        job = rest[20:]
    (
        two_out,
        pre_out,
        normed_out,
        one_out,
        query_grad_out,
        key_grad_out,
        value_grad_out,
        input_out,
        gains_out,
        slopes_out,
        weight_ref,
        dist_ref,
        mask_ref,
        query_t,
        key_t,
        mixed_t,
        mixed_rows,
        delta_ref,
        query_grad_t,
        sems,
    ) = rest[:20]
    step = pl.program_id(0)
    if place is not None:
        spot = Spot(*place)
        engine = Reduce(
            spot,
            chunk_count(grad_rows.shape[0] // (2 * spot.chips)),
            grad_rows,
            landing[0],
            landing[1],
            job[0],
            job[1],
            job[2:],
        )

        early_ticks = engine.ticks - 1

        @pl.when(step == 0)
        def _():
            meet(spot)
            engine.start()
            engine.tick(0)

    pairs = head_count // 2
    sites = pairs + 2

    def reduce_ticks(site):
        if place is None:
            return
        total = sites * query_steps
        here = step * sites + site
        for index in range(-(-early_ticks // total)):
            tick = lax.div(here * early_ticks, total) + index + 1

            @pl.when(tick <= lax.div((here + 1) * early_ticks, total))
            def _():
                engine.tick(tick)

    width = weight_ref.shape[1]
    inner = (weight_ref.shape[0] - 4 * width) // 2
    queries, keys = query_ref.shape[1], key_ref.shape[1]
    head = width // head_count
    ranges = [
        (0, 3 * width),
        (3 * width, width),
        (4 * width, inner),
        (4 * width + inner, inner),
    ]
    copies = weight_copies(weight_hbm, weight_ref, sems, ranges)
    key_step = 1 if is_first else 2
    scale = float(head) ** (-0.5)

    @pl.when(step == 0)
    def _():
        for index in (3, 2, 1, 0):
            copies[index].start()
        fill_distance(dist_ref, key_step, 2)
        gains_out[...] = jnp.zeros_like(gains_out)
        slopes_out[...] = jnp.zeros_like(slopes_out)

    def need(index):
        @pl.when(step == 0)
        def _():
            copies[index].wait()

    fill_mask(mask_ref, key_step, lengths_ref[step])
    query_t[...] = (query_ref[0].astype(F32) * scale).T.astype(BF)
    key_t[...] = key_ref[0].astype(F32).T.astype(BF)

    grad = grad_ref[0].astype(F32)
    unit_two, inverse_two = norm_parts(total_two_ref[0])
    gains_out[2:3] += jnp.sum(grad * unit_two, axis=0, keepdims=True)
    gains_out[3:4] += jnp.sum(grad, axis=0, keepdims=True)
    back_two = norm_back(grad, unit_two, inverse_two, gains_ref[2:3])
    two_low = back_two.astype(BF)
    two_out[0] = two_low
    need(3)
    need(2)
    back_normed = back_two
    for chunk in range(inner // width):
        inner_rows = pl.ds(4 * width + chunk * width, width)
        outer_rows = pl.ds(4 * width + inner + chunk * width, width)
        columns = pl.ds(chunk * width, width)
        back_hidden = dot_nt(two_low, weight_ref[outer_rows, :])
        pre_grad = (back_hidden * slope_ref[0, :, columns].astype(F32)).astype(BF)
        pre_out[0, :, columns] = pre_grad
        back_normed = back_normed + dot_nn(pre_grad, weight_ref[inner_rows, :])
        if chunk % 2 == 1 and chunk < 4:
            reduce_ticks(chunk // 2)
    unit_one, inverse_one = norm_parts(total_one_ref[0])
    normed_out[0] = (unit_one * gains_ref[0:1] + gains_ref[1:2]).astype(BF)
    gains_out[0:1] += jnp.sum(back_normed * unit_one, axis=0, keepdims=True)
    gains_out[1:2] += jnp.sum(back_normed, axis=0, keepdims=True)
    back_one = norm_back(back_normed, unit_one, inverse_one, gains_ref[0:1])
    one_low = back_one.astype(BF)
    one_out[0] = one_low
    need(1)
    back_mixed = dot_nt(one_low, weight_ref[3 * width : 4 * width])
    mixed_low = back_mixed.astype(BF)
    mixed_rows[...] = mixed_low
    mixed_wide = mixed_low.astype(F32).T
    mixed_t[...] = mixed_wide.astype(BF)
    product = mixed_wide * att_ref[0].astype(F32).T
    delta_ref[...] = jnp.sum(product.reshape(head_count, head, queries), axis=1)

    def pair_step(pair, carry):
        start = pl.multiple_of(pair * 2 * head, 2 * head)
        lanes = pl.ds(start, 2 * head)
        key_pair = key_ref[0, :, lanes]
        value_pair = value_ref[0, :, lanes]
        query_pair = query_ref[0, :, lanes]
        mixed_pair = mixed_rows[:, lanes]
        query_pair_t = query_t[lanes, :]
        mixed_pair_t = mixed_t[lanes, :]
        key_grad = jnp.zeros((keys, 2 * head), F32)
        value_grad = jnp.zeros((keys, 2 * head), F32)
        for which in range(2):
            index = 2 * pair + which
            half = lane_half(2 * head, which)
            scores = dot_nn(key_pair, pick_rows(query_pair_t, which))
            scores = scores - slopes_ref[index] * dist_ref[...] + mask_ref[...]
            shares = jnp.exp(scores - lse_ref[0, pl.ds(index, 1), :])
            back_shares = dot_nn(value_pair, pick_rows(mixed_pair_t, which))
            back_scores = shares * (back_shares - delta_ref[pl.ds(index, 1), :])
            slopes_out[pl.ds(index, 1), :] += jnp.sum(
                back_scores * dist_ref[...], axis=0, keepdims=True
            )
            scores_low = back_scores.astype(BF)
            value_grad = value_grad + dot_nn(shares.astype(BF), mixed_pair * half)
            key_grad = key_grad + dot_nn(scores_low, query_pair * half)
            rows = pl.ds(start + which * head, head)
            query_grad_t[rows, :] = dot_nn(key_t[rows, :], scores_low)
        reduce_ticks(pair + 2)
        key_grad_out[0, :, lanes] = (key_grad * scale).astype(BF)
        value_grad_out[0, :, lanes] = value_grad.astype(BF)
        return carry

    lax.fori_loop(0, head_count // 2, pair_step, 0, unroll=True)
    query_grad = (query_grad_t[...] * scale).T.astype(BF)
    query_grad_out[0] = query_grad
    need(0)
    back_query = back_one + dot_nt(query_grad, weight_ref[0:width])
    back_memory = dot_nt(key_grad_out[0], weight_ref[width : 2 * width]) + dot_nt(
        value_grad_out[0], weight_ref[2 * width : 3 * width]
    )
    if is_first:
        spread = pair_matrix(queries, keys, 1.0, False)
        half_grad = back_query * 0.5
        upper = half_grad.astype(BF)
        lower = (half_grad - upper.astype(F32)).astype(BF)
        back_memory = back_memory + dot_nn(spread, upper) + dot_nn(spread, lower)
        input_out[0] = back_memory
    else:
        input_out[0] = back_query + back_memory
    if place is not None:

        @pl.when(step == pl.num_programs(0) - 1)
        def _():
            def late_tick(tick, carry):
                engine.tick(tick)
                return carry

            lax.fori_loop(early_ticks + 1, engine.ticks, late_tick, 0)
            for part in range(engine.count):
                engine.swap_copy(spot.chip, part).wait_recv()
                engine.settle(part)
            engine.drain()


def layer_back(is_first, grad, kept, lengths, slopes, gains, weight_full, grad_rows=None):
    (query_rows, key_rows, value_rows, lse, attended, total_one, steep, total_two) = kept
    batch, queries, width = query_rows.shape
    keys = key_rows.shape[1]
    head_count = slopes.shape[0]
    rows = weight_full.shape[0]
    inner = (rows - 4 * width) // 2
    head_rows = lse.shape[1]

    def block(length, size):
        return pl.BlockSpec((1, length, size), lambda i, *_: (i, 0, 0))

    def shape(length, size, dtype):
        return jax.ShapeDtypeStruct((batch, length, size), dtype)

    outs = [
        (queries, width, BF),
        (queries, inner, BF),
        (queries, width, BF),
        (queries, width, BF),
        (queries, width, BF),
        (keys, width, BF),
        (keys, width, BF),
        (keys, width, F32),
    ]
    flops = 2 * batch * width * (
        2 * queries * width + 2 * keys * width + 2 * queries * inner + 5 * queries * keys
    )
    hosted = grad_rows is not None
    place, job_scratch, lands, params = None, [], [], {}
    if hosted:
        place = (lax.axis_size("fsdp") // 2, lax.axis_size("group"))
        shard_rows = rows // (2 * place[0])
        job_scratch = reduce_scratch(place[0], shard_rows, width)
        lands = reduce_lands(place[0], shard_rows, width)
        params = dict(collective_id=2, has_side_effects=True)
    anywhere = pl.BlockSpec(memory_space=pl.ANY)
    return pl.pallas_call(
        functools.partial(back_kernel, is_first, head_count, place, batch),
        grid_spec=pltpu.PrefetchScalarGridSpec(
            num_scalar_prefetch=2,
            grid=(batch,),
            in_specs=[
                block(queries, width),
                block(queries, width),
                block(queries, width),
                block(queries, inner),
                block(queries, width),
                block(keys, width),
                block(keys, width),
                block(queries, width),
                block(head_rows, queries),
                pl.BlockSpec((4, width), lambda i, *_: (0, 0)),
                anywhere,
            ]
            + [anywhere] * hosted,
            out_specs=[block(length, size) for length, size, _ in outs]
            + [
                pl.BlockSpec((4, width), lambda i, *_: (0, 0)),
                pl.BlockSpec((head_rows, queries), lambda i, *_: (0, 0)),
            ]
            + [anywhere] * len(lands),
            scratch_shapes=[
                pltpu.VMEM((rows, width), BF),
                pltpu.VMEM((keys, queries), F32),
                pltpu.VMEM((keys, queries), F32),
                pltpu.VMEM((width, queries), BF),
                pltpu.VMEM((width, keys), BF),
                pltpu.VMEM((width, queries), BF),
                pltpu.VMEM((queries, width), BF),
                pltpu.VMEM((head_count, queries), F32),
                pltpu.VMEM((width, queries), F32),
                pltpu.SemaphoreType.DMA((4,)),
            ]
            + job_scratch,
        ),
        out_shape=[shape(*out) for out in outs]
        + [
            jax.ShapeDtypeStruct((4, width), F32),
            jax.ShapeDtypeStruct((head_rows, queries), F32),
        ]
        + lands,
        compiler_params=pltpu.CompilerParams(vmem_limit_bytes=VMEM_LIMIT, **params),
        cost_estimate=pl.CostEstimate(
            flops=flops, bytes_accessed=rows * width * 2 + 40000000, transcendentals=0
        ),
        name="layer_back",
    )(
        lengths,
        slopes,
        grad,
        total_two,
        total_one,
        steep,
        query_rows,
        key_rows,
        value_rows,
        attended,
        lse,
        gains,
        weight_full,
        *([grad_rows] * hosted),
    )


def last_kernel(
    head_count,
    lengths_ref,
    slopes_ref,
    x_ref,
    grad_ref,
    gains_ref,
    weight_hbm,
    layer_out,
    low_out,
    att_out,
    hidden_out,
    two_out,
    pre_out,
    normed_out,
    one_out,
    query_grad_out,
    key_grad_out,
    value_grad_out,
    back_out,
    gains_out,
    slopes_out,
    weight_ref,
    dist_ref,
    mask_ref,
    query_rows,
    key_rows,
    value_rows,
    query_t,
    key_t,
    value_t,
    att_t,
    shares_ref,
    steep_ref,
    mixed_rows,
    mixed_t,
    delta_ref,
    query_grad_t,
    sems,
):
    step = pl.program_id(0)
    width = weight_ref.shape[1]
    inner = (weight_ref.shape[0] - 4 * width) // 2
    chunks = inner // width
    length = low_out.shape[1]
    head = width // head_count
    scale = float(head) ** (-0.5)
    rolling = Rolling(
        weight_copies(weight_hbm, weight_ref, sems, feed_cuts(width, inner)), step == 0
    )

    @pl.when(step == 0)
    def _():
        rolling.start()
        fill_distance(dist_ref, 2, 2)
        gains_out[...] = jnp.zeros_like(gains_out)
        slopes_out[...] = jnp.zeros_like(slopes_out)

    fill_mask(mask_ref, 2, lengths_ref[step])
    residual = x_ref[0]
    low = residual.astype(BF)
    low_out[0] = low
    rolling.need(0)
    queries = dot_nn(low, weight_ref[0:width]).astype(BF)
    query_rows[...] = queries
    query_t[...] = (queries.astype(F32) * scale).T.astype(BF)
    rolling.need(1)
    keys = dot_nn(low, weight_ref[width : 2 * width]).astype(BF)
    key_rows[...] = keys
    key_t[...] = keys.astype(F32).T.astype(BF)
    values = dot_nn(low, weight_ref[2 * width : 3 * width]).astype(BF)
    value_rows[...] = values
    value_t[...] = values.astype(F32).T.astype(BF)

    def ahead_pair(pair, carry):
        start = pl.multiple_of(pair * 2 * head, 2 * head)
        key_pair = key_rows[:, pl.ds(start, 2 * head)]
        query_pair = query_t[pl.ds(start, 2 * head), :]
        for which in range(2):
            index = 2 * pair + which
            scores = dot_nn(key_pair, pick_rows(query_pair, which))
            scores = scores - slopes_ref[index] * dist_ref[...] + mask_ref[...]
            peak = jnp.max(scores, axis=0, keepdims=True)
            lifted = jnp.exp(scores - peak)
            total = jnp.sum(lifted, axis=0, keepdims=True)
            shares = lifted * (1.0 / total)
            shares_ref[index] = shares
            rows = pl.ds(start + which * head, head)
            att_t[rows, :] = dot_nn(value_t[rows, :], shares.astype(BF))
        return carry

    lax.fori_loop(0, head_count // 2, ahead_pair, 0, unroll=True)
    attended = att_t[...].T.astype(BF)
    att_out[0] = attended
    rolling.need(2)
    total_one = residual + dot_nn(attended, weight_ref[3 * width : 4 * width])
    unit_one, inverse_one = norm_parts(total_one)
    normed = unit_one * gains_ref[0:1] + gains_ref[1:2]
    normed_low = normed.astype(BF)
    normed_out[0] = normed_low
    rolling.need(3)
    rolling.need(4)
    total_two = normed
    for chunk in range(chunks):
        inner_rows = pl.ds(4 * width + chunk * width, width)
        outer_rows = pl.ds(4 * width + inner + chunk * width, width)
        pre = dot_nt(normed_low, weight_ref[inner_rows, :])
        square = pre * pre
        bend = jnp.tanh(pre * (GELU_COEF + (GELU_COEF * GELU_CUBE) * square))
        half = 0.5 + 0.5 * bend
        hidden = (pre * half).astype(BF)
        steep = half + (0.5 * pre) * (1.0 - bend * bend) * (
            GELU_COEF + (3.0 * GELU_COEF * GELU_CUBE) * square
        )
        columns = pl.ds(chunk * width, width)
        hidden_out[0, :, columns] = hidden
        steep_ref[:, columns] = steep.astype(BF)
        total_two = total_two + dot_nn(hidden, weight_ref[outer_rows, :])
    unit_two, inverse_two = norm_parts(total_two)
    layer_out[0] = (unit_two * gains_ref[2:3] + gains_ref[3:4]).astype(layer_out.dtype)

    grad = grad_ref[0].astype(F32)
    gains_out[2:3] += jnp.sum(grad * unit_two, axis=0, keepdims=True)
    gains_out[3:4] += jnp.sum(grad, axis=0, keepdims=True)
    back_two = norm_back(grad, unit_two, inverse_two, gains_ref[2:3])
    two_low = back_two.astype(BF)
    two_out[0] = two_low
    back_normed = back_two
    for chunk in range(chunks):
        inner_rows = pl.ds(4 * width + chunk * width, width)
        outer_rows = pl.ds(4 * width + inner + chunk * width, width)
        columns = pl.ds(chunk * width, width)
        back_hidden = dot_nt(two_low, weight_ref[outer_rows, :])
        pre_grad = (back_hidden * steep_ref[:, columns].astype(F32)).astype(BF)
        pre_out[0, :, columns] = pre_grad
        back_normed = back_normed + dot_nn(pre_grad, weight_ref[inner_rows, :])
    gains_out[0:1] += jnp.sum(back_normed * unit_one, axis=0, keepdims=True)
    gains_out[1:2] += jnp.sum(back_normed, axis=0, keepdims=True)
    back_one = norm_back(back_normed, unit_one, inverse_one, gains_ref[0:1])
    back_out[0] = back_one
    one_low = back_one.astype(BF)
    one_out[0] = one_low
    mixed_low = dot_nt(one_low, weight_ref[3 * width : 4 * width]).astype(BF)
    mixed_rows[...] = mixed_low
    mixed_wide = mixed_low.astype(F32).T
    mixed_t[...] = mixed_wide.astype(BF)
    delta_ref[...] = jnp.sum((mixed_wide * att_t[...]).reshape(head_count, head, length), axis=1)

    def back_pair(pair, carry):
        start = pl.multiple_of(pair * 2 * head, 2 * head)
        lanes = pl.ds(start, 2 * head)
        value_pair = value_rows[:, lanes]
        query_pair = query_rows[:, lanes]
        mixed_pair = mixed_rows[:, lanes]
        mixed_pair_t = mixed_t[lanes, :]
        key_grad = jnp.zeros((length, 2 * head), F32)
        value_grad = jnp.zeros((length, 2 * head), F32)
        for which in range(2):
            index = 2 * pair + which
            half = lane_half(2 * head, which)
            shares = shares_ref[index]
            back_shares = dot_nn(value_pair, pick_rows(mixed_pair_t, which))
            back_scores = shares * (back_shares - delta_ref[pl.ds(index, 1), :])
            slopes_out[pl.ds(index, 1), :] += jnp.sum(
                back_scores * dist_ref[...], axis=0, keepdims=True
            )
            scores_low = back_scores.astype(BF)
            value_grad = value_grad + dot_nn(shares.astype(BF), mixed_pair * half)
            key_grad = key_grad + dot_nn(scores_low, query_pair * half)
            rows = pl.ds(start + which * head, head)
            query_grad_t[rows, :] = dot_nn(key_t[rows, :], scores_low)
        key_grad_out[0, :, lanes] = (key_grad * scale).astype(BF)
        value_grad_out[0, :, lanes] = value_grad.astype(BF)
        return carry

    lax.fori_loop(0, head_count // 2, back_pair, 0, unroll=True)
    query_grad_out[0] = (query_grad_t[...] * scale).T.astype(BF)


def layer_last(x, grad, lengths, slopes, gains, weight_full):
    batch, length, width = x.shape
    head_count = slopes.shape[0]
    rows = weight_full.shape[0]
    inner = (rows - 4 * width) // 2
    head_rows = -(-head_count // 8) * 8

    def block(size):
        return pl.BlockSpec((1, length, size), lambda i, *_: (i, 0, 0))

    def shape(size, dtype):
        return jax.ShapeDtypeStruct((batch, length, size), dtype)

    outs = [(width, BF)] * 3 + [(inner, BF), (width, BF), (inner, BF)] + [(width, BF)] * 5
    outs = outs + [(width, F32)]
    fixed = [
        pl.BlockSpec((4, width), lambda i, *_: (0, 0)),
        pl.BlockSpec((head_rows, length), lambda i, *_: (0, 0)),
    ]
    return pl.pallas_call(
        functools.partial(last_kernel, head_count),
        grid_spec=pltpu.PrefetchScalarGridSpec(
            num_scalar_prefetch=2,
            grid=(batch,),
            in_specs=[block(width), block(width), fixed[0], pl.BlockSpec(memory_space=pl.ANY)],
            out_specs=[block(size) for size, _ in outs] + fixed,
            scratch_shapes=[
                pltpu.VMEM((rows, width), BF),
                pltpu.VMEM((length, length), F32),
                pltpu.VMEM((length, length), F32),
                pltpu.VMEM((length, width), BF),
                pltpu.VMEM((length, width), BF),
                pltpu.VMEM((length, width), BF),
                pltpu.VMEM((width, length), BF),
                pltpu.VMEM((width, length), BF),
                pltpu.VMEM((width, length), BF),
                pltpu.VMEM((width, length), F32),
                pltpu.VMEM((head_count, length, length), F32),
                pltpu.VMEM((length, inner), BF),
                pltpu.VMEM((length, width), BF),
                pltpu.VMEM((width, length), BF),
                pltpu.VMEM((head_count, length), F32),
                pltpu.VMEM((width, length), F32),
                pltpu.SemaphoreType.DMA((5,)),
            ],
        ),
        out_shape=[shape(size, dtype) for size, dtype in outs]
        + [
            jax.ShapeDtypeStruct((4, width), F32),
            jax.ShapeDtypeStruct((head_rows, length), F32),
        ],
        compiler_params=pltpu.CompilerParams(vmem_limit_bytes=VMEM_LIMIT),
        cost_estimate=pl.CostEstimate(
            flops=60000000000, bytes_accessed=80000000, transcendentals=0
        ),
        name="layer_last",
    )(lengths, slopes, x, grad, gains, weight_full)


def weight_product(left, right):
    return lax.dot_general(
        left, right, (((0, 1), (0, 1)), ((), ())), preferred_element_type=F32
    )


def matrix_gradient(query_low, memory_low, attended, hidden, back):
    (two_low, pre_grad, normed_low, one_low, query_grad, key_grad, value_grad) = back
    return jnp.concatenate(
        [
            weight_product(query_low, query_grad),
            weight_product(memory_low, key_grad),
            weight_product(memory_low, value_grad),
            weight_product(attended, one_low),
            weight_product(pre_grad, normed_low),
            weight_product(hidden, two_low),
        ],
        axis=0,
    )


def adam_step(master, gradient, first_mom, second_mom, rate):
    first_new = BETA_ONE * first_mom + (1.0 - BETA_ONE) * gradient
    second_new = BETA_TWO * second_mom + (1.0 - BETA_TWO) * gradient * gradient
    first_hat = first_new / (1.0 - BETA_ONE**STEP)
    second_hat = second_new / (1.0 - BETA_TWO**STEP)
    inner_move = rate * (first_hat / (jnp.sqrt(second_hat) + ADAM_EPS) + DECAY_RATE * master)
    return (first_new, second_new, inner_move)


def outer_step(master, moves_sum, momentum_old, group_count):
    mean_move = moves_sum / group_count
    momentum_new = MOMENTUM * momentum_old + mean_move
    return (mean_move, momentum_new, master - OUTER_RATE * (mean_move + MOMENTUM * momentum_new))


def shards(
    hidden_in,
    lengths,
    out_grad,
    weights,
    weight_m,
    weight_v,
    outer_mom,
    small,
    small_m,
    small_v,
    small_mom,
):
    width = weights.shape[2]
    part_size = small.shape[0] // 2
    masters_low = [weights[layer].astype(BF) for layer in range(2)]

    gains = []
    slopes = []
    for layer in range(2):
        part = small[layer * part_size : (layer + 1) * part_size]
        gains.append(part[: 4 * width].reshape(4, width))
        slopes.append(part[4 * width :])

    matrix_two = lax.all_gather(masters_low[1], "fsdp", axis=0, tiled=True)
    matrix_one = gather_rows(masters_low[0])
    (q1, k1, v1, lse1, att1, one1, hid1, steep1, two1, first_out, low1) = layer_ahead(
        True, hidden_in, lengths, slopes[0], gains[0], matrix_one, F32
    )
    (block_out, low2, att2, hid2, *back_two) = layer_last(
        first_out, out_grad, lengths, slopes[1], gains[1], matrix_two
    )
    matrix_grad_two = matrix_gradient(low2, low2, att2, hid2, back_two[:7]).astype(BF)
    rest_two, matrix_grad_two = lax.optimization_barrier(
        ((back_two[4], back_two[5], back_two[6], back_two[7]), matrix_grad_two)
    )
    first_grad = rest_two[3]
    for index in range(3):
        first_grad = first_grad + jnp.einsum(
            "btn,an->bta",
            rest_two[index],
            matrix_two[index * width : (index + 1) * width],
            preferred_element_type=F32,
        )
    shard_two = lax.psum_scatter(matrix_grad_two, "fsdp", scatter_dimension=0, tiled=True)
    back_one = layer_back(
        True,
        first_grad,
        (q1, k1, v1, lse1, att1, one1, steep1, two1),
        lengths,
        slopes[0],
        gains[0],
        matrix_one,
    )
    input_grad = back_one[7]
    matrix_grad_one = matrix_gradient(low1, hidden_in, att1, hid1, back_one[:7]).astype(BF)
    head_count = slopes[0].shape[0]
    small_parts = []
    for back in (back_one, back_two):
        small_parts += [back[8].reshape(-1), -jnp.sum(back[9][:head_count], axis=1)]
    grad_shard, weight_sum, small_grad, small_sum = finish(
        matrix_grad_one,
        shard_two,
        weights,
        weight_m,
        weight_v,
        jnp.concatenate(small_parts)[None],
        small[None],
        small_m,
        small_v,
    )[:4]
    weight_first, weight_second, _ = adam_step(
        weights, grad_shard[None].astype(F32), weight_m, weight_v, INNER_RATE
    )
    small_first, small_second, _ = adam_step(small, small_grad, small_m, small_v, SMALL_RATE)
    weight_sum, small_sum = weight_sum.astype(F32), small_sum[0]
    group_count = lax.axis_size("group")
    weight_mean, weight_mom, weight_new = outer_step(weights, weight_sum, outer_mom, group_count)
    small_mean, small_momentum, small_after = outer_step(small, small_sum, small_mom, group_count)
    return (
        block_out,
        input_grad,
        weight_new,
        weight_new.astype(BF),
        weight_first,
        weight_second,
        weight_mean,
        weight_mom,
        small_after,
        small_first,
        small_second,
        small_mean,
        small_momentum,
    )


def solution(mesh):
    in_specs = (
        P(("group", "fsdp"), None, None),
        P(("group", "fsdp")),
        P(("group", "fsdp"), None, None),
        P(None, "fsdp", None),
        P("group", None, "fsdp", None),
        P("group", None, "fsdp", None),
        P(None, "fsdp", None),
        P(),
        P("group", None),
        P("group", None),
        P(),
    )
    out_specs = (
        P(("group", "fsdp"), None, None),
        P(("group", "fsdp"), None, None),
        P(None, "fsdp", None),
        P(None, "fsdp", None),
        P("group", None, "fsdp", None),
        P("group", None, "fsdp", None),
        P(None, "fsdp", None),
        P(None, "fsdp", None),
        P(),
        P("group", None),
        P("group", None),
        P(),
        P(),
    )
    return jax.shard_map(shards, mesh=mesh, in_specs=in_specs, out_specs=out_specs, check_vma=False)
```

```python
import functools

import jax
import jax.numpy as jnp
from jax import lax
from jax.experimental import pallas as pl
from jax.experimental.pallas import tpu as pltpu
from jax.sharding import PartitionSpec as P

STEP = 10


EPS_NORM = 1e-06
MASK_FILL = -1e30
BETA_ONE = 0.9
BETA_TWO = 0.999
ADAM_EPS = 1e-08
DECAY_RATE = 0.01
INNER_RATE = 0.03
SMALL_RATE = 0.6
OUTER_RATE = 0.7
MOMENTUM = 0.9
GELU_COEF = 0.7978845608028654
GELU_CUBE = 0.044715

BF = jnp.bfloat16
F32 = jnp.float32
VMEM_LIMIT = 60 * 1024 * 1024
MESH_ID = pl.DeviceIdType.MESH


def dot_nn(left, right):
    return lax.dot_general(left, right, (((1,), (0,)), ((), ())), preferred_element_type=F32)


def dot_nt(left, right):
    return lax.dot_general(left, right, (((1,), (1,)), ((), ())), preferred_element_type=F32)


def dot_tn(left, right):
    return lax.dot_general(left, right, (((0,), (0,)), ((), ())), preferred_element_type=F32)


def norm_parts(total):
    center = total - jnp.mean(total, axis=-1, keepdims=True)
    inverse = lax.rsqrt(jnp.mean(center * center, axis=-1, keepdims=True) + EPS_NORM)
    return center * inverse, inverse


def norm_back(grad, unit, inverse, gain):
    scaled = grad * gain
    lead = jnp.mean(scaled, axis=-1, keepdims=True)
    along = jnp.mean(scaled * unit, axis=-1, keepdims=True)
    return inverse * (scaled - lead - unit * along)


def fill_distance(dist_ref, key_step, query_step):
    shape = dist_ref.shape
    keys = lax.broadcasted_iota(jnp.int32, shape, 0) * key_step
    queries = lax.broadcasted_iota(jnp.int32, shape, 1) * query_step
    dist_ref[...] = jnp.abs(queries - keys).astype(F32)


def fill_mask(mask_ref, key_step, length):
    keys = lax.broadcasted_iota(jnp.int32, mask_ref.shape, 0) * key_step
    mask_ref[...] = jnp.where(keys < length, 0.0, MASK_FILL)


def pick_rows(pair_rows, which):
    half = pair_rows.shape[0] // 2
    zero = jnp.zeros((half, pair_rows.shape[1]), pair_rows.dtype)
    if which == 0:
        return jnp.concatenate([pair_rows[:half], zero], axis=0)
    return jnp.concatenate([zero, pair_rows[half:]], axis=0)


def lane_half(width, which):
    lanes = lax.broadcasted_iota(jnp.int32, (1, width), 1)
    inside = lanes < width // 2 if which == 0 else lanes >= width // 2
    return jnp.where(inside, 1.0, 0.0).astype(BF)


def pair_matrix(queries, keys, value, by_query):
    shape = (queries, keys) if by_query else (keys, queries)
    query_index = lax.broadcasted_iota(jnp.int32, shape, 0 if by_query else 1)
    key_index = lax.broadcasted_iota(jnp.int32, shape, 1 if by_query else 0)
    offset = key_index - 2 * query_index
    return jnp.where((offset == 0) | (offset == 1), value, 0.0).astype(BF)


def remote(source, target, send_sem, recv_sem, device):
    return pltpu.make_async_remote_copy(
        src_ref=source,
        dst_ref=target,
        send_sem=send_sem,
        recv_sem=recv_sem,
        device_id=device,
        device_id_type=pl.DeviceIdType.MESH,
    )


class Spot:
    def __init__(self, chips, group_count):
        self.chips = chips
        self.group_count = group_count
        self.group = lax.axis_index("group")
        self.member = lax.axis_index("fsdp")
        self.chip = self.member // 2
        self.core = self.member % 2

    def line(self, chip):
        return {"fsdp": 2 * chip + self.core}

    def partner(self):
        return {"fsdp": 2 * self.chip + 1 - self.core}

    def other(self, turn):
        return {"group": lax.rem(self.group + turn, self.group_count)}

    def back_group(self, turn):
        return lax.rem(self.group + self.group_count - turn, self.group_count)

    def ahead_chip(self, hop):
        return lax.rem(self.chip + hop, self.chips)

    def back_chip(self, hop):
        return lax.rem(self.chip + self.chips - hop, self.chips)


def meet(spot):
    barrier = pltpu.get_barrier_semaphore()
    for hop in range(1, spot.chips):
        pl.semaphore_signal(
            barrier, inc=1, device_id=spot.line(spot.ahead_chip(hop)), device_id_type=MESH_ID
        )
    pl.semaphore_signal(barrier, inc=1, device_id=spot.partner(), device_id_type=MESH_ID)
    for turn in range(1, spot.group_count):
        pl.semaphore_signal(barrier, inc=1, device_id=spot.other(turn), device_id_type=MESH_ID)
    pl.semaphore_wait(barrier, spot.chips - 1 + 1 + spot.group_count - 1)


class Gather:
    def __init__(self, spot, shard_ref, full_ref, sems):
        self.spot = spot
        self.shard = shard_ref
        self.full = full_ref
        self.line_send, self.line_recv, self.cross_send, self.cross_recv = sems[:4]
        self.core_send, self.core_recv, self.own_sem = sems[4:]
        self.rows = shard_ref.shape[0]
        self.part = self.rows // spot.group_count
        self.last = spot.chips - 1

    def piece(self, chip, core, group):
        start = (2 * chip + core) * self.rows + group * self.part
        return self.full.at[pl.ds(start, self.part)]

    def whole(self, chip, core):
        return self.full.at[pl.ds((2 * chip + core) * self.rows, self.rows)]

    def line_own(self, side):
        spot = self.spot
        return remote(
            self.shard.at[pl.ds(spot.group * self.part, self.part)],
            self.piece(spot.chip, spot.core, spot.group),
            self.line_send.at[spot.chips + side],
            self.line_recv.at[spot.chip],
            spot.line(spot.chip + 1 - 2 * side),
        )

    def line_pass(self, source, chip):
        here = self.piece(source, self.spot.core, self.spot.group)
        return remote(
            here, here, self.line_send.at[source], self.line_recv.at[source], self.spot.line(chip)
        )

    def cross_copy(self, source, turn):
        here = self.piece(source, self.spot.core, self.spot.group)
        slot = source * self.spot.group_count + turn
        return remote(
            here, here, self.cross_send.at[slot], self.cross_recv.at[slot], self.spot.other(turn)
        )

    def cross_arrival(self, source, turn):
        here = self.piece(source, self.spot.core, self.spot.back_group(turn))
        slot = source * self.spot.group_count + turn
        return remote(
            here, here, self.cross_send.at[slot], self.cross_recv.at[slot], self.spot.partner()
        )

    def core_copy(self, source, turn):
        here = self.piece(source, self.spot.core, self.spot.back_group(turn))
        slot = source * self.spot.group_count + turn
        return remote(
            here, here, self.core_send.at[slot], self.core_recv.at[slot], self.spot.partner()
        )

    def core_arrival(self, source, turn):
        here = self.piece(source, 1 - self.spot.core, self.spot.back_group(turn))
        slot = source * self.spot.group_count + turn
        return remote(
            here, here, self.core_send.at[slot], self.core_recv.at[slot], self.spot.partner()
        )

    def core_own(self):
        slot = self.spot.chip * self.spot.group_count
        return remote(
            self.shard,
            self.whole(self.spot.chip, self.spot.core),
            self.core_send.at[slot],
            self.core_recv.at[slot],
            self.spot.partner(),
        )

    def core_own_arrival(self):
        slot = self.spot.chip * self.spot.group_count
        here = self.whole(self.spot.chip, 1 - self.spot.core)
        return remote(
            here, here, self.core_send.at[slot], self.core_recv.at[slot], self.spot.partner()
        )

    def own_copy(self):
        return pltpu.make_async_copy(
            self.shard, self.whole(self.spot.chip, self.spot.core), self.own_sem.at[0]
        )

    def each_side(self, distance, act):
        spot = self.spot
        for side in range(2):
            source = spot.chip - distance if side == 0 else spot.chip + distance
            target = spot.chip + 1 - 2 * side

            @pl.when((source >= 0) & (source <= self.last))
            def _():
                act(source, target, (target >= 0) & (target <= self.last))

    def start(self):
        spot = self.spot

        @pl.when(spot.chip < self.last)
        def _():
            self.line_own(0).start()

        @pl.when(spot.chip > 0)
        def _():
            self.line_own(1).start()

        self.core_own().start()
        self.own_copy().start()

    def line_stage(self, source, target, inside):
        self.line_pass(source, self.spot.chip).wait_recv()

        @pl.when(inside)
        def _():
            self.line_pass(source, target).start()

        for turn in range(1, self.spot.group_count):
            self.cross_copy(source, turn).start()
        self.core_copy(source, 0).start()

    def cross_stage(self, source, target, inside):
        for turn in range(1, self.spot.group_count):
            self.cross_arrival(source, turn).wait_recv()
            self.core_copy(source, turn).start()

    def end_stage(self, source, target, inside):
        @pl.when(inside)
        def _():
            self.line_pass(source, target).wait_send()

        for turn in range(self.spot.group_count):
            if turn > 0:
                self.cross_copy(source, turn).wait_send()
            self.core_copy(source, turn).wait_send()
            self.core_arrival(source, turn).wait_recv()

    def run(self):
        spot = self.spot
        self.start()
        for distance in range(1, spot.chips):
            self.each_side(distance, self.line_stage)
            if distance > 1:
                self.each_side(distance - 1, self.cross_stage)
        self.each_side(spot.chips - 1, self.cross_stage)
        for distance in range(1, spot.chips):
            self.each_side(distance, self.end_stage)
        self.own_copy().wait()
        self.core_own().wait_send()
        self.core_own_arrival().wait_recv()

        @pl.when(spot.chip < self.last)
        def _():
            self.line_own(0).wait_send()

        @pl.when(spot.chip > 0)
        def _():
            self.line_own(1).wait_send()


def gather_sems(chips, group_count):
    dma = pltpu.SemaphoreType.DMA
    crossing = (chips * group_count,)
    return [dma((chips + 2,)), dma((chips,))] + [dma(crossing)] * 4 + [dma((1,))]


def gather_kernel(chips, group_count, shard_ref, full_ref, *sems):
    spot = Spot(chips, group_count)
    meet(spot)
    Gather(spot, shard_ref, full_ref, sems).run()


def gather_rows(shard):
    members, group_count = lax.axis_size("fsdp"), lax.axis_size("group")
    rows, width = shard.shape
    return pl.pallas_call(
        functools.partial(gather_kernel, members // 2, group_count),
        out_shape=jax.ShapeDtypeStruct((rows * members, width), BF),
        in_specs=[pl.BlockSpec(memory_space=pl.ANY)],
        out_specs=pl.BlockSpec(memory_space=pl.ANY),
        scratch_shapes=gather_sems(members // 2, group_count),
        compiler_params=pltpu.CompilerParams(collective_id=0, has_side_effects=True),
        name="gather_rows",
    )(shard)


def chunk_count(rows):
    return max(
        count for count in range(1, 7) if rows % (32 * count) == 0
    )


class Reduce:
    def __init__(self, spot, count, grad, swap, lands, loads, sends, sems):
        self.spot = spot
        self.count = count
        self.grad = grad
        self.swap = swap
        self.lands = lands
        self.loads = loads
        self.sends = sends
        (self.load_sems, self.send_sems, self.recv_sems, self.swap_send, self.swap_recv) = sems
        self.last = spot.chips - 1
        self.rows = grad.shape[0] // (2 * spot.chips)
        self.piece = self.rows // count
        self.items = self.last * count
        self.ticks = self.items + self.last
        self.slots = sends.shape[1]

    def swap_copy(self, chip, part):
        spot = self.spot
        start = part * self.piece
        source = (2 * chip + 1 - spot.core) * self.rows + start
        return remote(
            self.grad.at[pl.ds(pl.multiple_of(source, 8), self.piece)],
            self.swap.at[pl.ds(pl.multiple_of(chip * self.rows + start, 8), self.piece)],
            self.swap_send.at[chip * self.count + part],
            self.swap_recv.at[chip * self.count + part],
            spot.partner(),
        )

    def start(self):
        for chip in range(self.last, -1, -1):
            for part in range(self.count - 1, -1, -1):
                self.swap_copy(chip, part).start()
        self.fetch(0)

    def own_rows(self, chip, part):
        start = (2 * chip + self.spot.core) * self.rows + part * self.piece
        return self.grad.at[pl.ds(pl.multiple_of(start, 8), self.piece)]

    def swap_rows(self, chip, part):
        start = chip * self.rows + part * self.piece
        return self.swap.at[pl.ds(pl.multiple_of(start, 8), self.piece)]

    def land_rows(self, way, item):
        start = (way * self.items + item) * self.piece
        return self.lands.at[pl.ds(pl.multiple_of(start, 8), self.piece)]

    def plan(self, way, tick):
        spot, count, last = self.spot, self.count, self.last
        distance = spot.chip + way * (last - 2 * spot.chip)
        item = tick - distance
        raised = item + count * spot.chips
        chip = last - way - (lax.div(raised, count) - spot.chips)
        part = count - 1 - lax.rem(raised, count)
        inside = (item >= 0) & (item < self.items)
        ahead = (1 - 2 * way) * (chip - spot.chip)
        passes = inside & (ahead > 0)
        takes = distance > 0
        return item, chip, part, passes, takes

    def near_loads(self, way, tick, chip, part):
        turn = lax.rem(tick, 2)
        return [
            pltpu.make_async_copy(
                source,
                self.loads.at[way, 2 * turn + which],
                self.load_sems.at[way * 5 + 2 * turn + which],
            )
            for which, source in enumerate((self.own_rows(chip, part), self.swap_rows(chip, part)))
        ]

    def land_load(self, way, item):
        return pltpu.make_async_copy(
            self.land_rows(way, item), self.loads.at[way, 4], self.load_sems.at[way * 5 + 4]
        )

    def fetch(self, tick):
        for way in range(2):
            item, chip, part, passes, takes = self.plan(way, tick)

            @pl.when(passes)
            def _():
                self.swap_copy(chip, part).wait_recv()
                for copy in self.near_loads(way, tick, chip, part):
                    copy.start()

    def hop(self, way, item):
        spot = self.spot
        return remote(
            self.sends.at[way, lax.rem(item, self.slots)],
            self.land_rows(way, item),
            self.send_sems.at[way * self.items + item],
            self.recv_sems.at[way * self.items + item],
            spot.line(spot.chip + 1 - 2 * way),
        )

    def arrival(self, way, item):
        here = self.land_rows(way, item)
        sem = way * self.items + item
        return remote(
            here, here, self.send_sems.at[sem], self.recv_sems.at[sem], self.spot.partner()
        )

    def tick(self, tick):
        spot = self.spot
        nearer = jnp.where(2 * spot.chip > self.last, 1, 0)
        for turn in range(2):
            way = nearer if turn == 0 else 1 - nearer
            item, chip, part, passes, takes = self.plan(way, tick)

            @pl.when(passes)
            def _():
                @pl.when(takes)
                def _():
                    self.arrival(way, item).wait_recv()
                    self.land_load(way, item).start()

                slot = lax.rem(item, self.slots)
                first = way * (self.last - spot.chip) * self.count

                @pl.when(item - first >= self.slots)
                def _():
                    self.hop(way, item - self.slots).wait_send()

                for copy in self.near_loads(way, tick, chip, part):
                    copy.wait()

                @pl.when(takes)
                def _():
                    self.land_load(way, item).wait()
                    self.add(way, tick, slot, True)

                @pl.when(jnp.logical_not(takes))
                def _():
                    self.add(way, tick, slot, False)

                self.hop(way, item).start()

        self.fetch(tick + 1)

    def settle(self, order):
        spot = self.spot

        @pl.when(spot.chip > 0)
        def _():
            self.arrival(0, (self.last - spot.chip) * self.count + order).wait_recv()

        @pl.when(spot.chip < self.last)
        def _():
            self.arrival(1, (self.last - 1 - spot.chip) * self.count + order).wait_recv()

    def add(self, way, tick, slot, landed):
        block = 32
        near = 2 * lax.rem(tick, 2)

        def step(index, carry):
            rows = pl.ds(pl.multiple_of(index * block, block), block)
            total = self.loads[way, near, rows, :].astype(F32)
            total = total + self.loads[way, near + 1, rows, :].astype(F32)
            if landed:
                total = total + self.loads[way, 4, rows, :].astype(F32)
            self.sends[way, slot, rows, :] = total.astype(BF)
            return carry

        lax.fori_loop(0, self.piece // block, step, 0)

    def drain(self):
        spot = self.spot
        for way in range(2):
            begin = 0 if way == 0 else (self.last - spot.chip) * self.count
            end = (self.last - spot.chip) * self.count if way == 0 else self.items
            for back in range(1, self.slots + 1):

                @pl.when(end - back >= begin)
                def _():
                    self.hop(way, end - back).wait_send()

        for chip in range(spot.chips):
            for part in range(self.count):
                self.swap_copy(chip, part).wait_send()


def reduce_scratch(chips, rows, width):
    count = chunk_count(rows)
    dma = pltpu.SemaphoreType.DMA
    items = (chips - 1) * count
    return [
        pltpu.VMEM((2, 5, rows // count, width), BF),
        pltpu.VMEM((2, 4, rows // count, width), BF),
        dma((10,)),
        dma((2 * items,)),
        dma((2 * items,)),
        dma((chips * count,)),
        dma((chips * count,)),
    ]


def reduce_lands(chips, rows, width):
    return [
        jax.ShapeDtypeStruct((chips * rows, width), BF),
        jax.ShapeDtypeStruct((2 * (chips - 1) * rows, width), BF),
    ]


def move_of(master, gradient, first_mom, second_mom, rate):
    return adam_step(master, gradient, first_mom, second_mom, rate)[2]


def finish_kernel(
    chips,
    group_count,
    grad_zero,
    shard_one,
    weight_hbm,
    first_hbm,
    second_hbm,
    small_grad,
    small_ref,
    small_first,
    small_second,
    grad_out,
    sum_out,
    small_grad_out,
    small_sum_out,
    swap_zero,
    lands_zero,
    parts,
    states,
    grads,
    moves,
    quarters,
    sums,
    small_land,
    small_moves,
    small_move,
    part_sems,
    state_sems,
    grad_sems,
    cross_send,
    cross_recv,
    share_send,
    share_recv,
    share_own,
    small_send,
    small_recv,
    small_cross_send,
    small_cross_recv,
    *engine_scratch,
):
    tick = pl.program_id(0)
    spot = Spot(chips, group_count)
    rows = sum_out.shape[1]
    count = moves.shape[1]
    piece = rows // count
    quarter = piece // group_count
    engine = Reduce(
        spot,
        count,
        grad_zero,
        swap_zero,
        lands_zero,
        engine_scratch[0],
        engine_scratch[1],
        engine_scratch[2:],
    )
    members = 2 * chips
    last = chips - 1

    def small_send_copy(hop):
        target = lax.rem(spot.member + hop, members)
        return remote(
            small_grad,
            small_land.at[spot.member],
            small_send.at[hop],
            small_recv.at[hop],
            {"fsdp": target},
        )

    def small_cross_copy(turn):
        return remote(
            small_move,
            small_moves.at[spot.group],
            small_cross_send.at[turn],
            small_cross_recv.at[turn],
            spot.other(turn),
        )

    @pl.when(tick == 0)
    def _():
        barrier = pltpu.get_barrier_semaphore()
        for hop in range(1, members):
            pl.semaphore_signal(
                barrier,
                inc=1,
                device_id={"fsdp": lax.rem(spot.member + hop, members)},
                device_id_type=MESH_ID,
            )
        for turn in range(1, group_count):
            pl.semaphore_signal(barrier, inc=1, device_id=spot.other(turn), device_id_type=MESH_ID)
        pl.semaphore_wait(barrier, members - 1 + group_count - 1)
        engine.start()
        for hop in range(1, members):
            small_send_copy(hop).start()
        parts[...] = jnp.zeros_like(parts)

    bases = (engine.ticks - count, 1)

    def part_loads(layer, order):
        part, slot = count - 1 - order, lax.rem(order, 2)
        here = pl.multiple_of(part * piece, 8)
        start = (2 * spot.chip + spot.core) * rows + here
        sources = (shard_one.at[pl.ds(here, piece)],) if layer == 1 else (
            grad_zero.at[pl.ds(pl.multiple_of(start, 8), piece)],
            swap_zero.at[pl.ds(pl.multiple_of(spot.chip * rows + here, 8), piece)],
            lands_zero.at[
                pl.ds(pl.multiple_of(((last - spot.chip) * count + order) * piece, 8), piece)
            ],
            lands_zero.at[
                pl.ds(
                    pl.multiple_of(
                        ((2 * last - 1 - spot.chip) * count + order) * piece, 8
                    ),
                    piece,
                )
            ],
        )
        return [
            pltpu.make_async_copy(
                source,
                parts.at[layer, slot, which],
                part_sems.at[(2 * layer + slot) * 4 + which],
            )
            for which, source in enumerate(sources)
        ]

    def state_loads(layer, order):
        part, slot = count - 1 - order, lax.rem(order, 2)
        window = pl.ds(pl.multiple_of(part * piece, 8), piece)
        sources = (
            weight_hbm.at[layer, window],
            first_hbm.at[0, layer, window],
            second_hbm.at[0, layer, window],
        )
        return [
            pltpu.make_async_copy(
                source,
                states.at[layer, slot, which],
                state_sems.at[(2 * layer + slot) * 3 + which],
            )
            for which, source in enumerate(sources)
        ]

    def each_near(layer, order, act):
        copies = part_loads(layer, order)
        for copy in copies[:2]:
            act(copy)

    def each_landed(layer, order, act):
        if layer == 1:
            return
        copies = part_loads(layer, order)

        @pl.when(spot.chip > 0)
        def _():
            act(copies[2])

        @pl.when(spot.chip < last)
        def _():
            act(copies[3])

    def grad_store(layer, order):
        part = count - 1 - order
        return pltpu.make_async_copy(
            grads.at[layer, part],
            grad_out.at[layer, pl.ds(pl.multiple_of(part * piece, 8), piece)],
            grad_sems.at[layer * count + part],
        )

    def cross_copy(layer, order, turn):
        part = count - 1 - order
        target = lax.rem(spot.group + turn, group_count)
        sem = (layer * count + part) * group_count + turn
        return remote(
            moves.at[layer, part, pl.ds(pl.multiple_of(target * quarter, 8), quarter)],
            quarters.at[layer, part, turn],
            cross_send.at[sem],
            cross_recv.at[sem],
            spot.other(turn),
        )

    def share_rows(layer, part, group):
        start = pl.multiple_of(part * piece + group * quarter, 8)
        return sum_out.at[layer, pl.ds(start, quarter)]

    def share_copy(layer, order, turn):
        part = count - 1 - order
        sem = (layer * count + part) * group_count + turn
        return remote(
            sums.at[layer, part],
            share_rows(layer, part, spot.group),
            share_send.at[sem],
            share_recv.at[sem],
            spot.other(turn),
        )

    def share_local(layer, order):
        part = count - 1 - order
        return pltpu.make_async_copy(
            sums.at[layer, part],
            share_rows(layer, part, spot.group),
            share_own.at[layer * count + part],
        )

    def prepare(tick):
        for layer in range(2):
            order = tick - bases[layer]

            @pl.when((order >= 0) & (order < count))
            def _():
                if layer == 0:
                    engine.swap_copy(spot.chip, count - 1 - order).wait_recv()
                each_near(layer, order, lambda copy: copy.start())
                for copy in state_loads(layer, order):
                    copy.start()

    engine.tick(tick)
    prepare(tick + 1)
    landed = tick - bases[0]

    @pl.when((landed >= 0) & (landed < count))
    def _():
        engine.settle(landed)
        each_landed(0, landed, lambda copy: copy.start())

    for layer in range(2):
        later = tick - bases[layer] - 1

        @pl.when((later >= 0) & (later < count))
        def _():
            part = count - 1 - later
            for turn in range(1, group_count):
                cross_copy(layer, later, turn).wait_recv()
            total = moves[
                layer, part, pl.ds(pl.multiple_of(spot.group * quarter, 8), quarter), :
            ].astype(F32)
            for turn in range(1, group_count):
                total = total + quarters[layer, part, turn].astype(F32)
            sums[layer, part] = total.astype(sums.dtype)
            for turn in range(1, group_count):
                share_copy(layer, later, turn).start()
            share_local(layer, later).start()

        order = tick - bases[layer]

        @pl.when((order >= 0) & (order < count))
        def _():
            part, slot = count - 1 - order, lax.rem(order, 2)
            each_near(layer, order, lambda copy: copy.wait())
            each_landed(layer, order, lambda copy: copy.wait())
            for copy in state_loads(layer, order):
                copy.wait()

            def step(index, carry):
                window = pl.ds(pl.multiple_of(index * 32, 32), 32)
                total = parts[layer, slot, 0, window, :].astype(F32)
                for which in range(1, 4):
                    total = total + parts[layer, slot, which, window, :].astype(F32)
                low = total.astype(BF)
                grads[layer, part, window, :] = low
                move = move_of(
                    states[layer, slot, 0, window, :],
                    low.astype(F32),
                    states[layer, slot, 1, window, :],
                    states[layer, slot, 2, window, :],
                    INNER_RATE,
                )
                moves[layer, part, window, :] = move.astype(moves.dtype)
                return carry

            lax.fori_loop(0, piece // 32, step, 0)
            for turn in range(1, group_count):
                cross_copy(layer, order, turn).start()
            grad_store(layer, order).start()

    @pl.when(tick == 2)
    def _():
        small_land[spot.member] = small_grad[...]
        for hop in range(1, members):
            small_send_copy(hop).wait_recv()
        total = small_land[0]
        for member in range(1, members):
            total = total + small_land[member]
        small_grad_out[...] = total
        move = move_of(small_ref[...], total, small_first[...], small_second[...], SMALL_RATE)
        small_move[...] = move
        small_moves[spot.group] = move
        for turn in range(1, group_count):
            small_cross_copy(turn).start()

    @pl.when(tick == 4)
    def _():
        for turn in range(1, group_count):
            small_cross_copy(turn).wait_recv()
        total = small_moves[0]
        for group in range(1, group_count):
            total = total + small_moves[group]
        small_sum_out[...] = total

    @pl.when(tick == pl.num_programs(0) - 1)
    def _():
        engine.drain()
        for hop in range(1, members):
            small_send_copy(hop).wait_send()
        for turn in range(1, group_count):
            small_cross_copy(turn).wait_send()
        for layer in range(2):
            for order in range(count):
                grad_store(layer, order).wait()
                share_local(layer, order).wait()
                for turn in range(1, group_count):
                    cross_copy(layer, order, turn).wait_send()
                    share_copy(layer, order, turn).wait_send()
                    share_copy(layer, order, turn).wait_recv()


def finish(grad_zero, shard_one, weights, weight_m, weight_v, small_grad, small, small_m, small_v):
    members, group_count = lax.axis_size("fsdp"), lax.axis_size("group")
    chips = members // 2
    layers, rows, width = weights.shape
    count = chunk_count(rows)
    piece = rows // count
    quarter = piece // group_count
    wire = BF if quarter % 16 == 0 else F32
    small_size = small.shape[1]
    dma = pltpu.SemaphoreType.DMA
    ticks = (chips - 1) * count + chips - 1 + 1
    anywhere = pl.BlockSpec(memory_space=pl.ANY)
    local = pl.BlockSpec(memory_space=pltpu.VMEM)
    crossing = dma((layers * count * group_count,))
    return pl.pallas_call(
        functools.partial(finish_kernel, chips, group_count),
        grid=(ticks,),
        in_specs=[anywhere] * 5 + [local] * 4,
        out_specs=[anywhere, anywhere, local, local] + [anywhere] * 2,
        out_shape=[
            jax.ShapeDtypeStruct((layers, rows, width), BF),
            jax.ShapeDtypeStruct((layers, rows, width), wire),
            jax.ShapeDtypeStruct((1, small_size), F32),
            jax.ShapeDtypeStruct((1, small_size), F32),
        ]
        + reduce_lands(chips, rows, width),
        scratch_shapes=[
            pltpu.VMEM((layers, 2, 4, piece, width), BF),
            pltpu.VMEM((layers, 2, 3, piece, width), F32),
            pltpu.VMEM((layers, count, piece, width), BF),
            pltpu.VMEM((layers, count, piece, width), wire),
            pltpu.VMEM((layers, count, group_count, quarter, width), wire),
            pltpu.VMEM((layers, count, quarter, width), wire),
            pltpu.VMEM((members, 1, small_size), F32),
            pltpu.VMEM((group_count, 1, small_size), F32),
            pltpu.VMEM((1, small_size), F32),
            dma((8 * layers,)),
            dma((6 * layers,)),
            dma((layers * count,)),
            crossing,
            crossing,
            crossing,
            crossing,
            dma((layers * count,)),
            dma((members,)),
            dma((members,)),
            dma((group_count,)),
            dma((group_count,)),
        ]
        + reduce_scratch(chips, rows, width),
        compiler_params=pltpu.CompilerParams(
            vmem_limit_bytes=VMEM_LIMIT, collective_id=3, has_side_effects=True
        ),
        name="finish",
    )(grad_zero, shard_one, weights, weight_m, weight_v, small_grad, small, small_m, small_v)


def weight_copies(weight_hbm, weight_ref, sems, ranges):
    return [
        pltpu.make_async_copy(
            weight_hbm.at[pl.ds(start, size)], weight_ref.at[pl.ds(start, size)], sems.at[index]
        )
        for index, (start, size) in enumerate(ranges)
    ]


class Rolling:
    def __init__(self, copies, active, depth=2):
        self.copies = copies
        self.active = active
        self.depth = depth

    def start(self):
        for copy in self.copies[: self.depth]:
            copy.start()

    def need(self, index):
        @pl.when(self.active)
        def _():
            self.copies[index].wait()
            first = self.depth * (index + 1)
            for copy in self.copies[first : first + self.depth]:
                copy.start()


def feed_cuts(width, inner):
    ranges = [(0, width), (width, 2 * width), (3 * width, width)]
    return ranges + [(4 * width, inner), (4 * width + inner, inner)]


def ahead_kernel(
    is_first,
    head_count,
    place,
    lengths_ref,
    slopes_ref,
    x_ref,
    gains_ref,
    weight_hbm,
    *rest,
):
    if place is not None:
        shard_ref, rest = rest[0], rest[1:]
        full_ref, rest = rest[11], rest[:11] + rest[12:]
        job_sems = rest[18:]
    (
        query_out,
    key_out,
    value_out,
    lse_out,
    att_out,
    total_one_out,
    hidden_out,
    slope_out,
    total_two_out,
    layer_out,
    low_out,
    weight_ref,
    dist_ref,
    mask_ref,
    query_t,
    value_t,
    att_t,
    sems,
    ) = rest[:18]
    step = pl.program_id(0)
    if place is not None:
        spot = Spot(*place)
        job = Gather(spot, shard_ref, full_ref, job_sems)
        spread = [round(index * 7 / (job.tick_count - 1)) for index in range(job.tick_count)]

    def tick(quarter):
        if place is None:
            return
        for index in range(job.tick_count):
            if spread[index] % 2 == quarter:

                @pl.when(step == spread[index] // 2)
                def _():
                    if index == 0:
                        meet(spot)
                    job.tick(index)

    tick(0)
    width = weight_ref.shape[1]
    inner = (weight_ref.shape[0] - 4 * width) // 2
    queries, keys = query_out.shape[1], key_out.shape[1]
    head = width // head_count
    copies = weight_copies(weight_hbm, weight_ref, sems, feed_cuts(width, inner))
    rolling = Rolling(copies, step == 0)
    key_step = 1 if is_first else 2

    @pl.when(step == 0)
    def _():
        rolling.start()
        fill_distance(dist_ref, key_step, 2)

    fill_mask(mask_ref, key_step, lengths_ref[step])
    if is_first:
        memory_low = x_ref[0]
        residual = dot_nn(pair_matrix(queries, keys, 0.5, True), memory_low)
        query_low = residual.astype(BF)
    else:
        residual = x_ref[0]
        query_low = residual.astype(BF)
        memory_low = query_low
    low_out[0] = query_low
    rolling.need(0)
    query_rows = dot_nn(query_low, weight_ref[0:width]).astype(BF)
    query_out[0] = query_rows
    query_t[...] = (query_rows.astype(F32) * float(head) ** (-0.5)).T.astype(BF)
    rolling.need(1)
    key_out[0] = dot_nn(memory_low, weight_ref[width : 2 * width]).astype(BF)
    value_rows = dot_nn(memory_low, weight_ref[2 * width : 3 * width]).astype(BF)
    value_out[0] = value_rows
    value_t[...] = value_rows.astype(F32).T.astype(BF)

    def pair_step(pair, carry):
        start = pl.multiple_of(pair * 2 * head, 2 * head)
        key_pair = key_out[0, :, pl.ds(start, 2 * head)]
        query_pair = query_t[pl.ds(start, 2 * head), :]
        for which in range(2):
            index = 2 * pair + which
            scores = dot_nn(key_pair, pick_rows(query_pair, which))
            scores = scores - slopes_ref[index] * dist_ref[...] + mask_ref[...]
            peak = jnp.max(scores, axis=0, keepdims=True)
            lifted = jnp.exp(scores - peak)
            total = jnp.sum(lifted, axis=0, keepdims=True)
            shares = lifted.astype(BF)
            rows = pl.ds(start + which * head, head)
            mixed = dot_nn(value_t[rows, :], shares)
            att_t[rows, :] = mixed * (1.0 / total)
            lse_out[0, pl.ds(index, 1), :] = peak + jnp.log(total)
        return carry

    lax.fori_loop(0, head_count // 2, pair_step, 0, unroll=True)
    attended = att_t[...].T.astype(BF)
    att_out[0] = attended
    rolling.need(2)
    total_one = residual + dot_nn(attended, weight_ref[3 * width : 4 * width])
    total_one_out[0] = total_one
    unit, _ = norm_parts(total_one)
    normed = unit * gains_ref[0:1] + gains_ref[1:2]
    normed_low = normed.astype(BF)
    rolling.need(3)
    rolling.need(4)
    total_two = normed
    for chunk in range(inner // width):
        inner_rows = pl.ds(4 * width + chunk * width, width)
        outer_rows = pl.ds(4 * width + inner + chunk * width, width)
        pre = dot_nt(normed_low, weight_ref[inner_rows, :])
        square = pre * pre
        bend = jnp.tanh(pre * (GELU_COEF + (GELU_COEF * GELU_CUBE) * square))
        half = 0.5 + 0.5 * bend
        hidden = (pre * half).astype(BF)
        steep = half + (0.5 * pre) * (1.0 - bend * bend) * (
            GELU_COEF + (3.0 * GELU_COEF * GELU_CUBE) * square
        )
        columns = pl.ds(chunk * width, width)
        hidden_out[0, :, columns] = hidden
        slope_out[0, :, columns] = steep.astype(BF)
        total_two = total_two + dot_nn(hidden, weight_ref[outer_rows, :])
    total_two_out[0] = total_two
    unit_two, _ = norm_parts(total_two)
    result = unit_two * gains_ref[2:3] + gains_ref[3:4]
    layer_out[0] = result.astype(layer_out.dtype)
    tick(1)


def layer_ahead(is_first, x, lengths, slopes, gains, weight_full, out_dtype, shard=None):
    batch, memory_length, width = x.shape
    queries = memory_length // 2 if is_first else memory_length
    keys = memory_length
    head_count = slopes.shape[0]
    rows = weight_full.shape[0]
    inner = (rows - 4 * width) // 2
    head_rows = -(-head_count // 8) * 8

    def block(length, size):
        return pl.BlockSpec((1, length, size), lambda i, *_: (i, 0, 0))

    def shape(length, size, dtype):
        return jax.ShapeDtypeStruct((batch, length, size), dtype)

    outs = [
        (queries, width, BF),
        (keys, width, BF),
        (keys, width, BF),
        (head_rows, queries, F32),
        (queries, width, BF),
        (queries, width, F32),
        (queries, inner, BF),
        (queries, inner, BF),
        (queries, width, F32),
        (queries, width, out_dtype),
        (queries, width, BF),
    ]
    flops = 2 * batch * width * (
        2 * queries * width + 2 * keys * width + 2 * queries * inner + 2 * queries * keys
    )
    hosted = shard is not None
    place = (lax.axis_size("fsdp") // 2, lax.axis_size("group")) if hosted else None
    anywhere = [pl.BlockSpec(memory_space=pl.ANY)] * hosted
    full_shape = [jax.ShapeDtypeStruct((rows, width), BF)] * hosted
    job_sems = gather_sems(*place) if hosted else []
    params = dict(collective_id=1, has_side_effects=True) if hosted else {}
    return pl.pallas_call(
        functools.partial(ahead_kernel, is_first, head_count, place),
        grid_spec=pltpu.PrefetchScalarGridSpec(
            num_scalar_prefetch=2,
            grid=(batch,),
            in_specs=[
                block(memory_length, width),
                pl.BlockSpec((4, width), lambda i, *_: (0, 0)),
                pl.BlockSpec(memory_space=pl.ANY),
            ]
            + anywhere,
            out_specs=[block(length, size) for length, size, _ in outs] + anywhere,
            scratch_shapes=[
                pltpu.VMEM((rows, width), BF),
                pltpu.VMEM((keys, queries), F32),
                pltpu.VMEM((keys, queries), F32),
                pltpu.VMEM((width, queries), BF),
                pltpu.VMEM((width, keys), BF),
                pltpu.VMEM((width, queries), F32),
                pltpu.SemaphoreType.DMA((5,)),
            ]
            + job_sems,
        ),
        out_shape=[shape(*out) for out in outs] + full_shape,
        compiler_params=pltpu.CompilerParams(vmem_limit_bytes=VMEM_LIMIT, **params),
        cost_estimate=pl.CostEstimate(
            flops=flops, bytes_accessed=rows * width * 2 + 30000000, transcendentals=0
        ),
        name="layer_ahead",
    )(lengths, slopes, x, gains, weight_full, *([shard] * hosted))


def back_kernel(
    is_first,
    head_count,
    place,
    query_steps,
    lengths_ref,
    slopes_ref,
    grad_ref,
    total_two_ref,
    total_one_ref,
    slope_ref,
    query_ref,
    key_ref,
    value_ref,
    att_ref,
    lse_ref,
    gains_ref,
    weight_hbm,
    *rest,
):
    if place is not None:
        grad_rows, rest = rest[0], rest[1:]
        landing, rest = rest[10:12], rest[:10] + rest[12:]
        job = rest[20:]
    (
        two_out,
        pre_out,
        normed_out,
        one_out,
        query_grad_out,
        key_grad_out,
        value_grad_out,
        input_out,
        gains_out,
        slopes_out,
        weight_ref,
        dist_ref,
        mask_ref,
        query_t,
        key_t,
        mixed_t,
        mixed_rows,
        delta_ref,
        query_grad_t,
        sems,
    ) = rest[:20]
    step = pl.program_id(0)
    if place is not None:
        spot = Spot(*place)
        engine = Reduce(
            spot,
            chunk_count(grad_rows.shape[0] // (2 * spot.chips)),
            grad_rows,
            landing[0],
            landing[1],
            job[0],
            job[1],
            job[2:],
        )

        early_ticks = engine.ticks - 1

        @pl.when(step == 0)
        def _():
            meet(spot)
            engine.start()
            engine.tick(0)

    pairs = head_count // 2
    sites = pairs + 2

    def reduce_ticks(site):
        if place is None:
            return
        total = sites * query_steps
        here = step * sites + site
        for index in range(-(-early_ticks // total)):
            tick = lax.div(here * early_ticks, total) + index + 1

            @pl.when(tick <= lax.div((here + 1) * early_ticks, total))
            def _():
                engine.tick(tick)

    width = weight_ref.shape[1]
    inner = (weight_ref.shape[0] - 4 * width) // 2
    queries, keys = query_ref.shape[1], key_ref.shape[1]
    head = width // head_count
    ranges = [
        (0, 3 * width),
        (3 * width, width),
        (4 * width, inner),
        (4 * width + inner, inner),
    ]
    copies = weight_copies(weight_hbm, weight_ref, sems, ranges)
    key_step = 1 if is_first else 2
    scale = float(head) ** (-0.5)

    @pl.when(step == 0)
    def _():
        for index in (3, 2, 1, 0):
            copies[index].start()
        fill_distance(dist_ref, key_step, 2)
        gains_out[...] = jnp.zeros_like(gains_out)
        slopes_out[...] = jnp.zeros_like(slopes_out)

    def need(index):
        @pl.when(step == 0)
        def _():
            copies[index].wait()

    fill_mask(mask_ref, key_step, lengths_ref[step])
    query_t[...] = (query_ref[0].astype(F32) * scale).T.astype(BF)
    key_t[...] = key_ref[0].astype(F32).T.astype(BF)

    grad = grad_ref[0].astype(F32)
    unit_two, inverse_two = norm_parts(total_two_ref[0])
    gains_out[2:3] += jnp.sum(grad * unit_two, axis=0, keepdims=True)
    gains_out[3:4] += jnp.sum(grad, axis=0, keepdims=True)
    back_two = norm_back(grad, unit_two, inverse_two, gains_ref[2:3])
    two_low = back_two.astype(BF)
    two_out[0] = two_low
    need(3)
    need(2)
    back_normed = back_two
    for chunk in range(inner // width):
        inner_rows = pl.ds(4 * width + chunk * width, width)
        outer_rows = pl.ds(4 * width + inner + chunk * width, width)
        columns = pl.ds(chunk * width, width)
        back_hidden = dot_nt(two_low, weight_ref[outer_rows, :])
        pre_grad = (back_hidden * slope_ref[0, :, columns].astype(F32)).astype(BF)
        pre_out[0, :, columns] = pre_grad
        back_normed = back_normed + dot_nn(pre_grad, weight_ref[inner_rows, :])
        if chunk % 2 == 1 and chunk < 4:
            reduce_ticks(chunk // 2)
    unit_one, inverse_one = norm_parts(total_one_ref[0])
    normed_out[0] = (unit_one * gains_ref[0:1] + gains_ref[1:2]).astype(BF)
    gains_out[0:1] += jnp.sum(back_normed * unit_one, axis=0, keepdims=True)
    gains_out[1:2] += jnp.sum(back_normed, axis=0, keepdims=True)
    back_one = norm_back(back_normed, unit_one, inverse_one, gains_ref[0:1])
    one_low = back_one.astype(BF)
    one_out[0] = one_low
    need(1)
    back_mixed = dot_nt(one_low, weight_ref[3 * width : 4 * width])
    mixed_low = back_mixed.astype(BF)
    mixed_rows[...] = mixed_low
    mixed_wide = mixed_low.astype(F32).T
    mixed_t[...] = mixed_wide.astype(BF)
    product = mixed_wide * att_ref[0].astype(F32).T
    delta_ref[...] = jnp.sum(product.reshape(head_count, head, queries), axis=1)

    def pair_step(pair, carry):
        start = pl.multiple_of(pair * 2 * head, 2 * head)
        lanes = pl.ds(start, 2 * head)
        key_pair = key_ref[0, :, lanes]
        value_pair = value_ref[0, :, lanes]
        query_pair = query_ref[0, :, lanes]
        mixed_pair = mixed_rows[:, lanes]
        query_pair_t = query_t[lanes, :]
        mixed_pair_t = mixed_t[lanes, :]
        key_grad = jnp.zeros((keys, 2 * head), F32)
        value_grad = jnp.zeros((keys, 2 * head), F32)
        for which in range(2):
            index = 2 * pair + which
            half = lane_half(2 * head, which)
            scores = dot_nn(key_pair, pick_rows(query_pair_t, which))
            scores = scores - slopes_ref[index] * dist_ref[...] + mask_ref[...]
            shares = jnp.exp(scores - lse_ref[0, pl.ds(index, 1), :])
            back_shares = dot_nn(value_pair, pick_rows(mixed_pair_t, which))
            back_scores = shares * (back_shares - delta_ref[pl.ds(index, 1), :])
            slopes_out[pl.ds(index, 1), :] += jnp.sum(
                back_scores * dist_ref[...], axis=0, keepdims=True
            )
            scores_low = back_scores.astype(BF)
            value_grad = value_grad + dot_nn(shares.astype(BF), mixed_pair * half)
            key_grad = key_grad + dot_nn(scores_low, query_pair * half)
            rows = pl.ds(start + which * head, head)
            query_grad_t[rows, :] = dot_nn(key_t[rows, :], scores_low)
        reduce_ticks(pair + 2)
        key_grad_out[0, :, lanes] = (key_grad * scale).astype(BF)
        value_grad_out[0, :, lanes] = value_grad.astype(BF)
        return carry

    lax.fori_loop(0, head_count // 2, pair_step, 0, unroll=True)
    query_grad = (query_grad_t[...] * scale).T.astype(BF)
    query_grad_out[0] = query_grad
    need(0)
    back_query = back_one + dot_nt(query_grad, weight_ref[0:width])
    back_memory = dot_nt(key_grad_out[0], weight_ref[width : 2 * width]) + dot_nt(
        value_grad_out[0], weight_ref[2 * width : 3 * width]
    )
    if is_first:
        spread = pair_matrix(queries, keys, 1.0, False)
        half_grad = back_query * 0.5
        upper = half_grad.astype(BF)
        lower = (half_grad - upper.astype(F32)).astype(BF)
        back_memory = back_memory + dot_nn(spread, upper) + dot_nn(spread, lower)
        input_out[0] = back_memory
    else:
        input_out[0] = back_query + back_memory
    if place is not None:

        @pl.when(step == pl.num_programs(0) - 1)
        def _():
            def late_tick(tick, carry):
                engine.tick(tick)
                return carry

            lax.fori_loop(early_ticks + 1, engine.ticks, late_tick, 0)
            for part in range(engine.count):
                engine.swap_copy(spot.chip, part).wait_recv()
                engine.settle(part)
            engine.drain()


def layer_back(is_first, grad, kept, lengths, slopes, gains, weight_full, grad_rows=None):
    (query_rows, key_rows, value_rows, lse, attended, total_one, steep, total_two) = kept
    batch, queries, width = query_rows.shape
    keys = key_rows.shape[1]
    head_count = slopes.shape[0]
    rows = weight_full.shape[0]
    inner = (rows - 4 * width) // 2
    head_rows = lse.shape[1]

    def block(length, size):
        return pl.BlockSpec((1, length, size), lambda i, *_: (i, 0, 0))

    def shape(length, size, dtype):
        return jax.ShapeDtypeStruct((batch, length, size), dtype)

    outs = [
        (queries, width, BF),
        (queries, inner, BF),
        (queries, width, BF),
        (queries, width, BF),
        (queries, width, BF),
        (keys, width, BF),
        (keys, width, BF),
        (keys, width, F32),
    ]
    flops = 2 * batch * width * (
        2 * queries * width + 2 * keys * width + 2 * queries * inner + 5 * queries * keys
    )
    hosted = grad_rows is not None
    place, job_scratch, lands, params = None, [], [], {}
    if hosted:
        place = (lax.axis_size("fsdp") // 2, lax.axis_size("group"))
        shard_rows = rows // (2 * place[0])
        job_scratch = reduce_scratch(place[0], shard_rows, width)
        lands = reduce_lands(place[0], shard_rows, width)
        params = dict(collective_id=2, has_side_effects=True)
    anywhere = pl.BlockSpec(memory_space=pl.ANY)
    return pl.pallas_call(
        functools.partial(back_kernel, is_first, head_count, place, batch),
        grid_spec=pltpu.PrefetchScalarGridSpec(
            num_scalar_prefetch=2,
            grid=(batch,),
            in_specs=[
                block(queries, width),
                block(queries, width),
                block(queries, width),
                block(queries, inner),
                block(queries, width),
                block(keys, width),
                block(keys, width),
                block(queries, width),
                block(head_rows, queries),
                pl.BlockSpec((4, width), lambda i, *_: (0, 0)),
                anywhere,
            ]
            + [anywhere] * hosted,
            out_specs=[block(length, size) for length, size, _ in outs]
            + [
                pl.BlockSpec((4, width), lambda i, *_: (0, 0)),
                pl.BlockSpec((head_rows, queries), lambda i, *_: (0, 0)),
            ]
            + [anywhere] * len(lands),
            scratch_shapes=[
                pltpu.VMEM((rows, width), BF),
                pltpu.VMEM((keys, queries), F32),
                pltpu.VMEM((keys, queries), F32),
                pltpu.VMEM((width, queries), BF),
                pltpu.VMEM((width, keys), BF),
                pltpu.VMEM((width, queries), BF),
                pltpu.VMEM((queries, width), BF),
                pltpu.VMEM((head_count, queries), F32),
                pltpu.VMEM((width, queries), F32),
                pltpu.SemaphoreType.DMA((4,)),
            ]
            + job_scratch,
        ),
        out_shape=[shape(*out) for out in outs]
        + [
            jax.ShapeDtypeStruct((4, width), F32),
            jax.ShapeDtypeStruct((head_rows, queries), F32),
        ]
        + lands,
        compiler_params=pltpu.CompilerParams(vmem_limit_bytes=VMEM_LIMIT, **params),
        cost_estimate=pl.CostEstimate(
            flops=flops, bytes_accessed=rows * width * 2 + 40000000, transcendentals=0
        ),
        name="layer_back",
    )(
        lengths,
        slopes,
        grad,
        total_two,
        total_one,
        steep,
        query_rows,
        key_rows,
        value_rows,
        attended,
        lse,
        gains,
        weight_full,
        *([grad_rows] * hosted),
    )


def last_kernel(
    head_count,
    lengths_ref,
    slopes_ref,
    x_ref,
    grad_ref,
    gains_ref,
    weight_hbm,
    layer_out,
    low_out,
    att_out,
    hidden_out,
    two_out,
    pre_out,
    normed_out,
    one_out,
    query_grad_out,
    key_grad_out,
    value_grad_out,
    back_out,
    gains_out,
    slopes_out,
    weight_ref,
    dist_ref,
    mask_ref,
    query_rows,
    key_rows,
    value_rows,
    query_t,
    key_t,
    value_t,
    att_t,
    shares_ref,
    steep_ref,
    mixed_rows,
    mixed_t,
    delta_ref,
    query_grad_t,
    sems,
):
    step = pl.program_id(0)
    width = weight_ref.shape[1]
    inner = (weight_ref.shape[0] - 4 * width) // 2
    chunks = inner // width
    length = low_out.shape[1]
    head = width // head_count
    scale = float(head) ** (-0.5)
    rolling = Rolling(
        weight_copies(weight_hbm, weight_ref, sems, feed_cuts(width, inner)), step == 0
    )

    @pl.when(step == 0)
    def _():
        rolling.start()
        fill_distance(dist_ref, 2, 2)
        gains_out[...] = jnp.zeros_like(gains_out)
        slopes_out[...] = jnp.zeros_like(slopes_out)

    fill_mask(mask_ref, 2, lengths_ref[step])
    residual = x_ref[0]
    low = residual.astype(BF)
    low_out[0] = low
    rolling.need(0)
    queries = dot_nn(low, weight_ref[0:width]).astype(BF)
    query_rows[...] = queries
    query_t[...] = (queries.astype(F32) * scale).T.astype(BF)
    rolling.need(1)
    keys = dot_nn(low, weight_ref[width : 2 * width]).astype(BF)
    key_rows[...] = keys
    key_t[...] = keys.astype(F32).T.astype(BF)
    values = dot_nn(low, weight_ref[2 * width : 3 * width]).astype(BF)
    value_rows[...] = values
    value_t[...] = values.astype(F32).T.astype(BF)

    def ahead_pair(pair, carry):
        start = pl.multiple_of(pair * 2 * head, 2 * head)
        key_pair = key_rows[:, pl.ds(start, 2 * head)]
        query_pair = query_t[pl.ds(start, 2 * head), :]
        for which in range(2):
            index = 2 * pair + which
            scores = dot_nn(key_pair, pick_rows(query_pair, which))
            scores = scores - slopes_ref[index] * dist_ref[...] + mask_ref[...]
            peak = jnp.max(scores, axis=0, keepdims=True)
            lifted = jnp.exp(scores - peak)
            total = jnp.sum(lifted, axis=0, keepdims=True)
            shares = lifted * (1.0 / total)
            shares_ref[index] = shares
            rows = pl.ds(start + which * head, head)
            att_t[rows, :] = dot_nn(value_t[rows, :], shares.astype(BF))
        return carry

    lax.fori_loop(0, head_count // 2, ahead_pair, 0, unroll=True)
    attended = att_t[...].T.astype(BF)
    att_out[0] = attended
    rolling.need(2)
    total_one = residual + dot_nn(attended, weight_ref[3 * width : 4 * width])
    unit_one, inverse_one = norm_parts(total_one)
    normed = unit_one * gains_ref[0:1] + gains_ref[1:2]
    normed_low = normed.astype(BF)
    normed_out[0] = normed_low
    rolling.need(3)
    rolling.need(4)
    total_two = normed
    for chunk in range(chunks):
        inner_rows = pl.ds(4 * width + chunk * width, width)
        outer_rows = pl.ds(4 * width + inner + chunk * width, width)
        pre = dot_nt(normed_low, weight_ref[inner_rows, :])
        square = pre * pre
        bend = jnp.tanh(pre * (GELU_COEF + (GELU_COEF * GELU_CUBE) * square))
        half = 0.5 + 0.5 * bend
        hidden = (pre * half).astype(BF)
        steep = half + (0.5 * pre) * (1.0 - bend * bend) * (
            GELU_COEF + (3.0 * GELU_COEF * GELU_CUBE) * square
        )
        columns = pl.ds(chunk * width, width)
        hidden_out[0, :, columns] = hidden
        steep_ref[:, columns] = steep.astype(BF)
        total_two = total_two + dot_nn(hidden, weight_ref[outer_rows, :])
    unit_two, inverse_two = norm_parts(total_two)
    layer_out[0] = (unit_two * gains_ref[2:3] + gains_ref[3:4]).astype(layer_out.dtype)

    grad = grad_ref[0].astype(F32)
    gains_out[2:3] += jnp.sum(grad * unit_two, axis=0, keepdims=True)
    gains_out[3:4] += jnp.sum(grad, axis=0, keepdims=True)
    back_two = norm_back(grad, unit_two, inverse_two, gains_ref[2:3])
    two_low = back_two.astype(BF)
    two_out[0] = two_low
    back_normed = back_two
    for chunk in range(chunks):
        inner_rows = pl.ds(4 * width + chunk * width, width)
        outer_rows = pl.ds(4 * width + inner + chunk * width, width)
        columns = pl.ds(chunk * width, width)
        back_hidden = dot_nt(two_low, weight_ref[outer_rows, :])
        pre_grad = (back_hidden * steep_ref[:, columns].astype(F32)).astype(BF)
        pre_out[0, :, columns] = pre_grad
        back_normed = back_normed + dot_nn(pre_grad, weight_ref[inner_rows, :])
    gains_out[0:1] += jnp.sum(back_normed * unit_one, axis=0, keepdims=True)
    gains_out[1:2] += jnp.sum(back_normed, axis=0, keepdims=True)
    back_one = norm_back(back_normed, unit_one, inverse_one, gains_ref[0:1])
    back_out[0] = back_one
    one_low = back_one.astype(BF)
    one_out[0] = one_low
    mixed_low = dot_nt(one_low, weight_ref[3 * width : 4 * width]).astype(BF)
    mixed_rows[...] = mixed_low
    mixed_wide = mixed_low.astype(F32).T
    mixed_t[...] = mixed_wide.astype(BF)
    delta_ref[...] = jnp.sum((mixed_wide * att_t[...]).reshape(head_count, head, length), axis=1)

    def back_pair(pair, carry):
        start = pl.multiple_of(pair * 2 * head, 2 * head)
        lanes = pl.ds(start, 2 * head)
        value_pair = value_rows[:, lanes]
        query_pair = query_rows[:, lanes]
        mixed_pair = mixed_rows[:, lanes]
        mixed_pair_t = mixed_t[lanes, :]
        key_grad = jnp.zeros((length, 2 * head), F32)
        value_grad = jnp.zeros((length, 2 * head), F32)
        for which in range(2):
            index = 2 * pair + which
            half = lane_half(2 * head, which)
            shares = shares_ref[index]
            back_shares = dot_nn(value_pair, pick_rows(mixed_pair_t, which))
            back_scores = shares * (back_shares - delta_ref[pl.ds(index, 1), :])
            slopes_out[pl.ds(index, 1), :] += jnp.sum(
                back_scores * dist_ref[...], axis=0, keepdims=True
            )
            scores_low = back_scores.astype(BF)
            value_grad = value_grad + dot_nn(shares.astype(BF), mixed_pair * half)
            key_grad = key_grad + dot_nn(scores_low, query_pair * half)
            rows = pl.ds(start + which * head, head)
            query_grad_t[rows, :] = dot_nn(key_t[rows, :], scores_low)
        key_grad_out[0, :, lanes] = (key_grad * scale).astype(BF)
        value_grad_out[0, :, lanes] = value_grad.astype(BF)
        return carry

    lax.fori_loop(0, head_count // 2, back_pair, 0, unroll=True)
    query_grad_out[0] = (query_grad_t[...] * scale).T.astype(BF)


def layer_last(x, grad, lengths, slopes, gains, weight_full):
    batch, length, width = x.shape
    head_count = slopes.shape[0]
    rows = weight_full.shape[0]
    inner = (rows - 4 * width) // 2
    head_rows = -(-head_count // 8) * 8

    def block(size):
        return pl.BlockSpec((1, length, size), lambda i, *_: (i, 0, 0))

    def shape(size, dtype):
        return jax.ShapeDtypeStruct((batch, length, size), dtype)

    outs = [(width, BF)] * 3 + [(inner, BF), (width, BF), (inner, BF)] + [(width, BF)] * 5
    outs = outs + [(width, F32)]
    fixed = [
        pl.BlockSpec((4, width), lambda i, *_: (0, 0)),
        pl.BlockSpec((head_rows, length), lambda i, *_: (0, 0)),
    ]
    return pl.pallas_call(
        functools.partial(last_kernel, head_count),
        grid_spec=pltpu.PrefetchScalarGridSpec(
            num_scalar_prefetch=2,
            grid=(batch,),
            in_specs=[block(width), block(width), fixed[0], pl.BlockSpec(memory_space=pl.ANY)],
            out_specs=[block(size) for size, _ in outs] + fixed,
            scratch_shapes=[
                pltpu.VMEM((rows, width), BF),
                pltpu.VMEM((length, length), F32),
                pltpu.VMEM((length, length), F32),
                pltpu.VMEM((length, width), BF),
                pltpu.VMEM((length, width), BF),
                pltpu.VMEM((length, width), BF),
                pltpu.VMEM((width, length), BF),
                pltpu.VMEM((width, length), BF),
                pltpu.VMEM((width, length), BF),
                pltpu.VMEM((width, length), F32),
                pltpu.VMEM((head_count, length, length), F32),
                pltpu.VMEM((length, inner), BF),
                pltpu.VMEM((length, width), BF),
                pltpu.VMEM((width, length), BF),
                pltpu.VMEM((head_count, length), F32),
                pltpu.VMEM((width, length), F32),
                pltpu.SemaphoreType.DMA((5,)),
            ],
        ),
        out_shape=[shape(size, dtype) for size, dtype in outs]
        + [
            jax.ShapeDtypeStruct((4, width), F32),
            jax.ShapeDtypeStruct((head_rows, length), F32),
        ],
        compiler_params=pltpu.CompilerParams(vmem_limit_bytes=VMEM_LIMIT),
        cost_estimate=pl.CostEstimate(
            flops=60000000000, bytes_accessed=80000000, transcendentals=0
        ),
        name="layer_last",
    )(lengths, slopes, x, grad, gains, weight_full)


def weight_product(left, right):
    return lax.dot_general(
        left, right, (((0, 1), (0, 1)), ((), ())), preferred_element_type=F32
    )


def matrix_gradient(query_low, memory_low, attended, hidden, back):
    (two_low, pre_grad, normed_low, one_low, query_grad, key_grad, value_grad) = back
    return jnp.concatenate(
        [
            weight_product(query_low, query_grad),
            weight_product(memory_low, key_grad),
            weight_product(memory_low, value_grad),
            weight_product(attended, one_low),
            weight_product(pre_grad, normed_low),
            weight_product(hidden, two_low),
        ],
        axis=0,
    )


def adam_step(master, gradient, first_mom, second_mom, rate):
    first_new = BETA_ONE * first_mom + (1.0 - BETA_ONE) * gradient
    second_new = BETA_TWO * second_mom + (1.0 - BETA_TWO) * gradient * gradient
    first_hat = first_new / (1.0 - BETA_ONE**STEP)
    second_hat = second_new / (1.0 - BETA_TWO**STEP)
    inner_move = rate * (first_hat / (jnp.sqrt(second_hat) + ADAM_EPS) + DECAY_RATE * master)
    return (first_new, second_new, inner_move)


def outer_step(master, moves_sum, momentum_old, group_count):
    mean_move = moves_sum / group_count
    momentum_new = MOMENTUM * momentum_old + mean_move
    return (mean_move, momentum_new, master - OUTER_RATE * (mean_move + MOMENTUM * momentum_new))


def shards(
    hidden_in,
    lengths,
    out_grad,
    weights,
    weight_m,
    weight_v,
    outer_mom,
    small,
    small_m,
    small_v,
    small_mom,
):
    width = weights.shape[2]
    part_size = small.shape[0] // 2
    masters_low = [weights[layer].astype(BF) for layer in range(2)]

    gains = []
    slopes = []
    for layer in range(2):
        part = small[layer * part_size : (layer + 1) * part_size]
        gains.append(part[: 4 * width].reshape(4, width))
        slopes.append(part[4 * width :])

    matrix_two = lax.all_gather(masters_low[1], "fsdp", axis=0, tiled=True)
    matrix_one = gather_rows(masters_low[0])
    (q1, k1, v1, lse1, att1, one1, hid1, steep1, two1, first_out, low1) = layer_ahead(
        True, hidden_in, lengths, slopes[0], gains[0], matrix_one, F32
    )
    (block_out, low2, att2, hid2, *back_two) = layer_last(
        first_out, out_grad, lengths, slopes[1], gains[1], matrix_two
    )
    matrix_grad_two = matrix_gradient(low2, low2, att2, hid2, back_two[:7]).astype(BF)
    rest_two, matrix_grad_two = lax.optimization_barrier(
        ((back_two[4], back_two[5], back_two[6], back_two[7]), matrix_grad_two)
    )
    first_grad = rest_two[3]
    for index in range(3):
        first_grad = first_grad + jnp.einsum(
            "btn,an->bta",
            rest_two[index],
            matrix_two[index * width : (index + 1) * width],
            preferred_element_type=F32,
        )
    shard_two = lax.psum_scatter(matrix_grad_two, "fsdp", scatter_dimension=0, tiled=True)
    back_one = layer_back(
        True,
        first_grad,
        (q1, k1, v1, lse1, att1, one1, steep1, two1),
        lengths,
        slopes[0],
        gains[0],
        matrix_one,
    )
    input_grad = back_one[7]
    matrix_grad_one = matrix_gradient(low1, hidden_in, att1, hid1, back_one[:7]).astype(BF)
    head_count = slopes[0].shape[0]
    small_parts = []
    for back in (back_one, back_two):
        small_parts += [back[8].reshape(-1), -jnp.sum(back[9][:head_count], axis=1)]
    grad_shard, weight_sum, small_grad, small_sum = finish(
        matrix_grad_one,
        shard_two,
        weights,
        weight_m,
        weight_v,
        jnp.concatenate(small_parts)[None],
        small[None],
        small_m,
        small_v,
    )[:4]
    weight_first, weight_second, _ = adam_step(
        weights, grad_shard[None].astype(F32), weight_m, weight_v, INNER_RATE
    )
    small_first, small_second, _ = adam_step(small, small_grad, small_m, small_v, SMALL_RATE)
    weight_sum, small_sum = weight_sum.astype(F32), small_sum[0]
    group_count = lax.axis_size("group")
    weight_mean, weight_mom, weight_new = outer_step(weights, weight_sum, outer_mom, group_count)
    small_mean, small_momentum, small_after = outer_step(small, small_sum, small_mom, group_count)
    return (
        block_out,
        input_grad,
        weight_new,
        weight_new.astype(BF),
        weight_first,
        weight_second,
        weight_mean,
        weight_mom,
        small_after,
        small_first,
        small_second,
        small_mean,
        small_momentum,
    )


def solution(mesh):
    in_specs = (
        P(("group", "fsdp"), None, None),
        P(("group", "fsdp")),
        P(("group", "fsdp"), None, None),
        P(None, "fsdp", None),
        P("group", None, "fsdp", None),
        P("group", None, "fsdp", None),
        P(None, "fsdp", None),
        P(),
        P("group", None),
        P("group", None),
        P(),
    )
    out_specs = (
        P(("group", "fsdp"), None, None),
        P(("group", "fsdp"), None, None),
        P(None, "fsdp", None),
        P(None, "fsdp", None),
        P("group", None, "fsdp", None),
        P("group", None, "fsdp", None),
        P(None, "fsdp", None),
        P(None, "fsdp", None),
        P(),
        P("group", None),
        P("group", None),
        P(),
        P(),
    )
    return jax.shard_map(shards, mesh=mesh, in_specs=in_specs, out_specs=out_specs, check_vma=False)
```
